32 devices in a mesh: gx: 8 (over y, x, core), gy: 4 (over z).
Axes of the slice: x: 2, y: 2, z: 4, core: 2. Of those that a mesh axis runs over, the one named last changes fastest.
Arguments:
- tracers: float32 [2, 24, 64, 1024], P(None, None, 'gy', 'gx'), may hold values from -6 to 6
- uvel: float32 [24, 64, 1024], P(None, 'gy', 'gx'), may hold values from -6 to 6
- vvel: float32 [24, 64, 1024], P(None, 'gy', 'gx'), may hold values from -6 to 6
- sea_mask: int32 [64, 1024], P('gy', 'gx'), may hold values from 0 to 1, as said below
- levels: int32 [64, 1024], P('gy', 'gx'), may hold values from 1 to 24
- tracer_bar: float32 [2, 24, 64, 1024], P(None, None, 'gy', 'gx'), may hold values from -6 to 6
- eta_bar: float32 [64, 1024], P('gy', 'gx'), may hold values from -12 to 12
Outputs:
- tracer_adj: float32 [2, 24, 64, 1024], P(None, None, 'gy', 'gx')
- eta_adj: float32 [64, 1024], P('gy', 'gx')
The draws below stay inside these ranges and needn't reach their ends.
Inputs may be any that keep to these rules, and one draw needn't show every extreme that they name: `sea_mask`: the first and the last latitude row are land.
All inputs are finite; a program needn't handle non-finite values.
Results may differ from the reference program's by a relative error of at most 0.0001.
Values sent between devices are 32-bit elements; how exact they have to be, the bound alone decides.
No kernel may reach another device: no remote copies, remote signals or barrier semaphores. Data moves between devices by JAX's collectives and lax.ppermute only.
A program may use at most 64 MiB of HBM per device.

```python
import jax
import jax.numpy as jnp
from jax import lax

NZ = 24
ITERS = 3
NX = 1024
NY = 64


def draw_sea_mask(key, part):
    coins = jax.random.randint(key, (NY, NX), 0, 5)
    rows = lax.broadcasted_iota(jnp.int32, (NY, NX), 0)
    inside = (rows > 0) & (rows < NY - 1)
    return jnp.where(inside & (coins > 0), 1, 0).astype(jnp.int32)


def draw_eta_bar(key, part):
    rows = lax.broadcasted_iota(jnp.float32, (NY, NX), 0) / (NY - 1)
    columns = lax.broadcasted_iota(jnp.float32, (NY, NX), 1) / max(NX - 1, 1)
    ramp = (1.0 + 2.0 * rows) * (1.0 + 2.0 * columns) / 3.0
    noise = jnp.clip(jax.random.normal(key, (NY, NX), jnp.float32), -4.0, 4.0)
    return (noise * ramp).astype(jnp.float32)


def place_ends(entries, key, low, largest):
    shape = entries.shape
    index_at = [jax.random.randint(jax.random.fold_in(key, axis), (), 0, shape[axis]) for axis in range(len(shape))]
    entries = entries.at[tuple(index_at)].set(low)
    longest = shape.index(max(shape))
    index_at[longest] = (index_at[longest] + 1) % shape[longest]
    return entries.at[tuple(index_at)].set(largest)


def block_levels(own_key, extent, cuts, smallest, top_value):
    def one(dim, shards_of):
        draws = jax.random.uniform(jax.random.fold_in(jax.random.fold_in(own_key, 6), dim), (shards_of,), jnp.float32, smallest / len(cuts), top_value / len(cuts))
        return jnp.repeat(jnp.exp(draws), extent[dim] // shards_of).reshape((-1,) + (1,) * (len(extent) - dim - 1))

    loudness = one(*cuts[0])
    for cut in cuts[1:]:
        loudness = loudness * one(*cut)
    return loudness


def scatter_about(stream_key, dims, width, bound, split=(), dtype=jnp.bfloat16):
    result = width * jax.random.normal(stream_key, dims, jnp.float32)
    if split:
        result = result * block_levels(stream_key, dims, split, -0.22, 0.18)
    return jnp.clip(result, -bound, bound).astype(dtype)


def setup_inputs(seed: int = 0) -> dict:
    key_list = jax.random.split(jax.random.key(seed), 8)
    return {
        "tracers": scatter_about(key_list[0], (2, NZ, NY, NX), 1.0, 6.0, ((2, 4), (3, 8)), jnp.float32),
        "uvel": scatter_about(key_list[1], (NZ, NY, NX), 1.0, 6.0, ((1, 4), (2, 8)), jnp.float32),
        "vvel": scatter_about(key_list[2], (NZ, NY, NX), 1.0, 6.0, ((1, 4), (2, 8)), jnp.float32),
        "sea_mask": draw_sea_mask(jax.random.fold_in(key_list[7], 71), 0),
        "levels": place_ends(jax.random.randint(key_list[4], (NY, NX), 1, NZ + 1), jax.random.fold_in(key_list[4], 1), 1, NZ).astype(jnp.int32),
        "tracer_bar": scatter_about(key_list[5], (2, NZ, NY, NX), 1.0, 6.0, ((2, 4), (3, 8)), jnp.float32),
        "eta_bar": draw_eta_bar(jax.random.fold_in(key_list[7], 71), 0),
    }


advect_rate = 0.25
mix_floor = 0.2
mix_boost = 2.0
mix_slope = 2.0
mix_rate = 1.0
surface_stiffness = 2.0
thermal_steric = 0.5
haline_steric = 0.5

def wet_cells(sea_mask, levels, count):
    layer = lax.broadcasted_iota(jnp.int32, (count,) + sea_mask.shape, 0)
    return jnp.where(layer < levels[None], sea_mask[None], 0).astype(jnp.float32)

def thomas_solve(kappa, right_side):
    count = right_side.shape[1]
    nothing = jnp.zeros_like(kappa[0])
    primes = []
    partial_values = []
    for layer_index in range(count):
        below = kappa[layer_index] if layer_index < count - 1 else nothing
        above = kappa[layer_index - 1] if layer_index > 0 else nothing
        diagonal_term = 1.0 + mix_rate * (above + below)
        if layer_index == 0:
            divisor = diagonal_term
            current = right_side[:, 0] / divisor
        else:
            divisor = diagonal_term + mix_rate * above * primes[-1]
            current = (right_side[:, layer_index] + mix_rate * above * partial_values[-1]) / divisor
        primes.append(-mix_rate * below / divisor)
        partial_values.append(current)
    results = [partial_values[-1]]
    for layer_index in range(count - 2, -1, -1):
        results.append(partial_values[layer_index] - primes[layer_index] * results[-1])
    return jnp.stack(results[::-1], axis=1)

def vertical_mix(advanced, wet):
    density = advanced[1] - advanced[0]
    kappa = (mix_floor + mix_boost * jax.nn.sigmoid(mix_slope * (density[:-1] - density[1:]))) * wet[1:]
    return thomas_solve(kappa, advanced)

def column_adjoint(advanced, wet, mixed_bar):

    def forward(values):
        return vertical_mix(values, wet)
    unused, pull = jax.vjp(forward, advanced)
    return pull(mixed_bar)[0]

def advect(tracers, uvel, vvel, wet):
    east_flow = uvel * wet * jnp.roll(wet, -1, 2)
    north_flow = vvel * wet * jnp.roll(wet, -1, 1)
    east_flux = east_flow[None] * 0.5 * (tracers + jnp.roll(tracers, -1, 3))
    north_flux = north_flow[None] * 0.5 * (tracers + jnp.roll(tracers, -1, 2))
    divergence = east_flux - jnp.roll(east_flux, 1, 3) + north_flux - jnp.roll(north_flux, 1, 2)
    return tracers - advect_rate * wet[None] * divergence

def surface_apply(field, depth):
    east_weight = surface_stiffness * jnp.minimum(depth, jnp.roll(depth, -1, 1))
    north_weight = surface_stiffness * jnp.minimum(depth, jnp.roll(depth, -1, 0))
    east_flux = east_weight * (field - jnp.roll(field, -1, 1))
    north_flux = north_weight * (field - jnp.roll(field, -1, 0))
    return field + east_flux - jnp.roll(east_flux, 1, 1) + north_flux - jnp.roll(north_flux, 1, 0)

def surface_solve(target, depth):
    iterate = jnp.zeros_like(target)
    residual = target
    direction = target
    norm_now = jnp.sum(residual * residual)
    for iteration in range(ITERS):
        image = surface_apply(direction, depth)
        alpha = norm_now / jnp.sum(direction * image)
        iterate = iterate + alpha * direction
        residual = residual - alpha * image
        if iteration < ITERS - 1:
            norm_next = jnp.sum(residual * residual)
            direction = residual + norm_next / norm_now * direction
            norm_now = norm_next
    return iterate

def reference(tracers, uvel, vvel, sea_mask, levels, tracer_bar, eta_bar):
    wet = wet_cells(sea_mask, levels, NZ)
    depth = lax.optimization_barrier(jnp.sum(wet, axis=0)) / NZ
    eta_adj = surface_solve(eta_bar, depth)
    advanced = advect(tracers, uvel, vvel, wet)
    steric = jnp.array([thermal_steric, -haline_steric], jnp.float32)[:, None, None, None]
    mixed_bar = tracer_bar + steric * wet[None] * eta_adj[None, None]

    def per_row(items):
        return column_adjoint(items[0], items[1], items[2])
    rows_bar = lax.map(per_row, (jnp.moveaxis(advanced, 2, 0), jnp.moveaxis(wet, 1, 0), jnp.moveaxis(mixed_bar, 2, 0)))
    advanced_bar = jnp.moveaxis(rows_bar, 0, 2)

    def advect_only(values):
        return advect(values, uvel, vvel, wet)
    unused, pull = jax.vjp(advect_only, tracers)
    tracer_adj = pull(advanced_bar)[0]
    return (tracer_adj, eta_adj)
```

```python
import functools

import jax
import jax.numpy as jnp
from jax import lax
from jax.experimental import pallas as pl
from jax.experimental.pallas import tpu as pltpu
from jax.sharding import PartitionSpec as P

advect_rate = 0.25
mix_floor = 0.2
mix_boost = 2.0
mix_slope = 2.0
mix_rate = 1.0
surface_stiffness = 2.0
thermal_steric = 0.5
haline_steric = 0.5
sterics = (thermal_steric, -haline_steric)
spread = 4.0 * surface_stiffness
F32 = jnp.float32
VMEM = pl.BlockSpec(memory_space=pltpu.VMEM)


def lanes_of(shape):
    return lax.broadcasted_iota(jnp.int32, shape, 1)


def rows_of(shape):
    return lax.broadcasted_iota(jnp.int32, shape, 0)


def roll(cells, shift, axis):
    size = cells.shape[axis]
    shift = shift % size
    return cells if shift == 0 else pltpu.roll(cells, shift, axis)


def wet_depth(mask_ref, levels_ref):
    return (mask_ref[...] * levels_ref[...]).astype(F32)


def pack_columns(mask_ref, levels_ref, eta_ref, tracer_ref, u_ref, east_ref, west_ref):
    count = u_ref.shape[0]
    level = wet_depth(mask_ref, levels_ref)
    lane = lanes_of(level.shape)
    width = level.shape[1]
    east = jnp.zeros_like(level)
    west = jnp.zeros_like(level)
    for k in range(count):
        fields = (tracer_ref[0, k], tracer_ref[1, k], jnp.where(level > k, u_ref[k], 0.0))
        for f, field in enumerate(fields):
            at = f * count + k
            turned = roll(field, at + 1, 1)
            east = jnp.where(lane == at, turned, east)
            if f < 2:
                west = jnp.where(lane == at + 1, turned, west)
    east_ref[0] = east
    west_ref[0] = west
    eta = eta_ref[...]
    east_ref[1] = jnp.where(lane >= width - 3, eta, roll(level, -3, 1))
    west_ref[1] = jnp.where(lane < 3, eta, roll(level, 3, 1))


def pack_rows(mask_ref, levels_ref, tracer_ref, v_ref, north_ref, south_ref):
    count, height, _ = v_ref.shape
    level = wet_depth(mask_ref, levels_ref)
    for f in range(2):
        north_ref[f * count : (f + 1) * count, :] = tracer_ref[f, :, height - 1, :]
        south_ref[f * count : (f + 1) * count, :] = tracer_ref[f, :, 0, :]
    last = v_ref[:, height - 1, :]
    north_ref[2 * count :, :] = jnp.where(rows_of(last.shape).astype(F32) < level[height - 1 :, :], last, 0.0)


def side_tiles(from_west, from_east):
    lane = lanes_of(from_west.shape)
    first = lane < from_west.shape[1] // 2
    both = jnp.where(first, from_east, from_west)
    return both, jnp.where(first, roll(both, -3, 1), roll(both, 3, 1))


def join_rows(mask_ref, levels_ref, eta_ref, west_ref, east_ref, north_in, south_in, north_ref, south_ref):
    level = wet_depth(mask_ref, levels_ref)
    eta_side, level_side = side_tiles(west_ref[1], east_ref[1])
    tiles = (eta_ref[...], eta_side, level, level_side)
    height = level.shape[0]
    start = north_in.shape[0]
    north_ref[:start, :] = north_in[...]
    for index, tile in enumerate(tiles):
        north_ref[start + 8 * index : start + 8 * index + 8, :] = tile[height - 8 :, :]
    start = south_in.shape[0]
    south_ref[:start, :] = south_in[...]
    for index, tile in enumerate(tiles):
        south_ref[start + 8 * index : start + 8 * index + 8, :] = tile[:8, :]


def surface_basis(eta_ext, level_ext, count, block):
    height, width = block
    depth = level_ext / count
    east_weight = (surface_stiffness / spread) * jnp.minimum(depth, roll(depth, -1, 1))
    north_weight = (surface_stiffness / spread) * jnp.minimum(depth, roll(depth, -1, 0))

    def scaled(field):
        east_flux = east_weight * (field - roll(field, -1, 1))
        north_flux = north_weight * (field - roll(field, -1, 0))
        return (east_flux - roll(east_flux, 1, 1)) + (north_flux - roll(north_flux, 1, 0))

    first = scaled(eta_ext)
    second = scaled(first) - first
    third = scaled(second)
    vectors = [x[:height, :width] for x in (eta_ext, first, second, third)]
    pairs = ((0, 0), (0, 1), (0, 2), (1, 1), (1, 2), (2, 2), (2, 3))
    lane = lanes_of((1, width))
    line = jnp.zeros((1, width), F32)
    for index, (a, b) in enumerate(pairs):
        product = jnp.sum(vectors[a] * vectors[b], axis=0, keepdims=True)
        line = jnp.where(lane == index, jnp.sum(product, axis=1, keepdims=True), line)
    return first, second, line


def galerkin(sums):
    d00, d01, d02, d11, d12, d22, d2q = [sums[:, i : i + 1] for i in range(7)]
    k00 = d00 + spread * d01
    k01 = d01 + spread * d11
    k02 = d02 + spread * d12
    k11 = d11 + spread * (d11 + d12)
    k12 = d12 + spread * (d12 + d22)
    k22 = d22 + spread * d2q
    i00 = 1.0 / k00
    s11 = k11 - k01 * k01 * i00
    s12 = k12 - k01 * k02 * i00
    s22 = k22 - k02 * k02 * i00
    g1 = spread * (d01 * d01 - d00 * d11) * i00
    g2 = spread * (d02 * d01 - d00 * d12) * i00
    i11 = 1.0 / s11
    c12 = s12 * i11
    last = s22 - s12 * c12
    y2 = jnp.where(last > 4e-7 * s22, (g2 - g1 * c12) / last, 0.0)
    y1 = (g1 - s12 * y2) * i11
    y0 = (d00 - k01 * y1 - k02 * y2) * i00
    return y0, y1, y2


def shifted_depths(level, level_ext):
    height, width = level.shape
    east = jnp.minimum(level_ext, roll(level_ext, -1, 1))[:height, :width]
    north = jnp.minimum(level_ext, roll(level_ext, -1, 0))[:height, :width]
    return east, north


def extended(own, side, north_msg, south_msg, start_north, start_south, slot):
    upper = [north_msg[start_north + 8 * s : start_north + 8 * s + 8, :] for s in (slot, slot + 1)]
    lower = [south_msg[start_south + 8 * s : start_south + 8 * s + 8, :] for s in (slot, slot + 1)]
    left = jnp.concatenate([own, upper[0], lower[0]], axis=0)
    right = jnp.concatenate([side, upper[1], lower[1]], axis=0)
    return jnp.concatenate([left, right], axis=1)


def west_flow(msg, level, count):
    lane = lanes_of(msg.shape)
    flow = jnp.where(lane < count, roll(msg, -2 * count, 1), roll(msg, -count, 1))
    layer = (lane % count).astype(F32)
    return jnp.where(layer < level[:, :1], flow, 0.0)


def south_flow(msg, level, count):
    flow = msg[2 * count : 3 * count, :]
    flow = jnp.where(rows_of(flow.shape).astype(F32) < level[:1, :], flow, 0.0)
    return jnp.concatenate([flow, flow], axis=0)


def column_kernel(
    mask_ref, levels_ref, eta_ref, tracer_ref, u_ref, v_ref, bar_ref,
    west_ref, east_ref, own_west_ref, north_ref, south_ref, own_south_ref,
    adjoint_ref, east_out, west_out, north_out, south_out, level_out, basis_out, sums_out,
    ratio_ref, slope_ref, value_ref,
):
    count, height, width = u_ref.shape
    level = wet_depth(mask_ref, levels_ref)
    eta_side, level_side = side_tiles(west_ref[1], east_ref[1])
    starts = (2 * count, 3 * count)
    eta_ext = extended(eta_ref[...], eta_side, north_ref, south_ref, *starts, 0)
    level_ext = extended(level, level_side, north_ref, south_ref, *starts, 2)
    first, second, line = surface_basis(eta_ext, level_ext, count, (height, width))
    basis_out[0] = eta_ext
    basis_out[1] = first
    basis_out[2] = second
    level_out[...] = level_ext
    sums_out[...] = jnp.broadcast_to(line, sums_out.shape)

    east_depth, north_depth = shifted_depths(level, level_ext)
    lane = lanes_of((height, width))
    row = rows_of((height, width))
    from_west, from_east = west_ref[0], east_ref[0]
    west_flux = 0.5 * west_flow(from_west, level, count) * (from_west + roll(own_west_ref[0], -1, 1))
    south_flux = (
        0.5
        * south_flow(south_ref, level, count)
        * (south_ref[: 2 * count, :] + own_south_ref[...])
    )

    def advected(k):
        east_flow = jnp.where(east_depth > k, 0.5 * u_ref[k], 0.0)
        north_flow = jnp.where(north_depth > k, 0.5 * v_ref[k], 0.0)
        wet_rate = jnp.where(level > k, advect_rate, 0.0)
        result = []
        for f in range(2):
            at = f * count + k
            c = tracer_ref[f, k]
            c_east = jnp.where(lane == width - 1, roll(from_east, width - 2 - at, 1), roll(c, -1, 1))
            c_north = jnp.where(row == height - 1, north_ref[at : at + 1, :], roll(c, -1, 0))
            flux_e = east_flow * (c + c_east)
            flux_n = north_flow * (c + c_north)
            flux_w = jnp.where(lane == 0, roll(west_flux, -at, 1), roll(flux_e, 1, 1))
            flux_s = jnp.where(row == 0, south_flux[at : at + 1, :], roll(flux_n, 1, 0))
            result.append(c - wet_rate * ((flux_e - flux_w) + (flux_n - flux_s)))
        return result

    now = advected(0)
    kappa_up = None
    ratio_up = None
    values = None
    for k in range(count):
        if k < count - 1:
            later = advected(k + 1)
            step = (now[1] - now[0]) - (later[1] - later[0])
            gate = jax.nn.sigmoid(mix_slope * step)
            wet_below = level > k + 1
            kappa = jnp.where(wet_below, mix_floor + mix_boost * gate, 0.0)
            slope_ref[k] = jnp.where(wet_below, (mix_boost * mix_slope) * gate * (1.0 - gate), 0.0)
            diagonal = 1.0 + mix_rate * kappa
        else:
            later = None
            kappa = None
            diagonal = 1.0
        if k > 0:
            diagonal = diagonal + mix_rate * kappa_up * (1.0 - ratio_up)
        inverse = 1.0 / diagonal
        sides = [now[0], now[1], bar_ref[0, k], bar_ref[1, k]]
        if k > 0:
            sides = [side + mix_rate * kappa_up * value for side, value in zip(sides, values)]
        values = [side * inverse for side in sides]
        for f in range(4):
            value_ref[f, k] = values[f]
        if kappa is not None:
            ratio = mix_rate * kappa * inverse
            ratio_ref[k] = ratio
            kappa_up, ratio_up = kappa, ratio
        now = later

    east_pack = jnp.zeros((height, width), F32)
    west_pack = jnp.zeros((height, width), F32)
    pull_below = None
    below = values
    for k in range(count - 2, -1, -1):
        ratio = ratio_ref[k]
        here = [value_ref[f, k] + ratio * below[f] for f in range(4)]
        pull = (-mix_rate) * slope_ref[k] * (
            (here[2] - below[2]) * (here[0] - below[0]) + (here[3] - below[3]) * (here[1] - below[1])
        )
        emit(adjoint_ref, k + 1, below, pull_below, pull)
        below, pull_below = here, pull
    emit(adjoint_ref, 0, below, pull_below, None)

    for f in range(2):
        for k in range(count):
            at = f * count + k
            turned = roll(adjoint_ref[f, k], at + 1, 1)
            east_pack = jnp.where(lane == at, turned, east_pack)
            west_pack = jnp.where(lane == at + 1, turned, west_pack)
        north_out[f * count : (f + 1) * count, :] = adjoint_ref[f, :, height - 1, :]
        south_out[f * count : (f + 1) * count, :] = adjoint_ref[f, :, 0, :]
    east_out[...] = east_pack
    west_out[...] = west_pack


def emit(adjoint_ref, k, values, pull_here, pull_above):
    if pull_here is None:
        change = -pull_above if pull_above is not None else 0.0
    elif pull_above is None:
        change = pull_here
    else:
        change = pull_here - pull_above
    adjoint_ref[0, k] = values[2] - change
    adjoint_ref[1, k] = values[3] + change


def final_kernel(
    sums_ref, basis_ref, level_ref, u_ref, v_ref, adjoint_ref,
    west_ref, south_ref, from_west_ref, from_east_ref, own_west_ref, from_north_ref, from_south_ref, own_south_ref,
    tracer_out, eta_out,
):
    count, height, width = u_ref.shape
    sums = jnp.sum(sums_ref[...], axis=0, keepdims=True)
    y0, y1, y2 = galerkin(sums)
    eta_ext = y0 * basis_ref[0] + (y1 * basis_ref[1] + y2 * basis_ref[2])
    level_ext = level_ref[...]
    eta = eta_ext[:height, :width]
    level = level_ext[:height, :width]
    eta_out[...] = eta
    east_depth, north_depth = shifted_depths(level, level_ext)
    lane = lanes_of((height, width))
    row = rows_of((height, width))

    def lane_values(tile, offset, column):
        place = lane - offset
        layer = (place % count).astype(F32)
        steric = jnp.where(place < count, sterics[0], sterics[1])
        depth = level_ext[:height, column : column + 1]
        return tile + jnp.where(layer < depth, steric * eta_ext[:height, column : column + 1], 0.0)

    def row_values(tile, line):
        at = rows_of(tile.shape)
        layer = (at % count).astype(F32)
        steric = jnp.where(at < count, sterics[0], sterics[1])
        depth = level_ext[line : line + 1, :width]
        return tile + jnp.where(layer < depth, steric * eta_ext[line : line + 1, :width], 0.0)

    last_lane = level_ext.shape[1] - 1
    last_row = level_ext.shape[0] - 1
    east_values = lane_values(from_east_ref[...], 1, width)
    west_values = lane_values(from_west_ref[...], 0, last_lane)
    first_values = lane_values(roll(own_west_ref[...], -1, 1), 0, 0)
    west_part = west_flow(west_ref[0], level, count) * (west_values - first_values)
    north_values = row_values(from_north_ref[...], height)
    south_values = row_values(from_south_ref[...], last_row)
    bottom_values = row_values(own_south_ref[...], 0)
    south_part = south_flow(south_ref, level, count) * (south_values - bottom_values)
    for k in range(count):
        east_flow = jnp.where(east_depth > k, u_ref[k], 0.0)
        north_flow = jnp.where(north_depth > k, v_ref[k], 0.0)
        wet_eta = jnp.where(level > k, eta, 0.0)
        for f in range(2):
            at = f * count + k
            y = adjoint_ref[f, k] + sterics[f] * wet_eta
            y_east = jnp.where(lane == width - 1, roll(east_values, width - 2 - at, 1), roll(y, -1, 1))
            y_north = jnp.where(row == height - 1, north_values[at : at + 1, :], roll(y, -1, 0))
            part_e = east_flow * (y - y_east)
            part_n = north_flow * (y - y_north)
            part_w = jnp.where(lane == 0, roll(west_part, -at, 1), roll(part_e, 1, 1))
            part_s = jnp.where(row == 0, south_part[at : at + 1, :], roll(part_n, 1, 0))
            tracer_out[f, k] = y - (0.5 * advect_rate) * ((part_e + part_w) + (part_n + part_s))


def call(kernel, outs, name, scratch=()):
    return pl.pallas_call(
        kernel,
        out_shape=[jax.ShapeDtypeStruct(shape, F32) for shape in outs],
        out_specs=[VMEM] * len(outs),
        scratch_shapes=list(scratch),
        name=name,
    )


def around(axis, cells, step, wrap):
    count = lax.axis_size(axis)
    pairs = [(i, (i + step) % count) for i in range(count)]
    if not wrap:
        pairs = [(i, j) for i, j in pairs if j == i + step]
    return lax.ppermute(cells, axis, pairs)


def per_device(tracers, uvel, vvel, sea_mask, levels, tracer_bar, eta_bar):
    _, count, height, width = tracers.shape
    devices = lax.axis_size("gx") * lax.axis_size("gy")
    tile = (height, width)
    surface = (sea_mask, levels, eta_bar)
    to_east, to_west = call(pack_columns, [(2,) + tile] * 2, "pack_columns")(*surface, tracers, uvel)
    from_west = around("gx", to_east, 1, True)
    from_east = around("gx", to_west, -1, True)
    rows_north, rows_south = call(pack_rows, [(3 * count, width), (2 * count, width)], "pack_rows")(
        sea_mask, levels, tracers, vvel
    )
    to_north, to_south = call(join_rows, [(3 * count + 32, width), (2 * count + 32, width)], "join_rows")(
        *surface, from_west, from_east, rows_north, rows_south
    )
    from_south = around("gy", to_north, 1, False)
    from_north = around("gy", to_south, -1, False)
    ext = (height + 16, 2 * width)
    adjoint, east2, west2, north2, south2, level_ext, basis, sums = call(
        column_kernel,
        [(2, count) + tile, tile, tile, (2 * count, width), (2 * count, width), ext, (3,) + ext, (devices, width)],
        "columns",
        [pltpu.VMEM((count,) + tile, F32), pltpu.VMEM((count,) + tile, F32), pltpu.VMEM((4, count) + tile, F32)],
    )(*surface, tracers, uvel, vvel, tracer_bar, from_west, from_east, to_west, from_north, from_south, rows_south)
    from_west2 = around("gx", east2, 1, True)
    from_east2 = around("gx", west2, -1, True)
    from_south2 = around("gy", north2, 1, False)
    from_north2 = around("gy", south2, -1, False)
    all_sums = lax.all_to_all(sums.reshape(devices, 1, width), ("gx", "gy"), 0, 0).reshape(devices, width)
    tracer_adj, eta_adj = call(final_kernel, [tracers.shape, tile], "retreat")(
        all_sums, basis, level_ext, uvel, vvel, adjoint,
        from_west, from_south, from_west2, from_east2, west2, from_north2, from_south2, south2,
    )
    return (tracer_adj, eta_adj)


def solution(mesh):
    return jax.shard_map(
        per_device,
        mesh=mesh,
        in_specs=(
            P(None, None, "gy", "gx"),
            P(None, "gy", "gx"),
            P(None, "gy", "gx"),
            P("gy", "gx"),
            P("gy", "gx"),
            P(None, None, "gy", "gx"),
            P("gy", "gx"),
        ),
        out_specs=(P(None, None, "gy", "gx"), P("gy", "gx")),
        check_vma=False,
    )
```

```python
import jax
import jax.numpy as jnp
from jax import lax
from jax.experimental import pallas as pl
from jax.experimental.pallas import tpu as pltpu
from jax.sharding import PartitionSpec as P

advect_rate = 0.25
mix_floor = 0.2
mix_boost = 2.0
mix_slope = 2.0
mix_rate = 1.0
surface_stiffness = 2.0
thermal_steric = 0.5
haline_steric = 0.5
sterics = (thermal_steric, -haline_steric)
spread = 4.0 * surface_stiffness
F32 = jnp.float32
VMEM = pl.BlockSpec(memory_space=pltpu.VMEM)
SMEM = pl.BlockSpec(memory_space=pltpu.SMEM)
U_TILE, V_TILE, BAR_TILE, SURFACE_TILE = 2, 3, 4, 6


def lanes_of(shape):
    return lax.broadcasted_iota(jnp.int32, shape, 1)


def rows_of(shape):
    return lax.broadcasted_iota(jnp.int32, shape, 0)


def roll(cells, shift, axis):
    size = cells.shape[axis]
    shift = shift % size
    return cells if shift == 0 else pltpu.roll(cells, shift, axis)


def wet_depth(mask_ref, levels_ref):
    return (mask_ref[...] * levels_ref[...]).astype(F32)


def layer_rows(count, width):
    return rows_of((count, width)).astype(F32)


def pack_columns(mask_ref, levels_ref, eta_ref, tracer_ref, u_ref, v_ref, bar_ref, out_ref):
    count, height, width = u_ref.shape
    lane = lanes_of((height, width))
    group = lane // 4
    tiles = [jnp.zeros((height, width), F32)] * SURFACE_TILE
    for k in range(count):
        fields = (tracer_ref[0, k], tracer_ref[1, k], u_ref[k], v_ref[k], bar_ref[0, k], bar_ref[1, k])
        here = group == k
        tiles = [jnp.where(here, roll(field, 4 * k + 2, 1), tile) for field, tile in zip(fields, tiles)]
    for index, tile in enumerate(tiles):
        out_ref[index] = tile
    level = wet_depth(mask_ref, levels_ref)
    depth = jnp.where(lane < width // 2, roll(level, 3, 1), roll(level, -3, 1))
    out_ref[SURFACE_TILE] = jnp.where((lane < 3) | (lane >= width - 3), eta_ref[...], depth)


class Sides:
    def __init__(self, parity_ref, first_ref, second_ref, level):
        self.parity = parity_ref[0]
        self.refs = (first_ref, second_ref)
        self.level = level
        self.shape = level.shape
        lane = lanes_of(self.shape)
        self.lane = lane
        self.layer = (lane // 4).astype(F32)
        self.eastern = lane % 4 == 1
        east, west = self.pick(SURFACE_TILE)
        half = lane < self.shape[1] // 2
        self.eta = jnp.where(half, east, west)
        self.depth = jnp.where(half, roll(self.eta, -3, 1), roll(self.eta, 3, 1))

    def pick(self, tile):
        first, second = (ref[tile] for ref in self.refs)
        even = jnp.full(self.shape, self.parity, jnp.int32) == 0
        return jnp.where(even, first, second), jnp.where(even, second, first)

    def inner(self, tile):
        east, west = self.pick(tile)
        return jnp.where(self.eastern, roll(east, -1, 1), roll(west, 1, 1))

    def outer(self, tile):
        east, west = self.pick(tile)
        return jnp.where(self.eastern, roll(east, -2, 1), roll(west, 2, 1))

    def columns(self, cells, east, west):
        return jnp.where(self.eastern, cells[:, east : east + 1], cells[:, west : west + 1])

    def edge_flow(self, own_ref, u_inner):
        width = self.shape[1]
        own_depth = self.columns(self.level, width - 1, 0)
        beyond = self.columns(self.depth, 0, width - 1)
        flow = jnp.where(self.eastern, own_ref[U_TILE], u_inner)
        return jnp.where(self.layer < jnp.minimum(own_depth, beyond), flow, 0.0)


def pack_rows(mask_ref, levels_ref, tracer_ref, u_ref, v_ref, bar_ref, c_out, n_out, u_out, b_out, v_out):
    count, height, width = u_ref.shape
    level = wet_depth(mask_ref, levels_ref)
    layer = layer_rows(count, width)
    for side, (row, inside, face) in enumerate(((height - 1, height - 2, height - 2), (0, 1, 0))):
        depth = jnp.minimum(level[row : row + 1, :], level[inside : inside + 1, :])
        flow = jnp.where(layer < depth, 0.5 * v_ref[:, face, :], 0.0)
        u_out[side] = u_ref[:, row, :]
        for f in range(2):
            part = slice(f * count, (f + 1) * count)
            c = tracer_ref[f, :, row, :]
            c_out[side, part, :] = c
            n_out[side, part, :] = flow * (c + tracer_ref[f, :, inside, :])
            b_out[side, part, :] = bar_ref[f, :, row, :]
    v_out[...] = jnp.where(layer < level[height - 1 :, :], v_ref[:, height - 1, :], 0.0)


def join_rows(
    parity_ref, mask_ref, levels_ref, eta_ref, own_ref, first_ref, second_ref, c_ref, n_ref, u_ref, b_ref, v_ref,
    north_ref, south_ref,
):
    count, width = v_ref.shape
    level = wet_depth(mask_ref, levels_ref)
    height = level.shape[0]
    sides = Sides(parity_ref, first_ref, second_ref, level)
    inner = [sides.inner(f) for f in range(2)]
    flow = 0.5 * sides.edge_flow(own_ref, sides.inner(U_TILE))
    flux = [flow * (own_ref[f] + inner[f]) for f in range(2)]
    layer = layer_rows(count, width)
    lane = lanes_of((count, width))
    level_row = rows_of((count, width))
    pad = jnp.zeros((8, width), F32)
    for side, (row, sign, out_ref) in enumerate(((height - 1, -1.0, north_ref), (0, 1.0, south_ref))):
        depth = level[row : row + 1, :]
        east_flow = jnp.where(layer < jnp.minimum(depth, roll(depth, -1, 1)), 0.5 * u_ref[side], 0.0)
        rate = jnp.where(layer < depth, advect_rate, 0.0)
        for f in range(2):
            part = slice(f * count, (f + 1) * count)
            c = c_ref[side, part, :]
            line = flux[f][row : row + 1, :]
            east_end, west_end = (
                jnp.sum(jnp.where(lane == 4 * level_row + m, line, 0.0), axis=1, keepdims=True) for m in (1, 2)
            )
            flux_e = jnp.where(lane == width - 1, east_end, east_flow * (c + roll(c, -1, 1)))
            flux_w = jnp.where(lane == 0, west_end, roll(flux_e, 1, 1))
            out_ref[part, :] = c
            out_ref[2 * count + f * count : 2 * count + (f + 1) * count, :] = c - rate * (
                (flux_e - flux_w) + sign * n_ref[side, part, :]
            )
        out_ref[4 * count : 6 * count, :] = b_ref[side]
    start = 6 * count
    north_ref[start : start + count, :] = v_ref[...]
    row8 = rows_of((8, width))
    for index, (eta, depth) in enumerate(((eta_ref[...], level), (sides.eta, sides.depth))):
        at = start + 8 * index
        south_ref[at : at + 8, :] = jnp.where(row8 < 4, eta[:8, :], roll(depth[:8, :], 4, 0))
        at += count
        north_ref[at : at + 8, :] = jnp.where(row8 < 4, roll(depth[height - 8 :, :], 4, 0), eta[height - 8 :, :])
    v_inner = sides.inner(V_TILE)
    at = start + 16
    south_ref[at : at + 8, :] = jnp.where(row8 == 0, inner[0][:1, :], jnp.where(row8 == 1, inner[1][:1, :], pad))
    at += count
    north_ref[at : at + 8, :] = jnp.where(
        row8 == 0,
        inner[0][height - 1 :, :],
        jnp.where(row8 == 1, inner[1][height - 1 :, :], jnp.where(row8 == 2, v_inner[height - 1 :, :], pad)),
    )


def extended(own, side, north, south, turn):
    row8 = rows_of((8, own.shape[1]))
    parts = []
    for index, tile in enumerate((own, side)):
        up, down = (roll(msg[8 * index : 8 * index + 8, :], turn, 0) for msg in (north, south))
        parts.append(jnp.concatenate([tile, jnp.where(row8 < 4, up, down)], axis=0))
    return jnp.concatenate(parts, axis=1)


def surface_kernel(
    parity_ref, mask_ref, levels_ref, eta_ref, first_ref, second_ref, north_ref, south_ref,
    basis_out, level_out, sums_out, *, count,
):
    level = wet_depth(mask_ref, levels_ref)
    height, width = level.shape
    sides = Sides(parity_ref, first_ref, second_ref, level)
    north = north_ref[6 * count : 6 * count + 16, :]
    south = south_ref[7 * count : 7 * count + 16, :]
    eta_ext = extended(eta_ref[...], sides.eta, north, south, 0)
    level_ext = extended(level, sides.depth, north, south, 4)
    level_out[...] = level_ext
    depth = level_ext / count
    east_weight = (surface_stiffness / spread) * jnp.minimum(depth, roll(depth, -1, 1))
    north_weight = (surface_stiffness / spread) * jnp.minimum(depth, roll(depth, -1, 0))

    def scaled(field):
        east_flux = east_weight * (field - roll(field, -1, 1))
        north_flux = north_weight * (field - roll(field, -1, 0))
        return (east_flux - roll(east_flux, 1, 1)) + (north_flux - roll(north_flux, 1, 0))

    first = scaled(eta_ext)
    second = scaled(first) - first
    third = scaled(second)
    basis_out[0] = eta_ext
    basis_out[1] = first
    basis_out[2] = second
    vectors = [x[:height, :width] for x in (eta_ext, first, second, third)]
    pairs = ((0, 0), (0, 1), (0, 2), (1, 1), (1, 2), (2, 2), (2, 3))
    row = rows_of((8, width))
    table = jnp.zeros((8, width), F32)
    for index, (a, b) in enumerate(pairs):
        table = jnp.where(row == index, jnp.sum(vectors[a] * vectors[b], axis=0, keepdims=True), table)
    totals = jnp.sum(table, axis=1, keepdims=True)
    line = jnp.sum(jnp.where(lanes_of((8, width)) == row, totals, 0.0), axis=0, keepdims=True)
    sums_out[...] = jnp.broadcast_to(line, sums_out.shape)


def galerkin(sums):
    d00, d01, d02, d11, d12, d22, d2q = [sums[:, i : i + 1] for i in range(7)]
    k00 = d00 + spread * d01
    k01 = d01 + spread * d11
    k02 = d02 + spread * d12
    k11 = d11 + spread * (d11 + d12)
    k12 = d12 + spread * (d12 + d22)
    k22 = d22 + spread * d2q
    i00 = 1.0 / k00
    s11 = k11 - k01 * k01 * i00
    s12 = k12 - k01 * k02 * i00
    s22 = k22 - k02 * k02 * i00
    g1 = spread * (d01 * d01 - d00 * d11) * i00
    g2 = spread * (d02 * d01 - d00 * d12) * i00
    i11 = 1.0 / s11
    c12 = s12 * i11
    last = s22 - s12 * c12
    y2 = jnp.where(last > 4e-7 * s22, (g2 - g1 * c12) / last, 0.0)
    y1 = (g1 - s12 * y2) * i11
    y0 = (d00 - k01 * y1 - k02 * y2) * i00
    return y0, y1, y2


def column_kernel(
    parity_ref, mask_ref, levels_ref, tracer_ref, u_ref, v_ref, bar_ref,
    own_ref, first_ref, second_ref, c_rows, v_row, north_ref, south_ref, level_ref,
    base_out, flow_out,
    side_ref, turn_ref, ratio_ref, slope_ref, value_ref, adjoint_ref,
):
    count, height, width = u_ref.shape
    level_ext = level_ref[...]
    level = level_ext[:height, :width]
    sides = Sides(parity_ref, first_ref, second_ref, level)
    lane, row = lanes_of((height, width)), rows_of((height, width))
    layer = layer_rows(count, width)
    last_row, last_lane = level_ext.shape[0] - 1, level_ext.shape[1] - 1

    inner = [sides.inner(f) for f in range(2)]
    u_inner, v_inner = sides.inner(U_TILE), sides.inner(V_TILE)
    edge_flow = sides.edge_flow(own_ref, u_inner)
    edge_flux = [0.5 * edge_flow * (own_ref[f] + inner[f]) for f in range(2)]
    depth_in = sides.columns(sides.depth, 0, width - 1)
    depth_out = sides.columns(sides.depth, 1, width - 2)
    far_flow = jnp.where(sides.eastern, u_inner, sides.outer(U_TILE))
    far_flow = jnp.where(sides.layer < jnp.minimum(depth_in, depth_out), far_flow, 0.0)
    corner_depth = [
        jnp.where(sides.eastern[:1], level_ext[r : r + 1, width : width + 1], level_ext[r : r + 1, last_lane:])
        for r in (height, last_row)
    ]
    corner_north = north_ref[6 * count + 16 : 6 * count + 24, :]
    corner_south = south_ref[7 * count + 16 : 7 * count + 24, :]
    depth_up = jnp.where(row == height - 1, corner_depth[0], roll(depth_in, -1, 0))
    up_flow = jnp.where(sides.layer < jnp.minimum(depth_in, depth_up), v_inner, 0.0)
    low_flow = jnp.where(
        sides.layer[:1] < jnp.minimum(depth_in[:1], corner_depth[1]), corner_south[2:3, :], 0.0
    )
    rate = jnp.where(sides.layer < depth_in, advect_rate, 0.0)
    outward = jnp.where(sides.eastern, 1.0, -1.0)
    beyond = []
    for f in range(2):
        c = inner[f]
        far_flux = 0.5 * far_flow * (c + sides.outer(f))
        c_up = jnp.where(row == height - 1, corner_north[f : f + 1, :], roll(c, -1, 0))
        flux_n = 0.5 * up_flow * (c + c_up)
        low_flux = 0.5 * low_flow * (corner_south[f : f + 1, :] + c[:1])
        flux_s = jnp.where(row == 0, low_flux, roll(flux_n, 1, 0))
        beyond.append(c - rate * (outward * (far_flux - edge_flux[f]) + (flux_n - flux_s)))
    beyond += [sides.inner(BAR_TILE), sides.inner(BAR_TILE + 1), depth_in]
    filler = jnp.zeros((width - height * len(beyond), width), F32)
    turned = jnp.transpose(jnp.concatenate(beyond + [filler], axis=0))

    south_flow = jnp.where(layer < level[:1, :], south_ref[6 * count : 7 * count, :], 0.0)
    north_flow = jnp.where(layer < level_ext[height : height + 1, :width], v_row[...], 0.0)
    south_flux, north_flux = [], []
    side_ref[...] = jnp.zeros_like(side_ref)
    for f in range(2):
        part = slice(f * count, (f + 1) * count)
        summed = slice(2 * count + f * count, 2 * count + (f + 1) * count)
        bars = slice(4 * count + f * count, 4 * count + (f + 1) * count)
        south_flux.append(0.5 * south_flow * (south_ref[part, :] + c_rows[1, part, :]))
        north_flux.append(0.5 * north_flow * (c_rows[0, part, :] + north_ref[part, :]))
        side_ref[f, pl.ds(4, count, stride=8), :] = south_ref[summed, :] - advect_rate * south_flux[f]
        side_ref[f, pl.ds(5, count, stride=8), :] = north_ref[summed, :] + advect_rate * north_flux[f]
        side_ref[2 + f, pl.ds(4, count, stride=8), :] = south_ref[bars, :]
        side_ref[2 + f, pl.ds(5, count, stride=8), :] = north_ref[bars, :]
    for f in range(4):
        turn_ref[f] = roll(turned, -height * f, 1)
        for m in (1, 2):
            side_ref[f, pl.ds(m, count, stride=8), :] = turn_ref[f, pl.ds(m, count, stride=4), :]
    row8 = rows_of((8, width))
    side_level = roll(turned[:8, :], -4 * height, 1)
    side_level = jnp.where((row8 == 1) | (row8 == 2), side_level, 0.0)
    side_level = jnp.where(row8 == 4, level_ext[last_row:, :width], side_level)
    side_level = jnp.where(row8 == 5, level_ext[height : height + 1, :width], side_level)
    level_all = jnp.concatenate([level, side_level], axis=0)

    east_depth = jnp.minimum(level_ext, roll(level_ext, -1, 1))[:height, :width]
    north_depth = jnp.minimum(level_ext, roll(level_ext, -1, 0))[:height, :width]

    def with_side(own, f, k):
        return jnp.concatenate([own, side_ref[f, 8 * k : 8 * k + 8, :]], axis=0)

    def advected(k):
        flow_e = jnp.where(east_depth > k, 0.5 * u_ref[k], 0.0)
        flow_n = jnp.where(north_depth > k, 0.5 * v_ref[k], 0.0)
        wet_rate = jnp.where(level > k, advect_rate, 0.0)
        result = []
        for f in range(2):
            c = tracer_ref[f, k]
            ends = roll(edge_flux[f], -(4 * k + 2), 1)
            flux_e = jnp.where(lane == width - 1, ends, flow_e * (c + roll(c, -1, 1)))
            flux_w = jnp.where(lane == 0, ends, roll(flux_e, 1, 1))
            flux_n = jnp.where(row == height - 1, north_flux[f][k : k + 1, :], flow_n * (c + roll(c, -1, 0)))
            flux_s = jnp.where(row == 0, south_flux[f][k : k + 1, :], roll(flux_n, 1, 0))
            result.append(with_side(c - wet_rate * ((flux_e - flux_w) + (flux_n - flux_s)), f, k))
        return result

    now = advected(0)
    kappa_up = ratio_up = values = None
    for k in range(count):
        diagonal = 1.0
        kappa = later = None
        if k < count - 1:
            later = advected(k + 1)
            step = (now[1] - now[0]) - (later[1] - later[0])
            gate = jax.nn.sigmoid(mix_slope * step)
            wet_below = level_all > k + 1
            kappa = jnp.where(wet_below, mix_floor + mix_boost * gate, 0.0)
            slope_ref[k] = jnp.where(wet_below, (mix_boost * mix_slope) * gate * (1.0 - gate), 0.0)
            diagonal = diagonal + mix_rate * kappa
        if k > 0:
            diagonal = diagonal + mix_rate * kappa_up * (1.0 - ratio_up)
        inverse = 1.0 / diagonal
        right = [now[0], now[1], with_side(bar_ref[0, k], 2, k), with_side(bar_ref[1, k], 3, k)]
        if k > 0:
            right = [cells + mix_rate * kappa_up * value for cells, value in zip(right, values)]
        values = [cells * inverse for cells in right]
        for f in range(4):
            value_ref[f, k] = values[f]
        if kappa is not None:
            ratio_up, kappa_up = mix_rate * kappa * inverse, kappa
            ratio_ref[k] = ratio_up
        now = later

    def emit(k, cells, change):
        for f, sign in ((0, -1.0), (1, 1.0)):
            full = cells[2 + f] + sign * change
            adjoint_ref[f, k] = full[:height, :]
            side_ref[f, 8 * k : 8 * k + 8, :] = full[height:, :]

    below = values
    pull_below = None
    for k in range(count - 2, -1, -1):
        here = [value_ref[f, k] + ratio_ref[k] * below[f] for f in range(4)]
        pull = (-mix_rate) * slope_ref[k] * (
            (here[2] - below[2]) * (here[0] - below[0]) + (here[3] - below[3]) * (here[1] - below[1])
        )
        emit(k + 1, below, -pull if pull_below is None else pull_below - pull)
        below, pull_below = here, pull
    emit(0, below, pull_below)

    for f in range(2):
        for m in (1, 2):
            turn_ref[f, pl.ds(m, count, stride=4), :] = side_ref[f, pl.ds(m, count, stride=8), :]
    wide = lanes_of((width, width)) < height
    back = jnp.transpose(jnp.where(wide, turn_ref[0], roll(turn_ref[1], height, 1)))
    ends_of = [back[f * height : (f + 1) * height, :] for f in range(2)]
    south_line = [side_ref[f, pl.ds(4, count, stride=8), :] for f in range(2)]
    north_line = [side_ref[f, pl.ds(5, count, stride=8), :] for f in range(2)]
    for k in range(count):
        flow_e = jnp.where(east_depth > k, u_ref[k], 0.0)
        flow_n = jnp.where(north_depth > k, v_ref[k], 0.0)
        ends_flow = roll(edge_flow, -(4 * k + 2), 1)
        low = south_flow[k : k + 1, :]
        flow_out[0, k] = flow_e
        flow_out[1, k] = jnp.where(lane == 0, ends_flow, roll(flow_e, 1, 1))
        flow_out[2, k] = flow_n
        flow_out[3, k] = jnp.where(row == 0, low, roll(flow_n, 1, 0))
        for f in range(2):
            y = adjoint_ref[f, k]
            ends = roll(ends_of[f], -(4 * k + 2), 1)
            y_east = jnp.where(lane == width - 1, ends, roll(y, -1, 1))
            y_north = jnp.where(row == height - 1, north_line[f][k : k + 1, :], roll(y, -1, 0))
            part_e = flow_e * (y - y_east)
            part_n = flow_n * (y - y_north)
            part_w = jnp.where(lane == 0, ends_flow * (ends - y), roll(part_e, 1, 1))
            part_s = jnp.where(row == 0, low * (south_line[f][k : k + 1, :] - y), roll(part_n, 1, 0))
            base_out[f, k] = y - (0.5 * advect_rate) * ((part_e + part_w) + (part_n + part_s))


def final_kernel(sums_ref, basis_ref, level_ref, base_ref, flow_ref, tracer_out, eta_out):
    _, count, height, width = base_ref.shape
    y0, y1, y2 = galerkin(jnp.sum(sums_ref[...], axis=0, keepdims=True))
    eta_ext = y0 * basis_ref[0] + (y1 * basis_ref[1] + y2 * basis_ref[2])
    eta = eta_ext[:height, :width]
    level = level_ref[:height, :width]
    eta_out[...] = eta
    half = 0.5 * advect_rate
    east = half * (eta_ext - roll(eta_ext, -1, 1))
    north = half * (eta_ext - roll(eta_ext, -1, 0))
    west = roll(east, 1, 1)[:height, :width]
    south = roll(north, 1, 0)[:height, :width]
    east, north = east[:height, :width], north[:height, :width]
    for k in range(count):
        part = (flow_ref[0, k] * east + flow_ref[1, k] * west) + (flow_ref[2, k] * north + flow_ref[3, k] * south)
        share = jnp.where(level > k, eta, 0.0) - part
        for f in range(2):
            tracer_out[f, k] = base_ref[f, k] + sterics[f] * share


def call(kernel, outs, name, specs=None, scratch=(), cost=None):
    def run(*operands):
        return pl.pallas_call(
            kernel,
            out_shape=[jax.ShapeDtypeStruct(shape, F32) for shape in outs],
            in_specs=specs or [VMEM] * len(operands),
            out_specs=[VMEM] * len(outs),
            scratch_shapes=list(scratch),
            cost_estimate=cost,
            name=name,
        )(*operands)

    return run


def swap(cells, axis, first):
    count = lax.axis_size(axis)
    pairs = []
    for i in range(first, count, 2):
        j = (i + 1) % count
        pairs += [(i, j), (j, i)]
    return lax.ppermute(cells, axis, pairs)


def shift(cells, axis, step):
    count = lax.axis_size(axis)
    return lax.ppermute(cells, axis, [(i, i + step) for i in range(count) if 0 <= i + step < count])


def per_device(tracers, uvel, vvel, sea_mask, levels, tracer_bar, eta_bar):
    _, count, height, width = tracers.shape
    devices = lax.axis_size("gx") * lax.axis_size("gy")
    tile = (height, width)
    rows = (2, 2 * count, width)
    depths = (sea_mask, levels)
    parity = (lax.axis_index("gx") % 2).astype(jnp.int32).reshape(1)
    (own,) = call(pack_columns, [(SURFACE_TILE + 1,) + tile], "pack_columns")(
        *depths, eta_bar, tracers, uvel, vvel, tracer_bar
    )
    first, second = swap(own, "gx", 0), swap(own, "gx", 1)
    c_rows, n_rows, u_rows, b_rows, v_row = call(
        pack_rows, [rows, rows, (2, count, width), rows, (count, width)], "pack_rows"
    )(*depths, tracers, uvel, vvel, tracer_bar)
    to_north, to_south = call(
        join_rows, [(7 * count + 24, width), (6 * count + 24, width)], "join_rows", [SMEM] + [VMEM] * 11
    )(parity, *depths, eta_bar, own, first, second, c_rows, n_rows, u_rows, b_rows, v_row)
    from_south, from_north = shift(to_north, "gy", 1), shift(to_south, "gy", -1)
    ext = (height + 8, 2 * width)

    def surface(*refs):
        surface_kernel(*refs, count=count)

    basis, level_ext, sums = call(
        surface, [(3,) + ext, ext, (devices, width)], "surface", [SMEM] + [VMEM] * 7
    )(parity, *depths, eta_bar, first, second, from_north, from_south)
    all_sums = lax.all_to_all(sums.reshape(devices, 1, width), ("gx", "gy"), 0, 0).reshape(devices, width)
    taller = (height + 8, width)
    base, flows = call(
        column_kernel,
        [(2, count) + tile, (4, count) + tile],
        "columns",
        [SMEM] + [VMEM] * 14,
        [
            pltpu.VMEM((4, 8 * count, width), F32),
            pltpu.VMEM((4, width, width), F32),
            pltpu.VMEM((count,) + taller, F32),
            pltpu.VMEM((count,) + taller, F32),
            pltpu.VMEM((4, count) + taller, F32),
            pltpu.VMEM((2, count) + tile, F32),
        ],
        pl.CostEstimate(flops=400 * count * height * width, transcendentals=count * height * width, bytes_accessed=1 << 22),
    )(parity, *depths, tracers, uvel, vvel, tracer_bar, own, first, second, c_rows, v_row, from_north, from_south, level_ext)
    tracer_adj, eta_adj = call(final_kernel, [tracers.shape, tile], "finish")(all_sums, basis, level_ext, base, flows)
    return (tracer_adj, eta_adj)


def solution(mesh):
    return jax.shard_map(
        per_device,
        mesh=mesh,
        in_specs=(
            P(None, None, "gy", "gx"),
            P(None, "gy", "gx"),
            P(None, "gy", "gx"),
            P("gy", "gx"),
            P("gy", "gx"),
            P(None, None, "gy", "gx"),
            P("gy", "gx"),
        ),
        out_specs=(P(None, None, "gy", "gx"), P("gy", "gx")),
        check_vma=False,
    )
```

```python
import jax
import jax.numpy as jnp
from jax import lax
from jax.experimental import pallas as pl
from jax.experimental.pallas import tpu as pltpu
from jax.sharding import PartitionSpec as P

advect_rate = 0.25
mix_floor = 0.2
mix_boost = 2.0
mix_slope = 2.0
mix_rate = 1.0
surface_stiffness = 2.0
thermal_steric = 0.5
haline_steric = 0.5
sterics = (thermal_steric, -haline_steric)
spread = 4.0 * surface_stiffness
F32 = jnp.float32
VMEM = pl.BlockSpec(memory_space=pltpu.VMEM)
SMEM = pl.BlockSpec(memory_space=pltpu.SMEM)
vmem_grant = 8 << 20
U_TILE, V_TILE, BAR_TILE, SURFACE_TILE = 2, 3, 4, 6


def lanes_of(shape):
    return lax.broadcasted_iota(jnp.int32, shape, 1)


def rows_of(shape):
    return lax.broadcasted_iota(jnp.int32, shape, 0)


def roll(cells, shift, axis):
    size = cells.shape[axis]
    shift = shift % size
    return cells if shift == 0 else pltpu.roll(cells, shift, axis)


def wet_depth(mask_ref, levels_ref):
    return (mask_ref[...] * levels_ref[...]).astype(F32)


def layer_rows(count, width):
    return rows_of((count, width)).astype(F32)


def pack_columns(mask_ref, levels_ref, eta_ref, tracer_ref, u_ref, v_ref, bar_ref, out_ref):
    count, height, width = u_ref.shape
    lane = lanes_of((height, width))
    group = lane // 4
    tiles = [jnp.zeros((height, width), F32)] * SURFACE_TILE
    for k in range(count):
        fields = (tracer_ref[0, k], tracer_ref[1, k], u_ref[k], v_ref[k], bar_ref[0, k], bar_ref[1, k])
        here = group == k
        tiles = [jnp.where(here, roll(field, 4 * k + 2, 1), tile) for field, tile in zip(fields, tiles)]
    for index, tile in enumerate(tiles):
        out_ref[index] = tile
    level = wet_depth(mask_ref, levels_ref)
    depth = jnp.where(lane < width // 2, roll(level, 3, 1), roll(level, -3, 1))
    out_ref[SURFACE_TILE] = jnp.where((lane < 3) | (lane >= width - 3), eta_ref[...], depth)


class Sides:
    def __init__(self, parity_ref, first_ref, second_ref, level):
        self.parity = parity_ref[0]
        self.refs = (first_ref, second_ref)
        self.level = level
        self.shape = level.shape
        lane = lanes_of(self.shape)
        self.lane = lane
        self.layer = (lane // 4).astype(F32)
        self.eastern = lane % 4 == 1
        east, west = self.pick(SURFACE_TILE)
        half = lane < self.shape[1] // 2
        self.eta = jnp.where(half, east, west)
        self.depth = jnp.where(half, roll(self.eta, -3, 1), roll(self.eta, 3, 1))

    def pick(self, tile):
        first, second = (ref[tile] for ref in self.refs)
        even = jnp.full(self.shape, self.parity, jnp.int32) == 0
        return jnp.where(even, first, second), jnp.where(even, second, first)

    def inner(self, tile):
        east, west = self.pick(tile)
        return jnp.where(self.eastern, roll(east, -1, 1), roll(west, 1, 1))

    def outer(self, tile):
        east, west = self.pick(tile)
        return jnp.where(self.eastern, roll(east, -2, 1), roll(west, 2, 1))

    def columns(self, cells, east, west):
        return jnp.where(self.eastern, cells[:, east : east + 1], cells[:, west : west + 1])

    def edge_flow(self, own_ref, u_inner):
        width = self.shape[1]
        own_depth = self.columns(self.level, width - 1, 0)
        beyond = self.columns(self.depth, 0, width - 1)
        flow = jnp.where(self.eastern, own_ref[U_TILE], u_inner)
        return jnp.where(self.layer < jnp.minimum(own_depth, beyond), flow, 0.0)


def pack_rows(mask_ref, levels_ref, tracer_ref, u_ref, v_ref, bar_ref, c_out, n_out, u_out, b_out, v_out):
    count, height, width = u_ref.shape
    level = wet_depth(mask_ref, levels_ref)
    layer = layer_rows(count, width)
    for side, (row, inside, face) in enumerate(((height - 1, height - 2, height - 2), (0, 1, 0))):
        depth = jnp.minimum(level[row : row + 1, :], level[inside : inside + 1, :])
        flow = jnp.where(layer < depth, 0.5 * v_ref[:, face, :], 0.0)
        u_out[side] = u_ref[:, row, :]
        for f in range(2):
            part = slice(f * count, (f + 1) * count)
            c = tracer_ref[f, :, row, :]
            c_out[side, part, :] = c
            n_out[side, part, :] = flow * (c + tracer_ref[f, :, inside, :])
            b_out[side, part, :] = bar_ref[f, :, row, :]
    v_out[...] = jnp.where(layer < level[height - 1 :, :], v_ref[:, height - 1, :], 0.0)


def join_rows(
    parity_ref, mask_ref, levels_ref, eta_ref, own_ref, first_ref, second_ref, c_ref, n_ref, u_ref, b_ref, v_ref,
    north_ref, south_ref,
):
    count, width = v_ref.shape
    level = wet_depth(mask_ref, levels_ref)
    height = level.shape[0]
    sides = Sides(parity_ref, first_ref, second_ref, level)
    inner = [sides.inner(f) for f in range(2)]
    flow = 0.5 * sides.edge_flow(own_ref, sides.inner(U_TILE))
    flux = [flow * (own_ref[f] + inner[f]) for f in range(2)]
    layer = layer_rows(count, width)
    lane = lanes_of((count, width))
    level_row = rows_of((count, width))
    pad = jnp.zeros((8, width), F32)
    for side, (row, sign, out_ref) in enumerate(((height - 1, -1.0, north_ref), (0, 1.0, south_ref))):
        depth = level[row : row + 1, :]
        east_flow = jnp.where(layer < jnp.minimum(depth, roll(depth, -1, 1)), 0.5 * u_ref[side], 0.0)
        rate = jnp.where(layer < depth, advect_rate, 0.0)
        for f in range(2):
            part = slice(f * count, (f + 1) * count)
            c = c_ref[side, part, :]
            line = flux[f][row : row + 1, :]
            east_end, west_end = (
                jnp.sum(jnp.where(lane == 4 * level_row + m, line, 0.0), axis=1, keepdims=True) for m in (1, 2)
            )
            flux_e = jnp.where(lane == width - 1, east_end, east_flow * (c + roll(c, -1, 1)))
            flux_w = jnp.where(lane == 0, west_end, roll(flux_e, 1, 1))
            out_ref[part, :] = c
            out_ref[2 * count + f * count : 2 * count + (f + 1) * count, :] = c - rate * (
                (flux_e - flux_w) + sign * n_ref[side, part, :]
            )
        out_ref[4 * count : 6 * count, :] = b_ref[side]
    start = 6 * count
    north_ref[start : start + count, :] = v_ref[...]
    row8 = rows_of((8, width))
    for index, (eta, depth) in enumerate(((eta_ref[...], level), (sides.eta, sides.depth))):
        at = start + 8 * index
        south_ref[at : at + 8, :] = jnp.where(row8 < 4, eta[:8, :], roll(depth[:8, :], 4, 0))
        at += count
        north_ref[at : at + 8, :] = jnp.where(row8 < 4, roll(depth[height - 8 :, :], 4, 0), eta[height - 8 :, :])
    v_inner = sides.inner(V_TILE)
    at = start + 16
    south_ref[at : at + 8, :] = jnp.where(row8 == 0, inner[0][:1, :], jnp.where(row8 == 1, inner[1][:1, :], pad))
    at += count
    north_ref[at : at + 8, :] = jnp.where(
        row8 == 0,
        inner[0][height - 1 :, :],
        jnp.where(row8 == 1, inner[1][height - 1 :, :], jnp.where(row8 == 2, v_inner[height - 1 :, :], pad)),
    )


def extended(own, side, north, south, turn):
    row8 = rows_of((8, own.shape[1]))
    parts = []
    for index, tile in enumerate((own, side)):
        up, down = (roll(msg[8 * index : 8 * index + 8, :], turn, 0) for msg in (north, south))
        parts.append(jnp.concatenate([tile, jnp.where(row8 < 4, up, down)], axis=0))
    return jnp.concatenate(parts, axis=1)


def surface_kernel(
    parity_ref, mask_ref, levels_ref, eta_ref, first_ref, second_ref, north_ref, south_ref,
    basis_out, level_out, sums_out, *, count,
):
    level = wet_depth(mask_ref, levels_ref)
    height, width = level.shape
    sides = Sides(parity_ref, first_ref, second_ref, level)
    north = north_ref[6 * count : 6 * count + 16, :]
    south = south_ref[7 * count : 7 * count + 16, :]
    eta_ext = extended(eta_ref[...], sides.eta, north, south, 0)
    level_ext = extended(level, sides.depth, north, south, 4)
    level_out[...] = level_ext
    depth = level_ext / count
    east_weight = (surface_stiffness / spread) * jnp.minimum(depth, roll(depth, -1, 1))
    north_weight = (surface_stiffness / spread) * jnp.minimum(depth, roll(depth, -1, 0))

    def scaled(field):
        east_flux = east_weight * (field - roll(field, -1, 1))
        north_flux = north_weight * (field - roll(field, -1, 0))
        return (east_flux - roll(east_flux, 1, 1)) + (north_flux - roll(north_flux, 1, 0))

    first = scaled(eta_ext)
    second = scaled(first) - first
    third = scaled(second)
    basis_out[0] = eta_ext
    basis_out[1] = first
    basis_out[2] = second
    vectors = [x[:height, :width] for x in (eta_ext, first, second, third)]
    pairs = ((0, 0), (0, 1), (0, 2), (1, 1), (1, 2), (2, 2), (2, 3))
    row = rows_of((8, width))
    table = jnp.zeros((8, width), F32)
    for index, (a, b) in enumerate(pairs):
        table = jnp.where(row == index, jnp.sum(vectors[a] * vectors[b], axis=0, keepdims=True), table)
    totals = jnp.sum(table, axis=1, keepdims=True)
    line = jnp.sum(jnp.where(lanes_of((8, width)) == row, totals, 0.0), axis=0, keepdims=True)
    sums_out[...] = jnp.broadcast_to(line, sums_out.shape)


def galerkin(sums):
    d00, d01, d02, d11, d12, d22, d2q = [sums[:, i : i + 1] for i in range(7)]
    k00 = d00 + spread * d01
    k01 = d01 + spread * d11
    k02 = d02 + spread * d12
    k11 = d11 + spread * (d11 + d12)
    k12 = d12 + spread * (d12 + d22)
    k22 = d22 + spread * d2q
    i00 = 1.0 / k00
    s11 = k11 - k01 * k01 * i00
    s12 = k12 - k01 * k02 * i00
    s22 = k22 - k02 * k02 * i00
    g1 = spread * (d01 * d01 - d00 * d11) * i00
    g2 = spread * (d02 * d01 - d00 * d12) * i00
    i11 = 1.0 / s11
    c12 = s12 * i11
    last = s22 - s12 * c12
    y2 = jnp.where(last > 4e-7 * s22, (g2 - g1 * c12) / last, 0.0)
    y1 = (g1 - s12 * y2) * i11
    y0 = (d00 - k01 * y1 - k02 * y2) * i00
    return y0, y1, y2


def column_kernel(
    parity_ref, mask_ref, levels_ref, tracer_ref, u_ref, v_ref, bar_ref,
    own_ref, first_ref, second_ref, c_rows, v_row, north_ref, south_ref, level_ref,
    base_out, flow_out,
    side_ref, turn_ref, ratio_ref, slope_ref, value_ref, adjoint_ref,
):
    count, height, width = u_ref.shape
    level_ext = level_ref[...]
    level = level_ext[:height, :width]
    sides = Sides(parity_ref, first_ref, second_ref, level)
    lane, row = lanes_of((height, width)), rows_of((height, width))
    layer = layer_rows(count, width)
    last_row, last_lane = level_ext.shape[0] - 1, level_ext.shape[1] - 1

    inner = [sides.inner(f) for f in range(2)]
    u_inner, v_inner = sides.inner(U_TILE), sides.inner(V_TILE)
    edge_flow = sides.edge_flow(own_ref, u_inner)
    edge_flux = [0.5 * edge_flow * (own_ref[f] + inner[f]) for f in range(2)]
    depth_in = sides.columns(sides.depth, 0, width - 1)
    depth_out = sides.columns(sides.depth, 1, width - 2)
    far_flow = jnp.where(sides.eastern, u_inner, sides.outer(U_TILE))
    far_flow = jnp.where(sides.layer < jnp.minimum(depth_in, depth_out), far_flow, 0.0)
    corner_depth = [
        jnp.where(sides.eastern[:1], level_ext[r : r + 1, width : width + 1], level_ext[r : r + 1, last_lane:])
        for r in (height, last_row)
    ]
    corner_north = north_ref[6 * count + 16 : 6 * count + 24, :]
    corner_south = south_ref[7 * count + 16 : 7 * count + 24, :]
    depth_up = jnp.where(row == height - 1, corner_depth[0], roll(depth_in, -1, 0))
    up_flow = jnp.where(sides.layer < jnp.minimum(depth_in, depth_up), v_inner, 0.0)
    low_flow = jnp.where(
        sides.layer[:1] < jnp.minimum(depth_in[:1], corner_depth[1]), corner_south[2:3, :], 0.0
    )
    rate = jnp.where(sides.layer < depth_in, advect_rate, 0.0)
    outward = jnp.where(sides.eastern, 1.0, -1.0)
    beyond = []
    for f in range(2):
        c = inner[f]
        far_flux = 0.5 * far_flow * (c + sides.outer(f))
        c_up = jnp.where(row == height - 1, corner_north[f : f + 1, :], roll(c, -1, 0))
        flux_n = 0.5 * up_flow * (c + c_up)
        low_flux = 0.5 * low_flow * (corner_south[f : f + 1, :] + c[:1])
        flux_s = jnp.where(row == 0, low_flux, roll(flux_n, 1, 0))
        beyond.append(c - rate * (outward * (far_flux - edge_flux[f]) + (flux_n - flux_s)))
    beyond += [sides.inner(BAR_TILE), sides.inner(BAR_TILE + 1), depth_in]
    filler = jnp.zeros((width - height * len(beyond), width), F32)
    turned = jnp.transpose(jnp.concatenate(beyond + [filler], axis=0))

    south_flow = jnp.where(layer < level[:1, :], south_ref[6 * count : 7 * count, :], 0.0)
    north_flow = jnp.where(layer < level_ext[height : height + 1, :width], v_row[...], 0.0)
    south_flux, north_flux = [], []
    side_ref[...] = jnp.zeros_like(side_ref)
    for f in range(2):
        part = slice(f * count, (f + 1) * count)
        summed = slice(2 * count + f * count, 2 * count + (f + 1) * count)
        bars = slice(4 * count + f * count, 4 * count + (f + 1) * count)
        south_flux.append(0.5 * south_flow * (south_ref[part, :] + c_rows[1, part, :]))
        north_flux.append(0.5 * north_flow * (c_rows[0, part, :] + north_ref[part, :]))
        side_ref[f, pl.ds(4, count, stride=8), :] = south_ref[summed, :] - advect_rate * south_flux[f]
        side_ref[f, pl.ds(5, count, stride=8), :] = north_ref[summed, :] + advect_rate * north_flux[f]
        side_ref[2 + f, pl.ds(4, count, stride=8), :] = south_ref[bars, :]
        side_ref[2 + f, pl.ds(5, count, stride=8), :] = north_ref[bars, :]
    for f in range(4):
        turn_ref[f] = roll(turned, -height * f, 1)
        for m in (1, 2):
            side_ref[f, pl.ds(m, count, stride=8), :] = turn_ref[f, pl.ds(m, count, stride=4), :]
    row8 = rows_of((8, width))
    side_level = roll(turned[:8, :], -4 * height, 1)
    side_level = jnp.where((row8 == 1) | (row8 == 2), side_level, 0.0)
    side_level = jnp.where(row8 == 4, level_ext[last_row:, :width], side_level)
    side_level = jnp.where(row8 == 5, level_ext[height : height + 1, :width], side_level)
    level_all = jnp.concatenate([level, side_level], axis=0)

    east_depth = jnp.minimum(level_ext, roll(level_ext, -1, 1))[:height, :width]
    north_depth = jnp.minimum(level_ext, roll(level_ext, -1, 0))[:height, :width]

    def with_side(own, f, k):
        return jnp.concatenate([own, side_ref[f, 8 * k : 8 * k + 8, :]], axis=0)

    def advected(k):
        flow_e = jnp.where(east_depth > k, 0.5 * u_ref[k], 0.0)
        flow_n = jnp.where(north_depth > k, 0.5 * v_ref[k], 0.0)
        wet_rate = jnp.where(level > k, advect_rate, 0.0)
        result = []
        for f in range(2):
            c = tracer_ref[f, k]
            ends = roll(edge_flux[f], -(4 * k + 2), 1)
            flux_e = jnp.where(lane == width - 1, ends, flow_e * (c + roll(c, -1, 1)))
            flux_w = jnp.where(lane == 0, ends, roll(flux_e, 1, 1))
            flux_n = jnp.where(row == height - 1, north_flux[f][k : k + 1, :], flow_n * (c + roll(c, -1, 0)))
            flux_s = jnp.where(row == 0, south_flux[f][k : k + 1, :], roll(flux_n, 1, 0))
            result.append(with_side(c - wet_rate * ((flux_e - flux_w) + (flux_n - flux_s)), f, k))
        return result

    now = advected(0)
    kappa_up = ratio_up = values = None
    for k in range(count):
        diagonal = 1.0
        kappa = later = None
        if k < count - 1:
            later = advected(k + 1)
            step = (now[1] - now[0]) - (later[1] - later[0])
            gate = jax.nn.sigmoid(mix_slope * step)
            wet_below = level_all > k + 1
            kappa = jnp.where(wet_below, mix_floor + mix_boost * gate, 0.0)
            slope_ref[k] = jnp.where(wet_below, (mix_boost * mix_slope) * gate * (1.0 - gate), 0.0)
            diagonal = diagonal + mix_rate * kappa
        if k > 0:
            diagonal = diagonal + mix_rate * kappa_up * (1.0 - ratio_up)
        inverse = 1.0 / diagonal
        right = [now[0], now[1], with_side(bar_ref[0, k], 2, k), with_side(bar_ref[1, k], 3, k)]
        if k > 0:
            right = [cells + mix_rate * kappa_up * value for cells, value in zip(right, values)]
        values = [cells * inverse for cells in right]
        for f in range(4):
            value_ref[f, k] = values[f]
        if kappa is not None:
            ratio_up, kappa_up = mix_rate * kappa * inverse, kappa
            ratio_ref[k] = ratio_up
        now = later

    def emit(k, cells, change):
        for f, sign in ((0, -1.0), (1, 1.0)):
            full = cells[2 + f] + sign * change
            adjoint_ref[f, k] = full[:height, :]
            side_ref[f, 8 * k : 8 * k + 8, :] = full[height:, :]

    below = values
    pull_below = None
    for k in range(count - 2, -1, -1):
        here = [value_ref[f, k] + ratio_ref[k] * below[f] for f in range(4)]
        pull = (-mix_rate) * slope_ref[k] * (
            (here[2] - below[2]) * (here[0] - below[0]) + (here[3] - below[3]) * (here[1] - below[1])
        )
        emit(k + 1, below, -pull if pull_below is None else pull_below - pull)
        below, pull_below = here, pull
    emit(0, below, pull_below)

    for f in range(2):
        for m in (1, 2):
            turn_ref[f, pl.ds(m, count, stride=4), :] = side_ref[f, pl.ds(m, count, stride=8), :]
    wide = lanes_of((width, width)) < height
    back = jnp.transpose(jnp.where(wide, turn_ref[0], roll(turn_ref[1], height, 1)))
    ends_of = [back[f * height : (f + 1) * height, :] for f in range(2)]
    south_line = [side_ref[f, pl.ds(4, count, stride=8), :] for f in range(2)]
    north_line = [side_ref[f, pl.ds(5, count, stride=8), :] for f in range(2)]
    for k in range(count):
        flow_e = jnp.where(east_depth > k, u_ref[k], 0.0)
        flow_n = jnp.where(north_depth > k, v_ref[k], 0.0)
        ends_flow = roll(edge_flow, -(4 * k + 2), 1)
        low = south_flow[k : k + 1, :]
        flow_out[0, k] = flow_e
        flow_out[1, k] = jnp.where(lane == 0, ends_flow, roll(flow_e, 1, 1))
        flow_out[2, k] = flow_n
        flow_out[3, k] = jnp.where(row == 0, low, roll(flow_n, 1, 0))
        for f in range(2):
            y = adjoint_ref[f, k]
            ends = roll(ends_of[f], -(4 * k + 2), 1)
            y_east = jnp.where(lane == width - 1, ends, roll(y, -1, 1))
            y_north = jnp.where(row == height - 1, north_line[f][k : k + 1, :], roll(y, -1, 0))
            part_e = flow_e * (y - y_east)
            part_n = flow_n * (y - y_north)
            part_w = jnp.where(lane == 0, ends_flow * (ends - y), roll(part_e, 1, 1))
            part_s = jnp.where(row == 0, low * (south_line[f][k : k + 1, :] - y), roll(part_n, 1, 0))
            base_out[f, k] = y - (0.5 * advect_rate) * ((part_e + part_w) + (part_n + part_s))


def final_kernel(sums_ref, basis_ref, level_ref, base_ref, flow_ref, tracer_out, eta_out):
    _, count, height, width = base_ref.shape
    y0, y1, y2 = galerkin(jnp.sum(sums_ref[...], axis=0, keepdims=True))
    eta_ext = y0 * basis_ref[0] + (y1 * basis_ref[1] + y2 * basis_ref[2])
    eta = eta_ext[:height, :width]
    level = level_ref[:height, :width]
    eta_out[...] = eta
    half = 0.5 * advect_rate
    east = half * (eta_ext - roll(eta_ext, -1, 1))
    north = half * (eta_ext - roll(eta_ext, -1, 0))
    west = roll(east, 1, 1)[:height, :width]
    south = roll(north, 1, 0)[:height, :width]
    east, north = east[:height, :width], north[:height, :width]
    for k in range(count):
        part = (flow_ref[0, k] * east + flow_ref[1, k] * west) + (flow_ref[2, k] * north + flow_ref[3, k] * south)
        share = jnp.where(level > k, eta, 0.0) - part
        for f in range(2):
            tracer_out[f, k] = base_ref[f, k] + sterics[f] * share


def call(kernel, outs, name, specs=None, scratch=(), cost=None):
    def run(*operands):
        return pl.pallas_call(
            kernel,
            out_shape=[jax.ShapeDtypeStruct(shape, F32) for shape in outs],
            in_specs=specs or [VMEM] * len(operands),
            out_specs=[VMEM] * len(outs),
            scratch_shapes=list(scratch),
            cost_estimate=cost,
            compiler_params=pltpu.CompilerParams(vmem_limit_bytes=vmem_grant),
            name=name,
        )(*operands)

    return run


def swap(cells, axis, first):
    count = lax.axis_size(axis)
    pairs = []
    for i in range(first, count, 2):
        j = (i + 1) % count
        pairs += [(i, j), (j, i)]
    return lax.ppermute(cells, axis, pairs)


def shift(cells, axis, step):
    count = lax.axis_size(axis)
    return lax.ppermute(cells, axis, [(i, i + step) for i in range(count) if 0 <= i + step < count])


def per_device(tracers, uvel, vvel, sea_mask, levels, tracer_bar, eta_bar):
    _, count, height, width = tracers.shape
    devices = lax.axis_size("gx") * lax.axis_size("gy")
    tile = (height, width)
    rows = (2, 2 * count, width)
    depths = (sea_mask, levels)
    parity = (lax.axis_index("gx") % 2).astype(jnp.int32).reshape(1)
    (own,) = call(pack_columns, [(SURFACE_TILE + 1,) + tile], "pack_columns")(
        *depths, eta_bar, tracers, uvel, vvel, tracer_bar
    )
    first, second = swap(own, "gx", 0), swap(own, "gx", 1)
    c_rows, n_rows, u_rows, b_rows, v_row = call(
        pack_rows, [rows, rows, (2, count, width), rows, (count, width)], "pack_rows"
    )(*depths, tracers, uvel, vvel, tracer_bar)
    to_north, to_south = call(
        join_rows, [(7 * count + 24, width), (6 * count + 24, width)], "join_rows", [SMEM] + [VMEM] * 11
    )(parity, *depths, eta_bar, own, first, second, c_rows, n_rows, u_rows, b_rows, v_row)
    from_south, from_north = shift(to_north, "gy", 1), shift(to_south, "gy", -1)
    ext = (height + 8, 2 * width)

    def surface(*refs):
        surface_kernel(*refs, count=count)

    basis, level_ext, sums = call(
        surface, [(3,) + ext, ext, (devices, width)], "surface", [SMEM] + [VMEM] * 7
    )(parity, *depths, eta_bar, first, second, from_north, from_south)
    all_sums = lax.all_to_all(sums.reshape(devices, 1, width), ("gx", "gy"), 0, 0).reshape(devices, width)
    taller = (height + 8, width)
    base, flows = call(
        column_kernel,
        [(2, count) + tile, (4, count) + tile],
        "columns",
        [SMEM] + [VMEM] * 14,
        [
            pltpu.VMEM((4, 8 * count, width), F32),
            pltpu.VMEM((4, width, width), F32),
            pltpu.VMEM((count,) + taller, F32),
            pltpu.VMEM((count,) + taller, F32),
            pltpu.VMEM((4, count) + taller, F32),
            pltpu.VMEM((2, count) + tile, F32),
        ],
        pl.CostEstimate(flops=400 * count * height * width, transcendentals=count * height * width, bytes_accessed=1 << 22),
    )(parity, *depths, tracers, uvel, vvel, tracer_bar, own, first, second, c_rows, v_row, from_north, from_south, level_ext)
    tracer_adj, eta_adj = call(final_kernel, [tracers.shape, tile], "finish")(all_sums, basis, level_ext, base, flows)
    return (tracer_adj, eta_adj)


def solution(mesh):
    return jax.shard_map(
        per_device,
        mesh=mesh,
        in_specs=(
            P(None, None, "gy", "gx"),
            P(None, "gy", "gx"),
            P(None, "gy", "gx"),
            P("gy", "gx"),
            P("gy", "gx"),
            P(None, None, "gy", "gx"),
            P("gy", "gx"),
        ),
        out_specs=(P(None, None, "gy", "gx"), P("gy", "gx")),
        check_vma=False,
    )
```

```python
import jax
import jax.numpy as jnp
from jax import lax
from jax.experimental import pallas as pl
from jax.experimental.pallas import tpu as pltpu
from jax.sharding import PartitionSpec as P

advect_rate = 0.25
mix_floor = 0.2
mix_boost = 2.0
mix_slope = 2.0
mix_rate = 1.0
surface_stiffness = 2.0
thermal_steric = 0.5
haline_steric = 0.5
sterics = (thermal_steric, -haline_steric)
spread = 4.0 * surface_stiffness
F32 = jnp.float32
VMEM = pl.BlockSpec(memory_space=pltpu.VMEM)
SMEM = pl.BlockSpec(memory_space=pltpu.SMEM)
HBM = pl.BlockSpec(memory_space=pltpu.HBM)
vmem_grant = 8 << 20
chunk = 6
U_TILE, V_TILE, BAR_TILE, SURFACE_TILE = 2, 3, 4, 6


def lanes_of(shape):
    return lax.broadcasted_iota(jnp.int32, shape, 1)


def rows_of(shape):
    return lax.broadcasted_iota(jnp.int32, shape, 0)


def roll(cells, shift, axis):
    size = cells.shape[axis]
    shift = shift % size
    return cells if shift == 0 else pltpu.roll(cells, shift, axis)


def layer_rows(count, width):
    return rows_of((count, width)).astype(F32)


def pack_columns(
    mask_in, levels_in, eta_in, tracer_in, u_in, v_in, bar_in,
    out_ref, level_ref, eta_ref, tracer_ref, u_ref, v_ref, bar_ref,
    mask_ref, levels_ref, sems,
):
    pairs = (
        (tracer_in, tracer_ref), (u_in, u_ref), (v_in, v_ref), (bar_in, bar_ref),
        (mask_in, mask_ref), (levels_in, levels_ref), (eta_in, eta_ref),
    )
    copies = [pltpu.make_async_copy(source, target, sems.at[i]) for i, (source, target) in enumerate(pairs)]
    for copy in copies:
        copy.start()
    count, height, width = u_ref.shape
    lane = lanes_of((height, width))
    group = lane // 4
    fields = (
        (copies[0], tracer_ref.at[0]), (None, tracer_ref.at[1]), (copies[1], u_ref), (copies[2], v_ref),
        (copies[3], bar_ref.at[0]), (None, bar_ref.at[1]),
    )
    for index, (copy, field) in enumerate(fields):
        if copy is not None:
            copy.wait()
        tile = jnp.zeros((height, width), F32)
        for k in range(count):
            tile = jnp.where(group == k, roll(field[k], 4 * k + 2, 1), tile)
        out_ref[index] = tile
    for copy in copies[4:]:
        copy.wait()
    level = (mask_ref[...] * levels_ref[...]).astype(F32)
    level_ref[...] = level
    depth = jnp.where(lane < width // 2, roll(level, 3, 1), roll(level, -3, 1))
    out_ref[SURFACE_TILE] = jnp.where((lane < 3) | (lane >= width - 3), eta_ref[...], depth)


class Sides:
    def __init__(self, parity_ref, first_ref, second_ref, level):
        self.parity = parity_ref[0]
        self.refs = (first_ref, second_ref)
        self.level = level
        self.shape = level.shape
        lane = lanes_of(self.shape)
        self.lane = lane
        self.layer = (lane // 4).astype(F32)
        self.eastern = lane % 4 == 1
        east, west = self.pick(SURFACE_TILE)
        half = lane < self.shape[1] // 2
        self.eta = jnp.where(half, east, west)
        self.depth = jnp.where(half, roll(self.eta, -3, 1), roll(self.eta, 3, 1))

    def pick(self, tile):
        first, second = (ref[tile] for ref in self.refs)
        even = is_even(self.parity, self.shape)
        return jnp.where(even, first, second), jnp.where(even, second, first)

    def inner(self, tile):
        east, west = self.pick(tile)
        return jnp.where(self.eastern, roll(east, -1, 1), roll(west, 1, 1))

    def outer(self, tile):
        east, west = self.pick(tile)
        return jnp.where(self.eastern, roll(east, -2, 1), roll(west, 2, 1))

    def columns(self, cells, east, west):
        return jnp.where(self.eastern, cells[:, east : east + 1], cells[:, west : west + 1])

    def edge_flow(self, own_ref, u_inner):
        width = self.shape[1]
        own_depth = self.columns(self.level, width - 1, 0)
        beyond = self.columns(self.depth, 0, width - 1)
        flow = jnp.where(self.eastern, own_ref[U_TILE], u_inner)
        return jnp.where(self.layer < jnp.minimum(own_depth, beyond), flow, 0.0)


def pack_rows(level_ref, tracer_ref, u_ref, v_ref, bar_ref, c_out, n_out, u_out, b_out, v_out):
    count, height, width = u_ref.shape
    level = level_ref[...]
    layer = layer_rows(count, width)
    for side, (row, inside, face) in enumerate(((height - 1, height - 2, height - 2), (0, 1, 0))):
        depth = jnp.minimum(level[row : row + 1, :], level[inside : inside + 1, :])
        flow = jnp.where(layer < depth, 0.5 * v_ref[:, face, :], 0.0)
        u_out[side] = u_ref[:, row, :]
        for f in range(2):
            part = slice(f * count, (f + 1) * count)
            c = tracer_ref[f, :, row, :]
            c_out[side, part, :] = c
            n_out[side, part, :] = flow * (c + tracer_ref[f, :, inside, :])
            b_out[side, part, :] = bar_ref[f, :, row, :]
    v_out[...] = jnp.where(layer < level[height - 1 :, :], v_ref[:, height - 1, :], 0.0)


class Message:
    def __init__(self, count):
        self.tracers = [slice(f * count, (f + 1) * count) for f in range(2)]
        self.summed = [slice(f * count, (f + 1) * count) for f in range(2, 4)]
        self.bars = [slice(f * count, (f + 1) * count) for f in range(4, 6)]
        self.v = slice(6 * count, 7 * count)
        self.surface = [slice(7 * count + 8 * i, 7 * count + 8 * i + 8) for i in range(2)]
        self.corner = slice(7 * count + 16, 7 * count + 24)
        self.rows = 7 * count + 24


def is_even(index, shape):
    return jnp.full(shape, index, jnp.int32) == 0


def join_rows(
    parity_ref, level_ref, eta_ref, own_ref, first_ref, second_ref, c_ref, n_ref, u_ref, b_ref, v_ref,
    first_out, second_out,
):
    count, width = v_ref.shape
    level = level_ref[...]
    height = level.shape[0]
    plan = Message(count)
    sides = Sides(parity_ref, first_ref, second_ref, level)
    inner = [sides.inner(f) for f in range(2)]
    v_inner = sides.inner(V_TILE)
    flow = 0.5 * sides.edge_flow(own_ref, sides.inner(U_TILE))
    flux = [flow * (own_ref[f] + inner[f]) for f in range(2)]
    layer = layer_rows(count, width)
    lane = lanes_of((count, width))
    level_row = rows_of((count, width))
    row8 = rows_of((8, width))
    no_flow, pad = jnp.zeros((count, width), F32), jnp.zeros((8, width), F32)

    def put(part, north, south):
        even = is_even(parity_ref[1], north.shape)
        first_out[part, :] = jnp.where(even, north, south)
        second_out[part, :] = jnp.where(even, south, north)

    def summed(side, f, row, sign):
        depth = level[row : row + 1, :]
        east_flow = jnp.where(layer < jnp.minimum(depth, roll(depth, -1, 1)), 0.5 * u_ref[side], 0.0)
        rate = jnp.where(layer < depth, advect_rate, 0.0)
        c = c_ref[side, plan.tracers[f], :]
        line = flux[f][row : row + 1, :]
        east_end, west_end = (
            jnp.sum(jnp.where(lane == 4 * level_row + m, line, 0.0), axis=1, keepdims=True) for m in (1, 2)
        )
        flux_e = jnp.where(lane == width - 1, east_end, east_flow * (c + roll(c, -1, 1)))
        flux_w = jnp.where(lane == 0, west_end, roll(flux_e, 1, 1))
        return c - rate * ((flux_e - flux_w) + sign * n_ref[side, plan.tracers[f], :])

    for f in range(2):
        part = plan.tracers[f]
        put(part, c_ref[0, part, :], c_ref[1, part, :])
        put(plan.summed[f], summed(0, f, height - 1, -1.0), summed(1, f, 0, 1.0))
        put(plan.bars[f], b_ref[0, part, :], b_ref[1, part, :])
    put(plan.v, v_ref[...], no_flow)
    for part, eta, depth in zip(plan.surface, (eta_ref[...], sides.eta), (level, sides.depth)):
        north = jnp.where(row8 < 4, roll(depth[height - 8 :, :], 4, 0), eta[height - 8 :, :])
        put(part, north, jnp.where(row8 < 4, eta[:8, :], roll(depth[:8, :], 4, 0)))
    lines = [inner[0], inner[1], v_inner]
    north = south = pad
    for index, cells in enumerate(lines):
        north = jnp.where(row8 == index, cells[height - 1 :, :], north)
        south = jnp.where(row8 == index, cells[:1, :], south)
    put(plan.corner, north, south)


def extended(own, side, north, south, turn):
    row8 = rows_of((8, own.shape[1]))
    parts = []
    for index, tile in enumerate((own, side)):
        up, down = (roll(msg[index], turn, 0) for msg in (north, south))
        parts.append(jnp.concatenate([tile, jnp.where(row8 < 4, up, down)], axis=0))
    return jnp.concatenate(parts, axis=1)


def surface_kernel(
    parity_ref, level_ref, eta_ref, first_ref, second_ref, first_row, second_row,
    basis_out, level_out, sums_out, *, count,
):
    level = level_ref[...]
    height, width = level.shape
    sides = Sides(parity_ref, first_ref, second_ref, level)
    north, south = [], []
    for part in Message(count).surface:
        even = is_even(parity_ref[1], (8, width))
        north.append(jnp.where(even, first_row[part, :], second_row[part, :]))
        south.append(jnp.where(even, second_row[part, :], first_row[part, :]))
    eta_ext = extended(eta_ref[...], sides.eta, north, south, 0)
    level_ext = extended(level, sides.depth, north, south, 4)
    level_out[...] = level_ext
    depth = level_ext / count
    east_weight = (surface_stiffness / spread) * jnp.minimum(depth, roll(depth, -1, 1))
    north_weight = (surface_stiffness / spread) * jnp.minimum(depth, roll(depth, -1, 0))

    west_weight, south_weight = roll(east_weight, 1, 1), roll(north_weight, 1, 0)

    def scaled(field):
        along_x = east_weight * (field - roll(field, -1, 1)) + west_weight * (field - roll(field, 1, 1))
        along_y = north_weight * (field - roll(field, -1, 0)) + south_weight * (field - roll(field, 1, 0))
        return along_x + along_y

    first = scaled(eta_ext)
    second = scaled(first) - first
    third = scaled(second)
    basis_out[0] = eta_ext
    basis_out[1] = first
    basis_out[2] = second
    vectors = [x[:height, :width] for x in (eta_ext, first, second, third)]
    pairs = ((0, 0), (0, 1), (0, 2), (1, 1), (1, 2), (2, 2), (2, 3))
    row = rows_of((8, width))
    table = jnp.zeros((8, width), F32)
    for index, (a, b) in enumerate(pairs):
        table = jnp.where(row == index, jnp.sum(vectors[a] * vectors[b], axis=0, keepdims=True), table)
    totals = jnp.sum(table, axis=1, keepdims=True)
    line = jnp.sum(jnp.where(lanes_of((8, width)) == row, totals, 0.0), axis=0, keepdims=True)
    sums_out[...] = jnp.broadcast_to(line, sums_out.shape)


def galerkin(sums):
    d00, d01, d02, d11, d12, d22, d2q = [sums[:, i : i + 1] for i in range(7)]
    k00 = d00 + spread * d01
    k01 = d01 + spread * d11
    k02 = d02 + spread * d12
    k11 = d11 + spread * (d11 + d12)
    k12 = d12 + spread * (d12 + d22)
    k22 = d22 + spread * d2q
    i00 = 1.0 / k00
    s11 = k11 - k01 * k01 * i00
    s12 = k12 - k01 * k02 * i00
    s22 = k22 - k02 * k02 * i00
    g1 = spread * (d01 * d01 - d00 * d11) * i00
    g2 = spread * (d02 * d01 - d00 * d12) * i00
    i11 = 1.0 / s11
    c12 = s12 * i11
    last = s22 - s12 * c12
    y2 = jnp.where(last > 4e-7 * s22, (g2 - g1 * c12) / last, 0.0)
    y1 = (g1 - s12 * y2) * i11
    y0 = (d00 - k01 * y1 - k02 * y2) * i00
    return y0, y1, y2


def column_kernel(
    parity_ref, tracer_ref, u_ref, v_ref, bar_ref,
    own_ref, first_ref, second_ref, c_rows, v_row, first_row, second_row, level_ref,
    base_out, flow_out,
    side_ref, turn_ref, ratio_ref, slope_ref, value_ref, adjoint_ref,
):
    count, height, width = u_ref.shape
    level_ext = level_ref[...]
    level = level_ext[:height, :width]
    sides = Sides(parity_ref, first_ref, second_ref, level)
    lane, row = lanes_of((height, width)), rows_of((height, width))
    layer = layer_rows(count, width)
    last_row, last_lane = level_ext.shape[0] - 1, level_ext.shape[1] - 1
    plan = Message(count)

    def from_north(part):
        even = is_even(parity_ref[1], (part.stop - part.start, width))
        return jnp.where(even, first_row[part, :], second_row[part, :])

    def from_south(part):
        even = is_even(parity_ref[1], (part.stop - part.start, width))
        return jnp.where(even, second_row[part, :], first_row[part, :])


    inner = [sides.inner(f) for f in range(2)]
    u_inner, v_inner = sides.inner(U_TILE), sides.inner(V_TILE)
    edge_flow = sides.edge_flow(own_ref, u_inner)
    edge_flux = [0.5 * edge_flow * (own_ref[f] + inner[f]) for f in range(2)]
    depth_in = sides.columns(sides.depth, 0, width - 1)
    depth_out = sides.columns(sides.depth, 1, width - 2)
    far_flow = jnp.where(sides.eastern, u_inner, sides.outer(U_TILE))
    far_flow = jnp.where(sides.layer < jnp.minimum(depth_in, depth_out), far_flow, 0.0)
    corner_depth = [
        jnp.where(sides.eastern[:1], level_ext[r : r + 1, width : width + 1], level_ext[r : r + 1, last_lane:])
        for r in (height, last_row)
    ]
    corner_north, corner_south = from_north(plan.corner), from_south(plan.corner)
    depth_up = jnp.where(row == height - 1, corner_depth[0], roll(depth_in, -1, 0))
    up_flow = jnp.where(sides.layer < jnp.minimum(depth_in, depth_up), v_inner, 0.0)
    low_flow = jnp.where(
        sides.layer[:1] < jnp.minimum(depth_in[:1], corner_depth[1]), corner_south[2:3, :], 0.0
    )
    rate = jnp.where(sides.layer < depth_in, advect_rate, 0.0)
    outward = jnp.where(sides.eastern, 1.0, -1.0)
    beyond = []
    for f in range(2):
        c = inner[f]
        far_flux = 0.5 * far_flow * (c + sides.outer(f))
        c_up = jnp.where(row == height - 1, corner_north[f : f + 1, :], roll(c, -1, 0))
        flux_n = 0.5 * up_flow * (c + c_up)
        low_flux = 0.5 * low_flow * (corner_south[f : f + 1, :] + c[:1])
        flux_s = jnp.where(row == 0, low_flux, roll(flux_n, 1, 0))
        beyond.append(c - rate * (outward * (far_flux - edge_flux[f]) + (flux_n - flux_s)))
    beyond += [sides.inner(BAR_TILE), sides.inner(BAR_TILE + 1), depth_in]
    filler = jnp.zeros((width - height * len(beyond), width), F32)
    turned = jnp.transpose(jnp.concatenate(beyond + [filler], axis=0))

    south_flow = jnp.where(layer < level[:1, :], from_south(plan.v), 0.0)
    north_flow = jnp.where(layer < level_ext[height : height + 1, :width], v_row[...], 0.0)
    south_flux, north_flux = [], []
    side_ref[...] = jnp.zeros_like(side_ref)
    for f in range(2):
        part = plan.tracers[f]
        south_flux.append(0.5 * south_flow * (from_south(part) + c_rows[1, part, :]))
        north_flux.append(0.5 * north_flow * (c_rows[0, part, :] + from_north(part)))
        side_ref[f, pl.ds(4, count, stride=8), :] = from_south(plan.summed[f]) - advect_rate * south_flux[f]
        side_ref[f, pl.ds(5, count, stride=8), :] = from_north(plan.summed[f]) + advect_rate * north_flux[f]
        side_ref[2 + f, pl.ds(4, count, stride=8), :] = from_south(plan.bars[f])
        side_ref[2 + f, pl.ds(5, count, stride=8), :] = from_north(plan.bars[f])
    for f in range(4):
        turn_ref[f] = roll(turned, -height * f, 1)
        for m in (1, 2):
            side_ref[f, pl.ds(m, count, stride=8), :] = turn_ref[f, pl.ds(m, count, stride=4), :]
    row8 = rows_of((8, width))
    side_level = roll(turned[:8, :], -4 * height, 1)
    side_level = jnp.where((row8 == 1) | (row8 == 2), side_level, 0.0)
    side_level = jnp.where(row8 == 4, level_ext[last_row:, :width], side_level)
    side_level = jnp.where(row8 == 5, level_ext[height : height + 1, :width], side_level)
    level_all = jnp.concatenate([level, side_level], axis=0)

    east_depth = jnp.minimum(level_ext, roll(level_ext, -1, 1))[:height, :width]
    north_depth = jnp.minimum(level_ext, roll(level_ext, -1, 0))[:height, :width]

    def with_side(own, f, k):
        return jnp.concatenate([own, side_ref[f, 8 * k : 8 * k + 8, :]], axis=0)

    def advected(k):
        flow_e = jnp.where(east_depth > k, 0.5 * u_ref[k], 0.0)
        flow_n = jnp.where(north_depth > k, 0.5 * v_ref[k], 0.0)
        wet_rate = jnp.where(level > k, advect_rate, 0.0)
        result = []
        for f in range(2):
            c = tracer_ref[f, k]
            ends = roll(edge_flux[f], -(4 * k + 2), 1)
            flux_e = jnp.where(lane == width - 1, ends, flow_e * (c + roll(c, -1, 1)))
            flux_w = jnp.where(lane == 0, ends, roll(flux_e, 1, 1))
            flux_n = jnp.where(row == height - 1, north_flux[f][k : k + 1, :], flow_n * (c + roll(c, -1, 0)))
            flux_s = jnp.where(row == 0, south_flux[f][k : k + 1, :], roll(flux_n, 1, 0))
            result.append(with_side(c - wet_rate * ((flux_e - flux_w) + (flux_n - flux_s)), f, k))
        return result

    now = advected(0)
    kappa_up = ratio_up = values = None
    for k in range(count):
        diagonal = 1.0
        kappa = later = None
        if k < count - 1:
            later = advected(k + 1)
            step = (now[1] - now[0]) - (later[1] - later[0])
            gate = jax.nn.sigmoid(mix_slope * step)
            wet_below = level_all > k + 1
            kappa = jnp.where(wet_below, mix_floor + mix_boost * gate, 0.0)
            slope_ref[k] = jnp.where(wet_below, (mix_boost * mix_slope) * gate * (1.0 - gate), 0.0)
            diagonal = diagonal + mix_rate * kappa
        if k > 0:
            diagonal = diagonal + mix_rate * kappa_up * (1.0 - ratio_up)
        inverse = 1.0 / diagonal
        right = [now[0], now[1], with_side(bar_ref[0, k], 2, k), with_side(bar_ref[1, k], 3, k)]
        if k > 0:
            right = [cells + mix_rate * kappa_up * value for cells, value in zip(right, values)]
        values = [cells * inverse for cells in right]
        for f in range(4):
            value_ref[f, k] = values[f]
        if kappa is not None:
            ratio_up, kappa_up = mix_rate * kappa * inverse, kappa
            ratio_ref[k] = ratio_up
        now = later

    def emit(k, cells, change):
        for f, sign in ((0, -1.0), (1, 1.0)):
            full = cells[2 + f] + sign * change
            adjoint_ref[f, k] = full[:height, :]
            side_ref[f, 8 * k : 8 * k + 8, :] = full[height:, :]

    below = values
    pull_below = None
    for k in range(count - 2, -1, -1):
        here = [value_ref[f, k] + ratio_ref[k] * below[f] for f in range(4)]
        pull = (-mix_rate) * slope_ref[k] * (
            (here[2] - below[2]) * (here[0] - below[0]) + (here[3] - below[3]) * (here[1] - below[1])
        )
        emit(k + 1, below, -pull if pull_below is None else pull_below - pull)
        below, pull_below = here, pull
    emit(0, below, pull_below)

    for f in range(2):
        for m in (1, 2):
            turn_ref[f, pl.ds(m, count, stride=4), :] = side_ref[f, pl.ds(m, count, stride=8), :]
    wide = lanes_of((width, width)) < height
    back = jnp.transpose(jnp.where(wide, turn_ref[0], roll(turn_ref[1], height, 1)))
    ends_of = [back[f * height : (f + 1) * height, :] for f in range(2)]
    south_line = [side_ref[f, pl.ds(4, count, stride=8), :] for f in range(2)]
    north_line = [side_ref[f, pl.ds(5, count, stride=8), :] for f in range(2)]
    for k in range(count):
        flow_e = jnp.where(east_depth > k, u_ref[k], 0.0)
        flow_n = jnp.where(north_depth > k, v_ref[k], 0.0)
        ends_flow = roll(edge_flow, -(4 * k + 2), 1)
        low = south_flow[k : k + 1, :]
        flow_out[0, k] = flow_e
        flow_out[1, k] = jnp.where(lane == 0, ends_flow, roll(flow_e, 1, 1))
        flow_out[2, k] = flow_n
        flow_out[3, k] = jnp.where(row == 0, low, roll(flow_n, 1, 0))
        for f in range(2):
            y = adjoint_ref[f, k]
            ends = roll(ends_of[f], -(4 * k + 2), 1)
            y_east = jnp.where(lane == width - 1, ends, roll(y, -1, 1))
            y_north = jnp.where(row == height - 1, north_line[f][k : k + 1, :], roll(y, -1, 0))
            part_e = flow_e * (y - y_east)
            part_n = flow_n * (y - y_north)
            part_w = jnp.where(lane == 0, ends_flow * (ends - y), roll(part_e, 1, 1))
            part_s = jnp.where(row == 0, low * (south_line[f][k : k + 1, :] - y), roll(part_n, 1, 0))
            base_out[f, k] = y - (0.5 * advect_rate) * ((part_e + part_w) + (part_n + part_s))


def final_kernel(sums_ref, basis_ref, level_ref, base_ref, flow_ref, tracer_hbm, eta_hbm, tracer_out, eta_out, sems):
    _, count, height, width = base_ref.shape
    y0, y1, y2 = galerkin(jnp.sum(sums_ref[...], axis=0, keepdims=True))
    eta_ext = y0 * basis_ref[0] + (y1 * basis_ref[1] + y2 * basis_ref[2])
    eta = eta_ext[:height, :width]
    level = level_ref[:height, :width]
    eta_out[...] = eta
    copies = [pltpu.make_async_copy(eta_out, eta_hbm, sems.at[0])]
    copies[0].start()
    half = 0.5 * advect_rate
    east = half * (eta_ext - roll(eta_ext, -1, 1))
    north = half * (eta_ext - roll(eta_ext, -1, 0))
    west = roll(east, 1, 1)[:height, :width]
    south = roll(north, 1, 0)[:height, :width]
    east, north = east[:height, :width], north[:height, :width]
    for k in range(count):
        part = (flow_ref[0, k] * east + flow_ref[1, k] * west) + (flow_ref[2, k] * north + flow_ref[3, k] * south)
        share = jnp.where(level > k, eta, 0.0) - part
        for f in range(2):
            tracer_out[f, k] = base_ref[f, k] + sterics[f] * share
        if (k + 1) % chunk == 0 or k == count - 1:
            levels = pl.ds(k - k % chunk, k % chunk + 1)
            at = len(copies)
            copies.append(pltpu.make_async_copy(tracer_out.at[:, levels], tracer_hbm.at[:, levels], sems.at[at]))
            copies[-1].start()
    for copy in copies:
        copy.wait()


def call(kernel, outs, name, specs=None, scratch=(), cost=None, out_spec=VMEM):
    def run(*operands):
        return pl.pallas_call(
            kernel,
            out_shape=[jax.ShapeDtypeStruct(shape, F32) for shape in outs],
            in_specs=specs or [VMEM] * len(operands),
            out_specs=[out_spec] * len(outs),
            scratch_shapes=list(scratch),
            cost_estimate=cost,
            compiler_params=pltpu.CompilerParams(vmem_limit_bytes=vmem_grant),
            name=name,
        )(*operands)

    return run


def swap(cells, axis, first, wrap):
    count = lax.axis_size(axis)
    pairs = []
    for i in range(first, count, 2):
        if i + 1 < count or wrap:
            j = (i + 1) % count
            pairs += [(i, j), (j, i)]
    return lax.ppermute(cells, axis, pairs)


def per_device(tracers, uvel, vvel, sea_mask, levels, tracer_bar, eta_bar):
    _, count, height, width = tracers.shape
    devices = lax.axis_size("gx") * lax.axis_size("gy")
    tile = (height, width)
    rows = (2, 2 * count, width)
    parity = jnp.stack([lax.axis_index("gx") % 2, lax.axis_index("gy") % 2]).astype(jnp.int32)
    field = (count,) + tile
    inputs = (sea_mask, levels, eta_bar, tracers, uvel, vvel, tracer_bar)
    own, level, eta, tracers, uvel, vvel, tracer_bar = call(
        pack_columns,
        [(SURFACE_TILE + 1,) + tile, tile, tile, (2,) + field, field, field, (2,) + field],
        "pack_columns",
        [HBM] * 7,
        [pltpu.VMEM(tile, jnp.int32), pltpu.VMEM(tile, jnp.int32), pltpu.SemaphoreType.DMA((7,))],
    )(*(pltpu.with_memory_space_constraint(x, pltpu.HBM) for x in inputs))
    first, second = swap(own, "gx", 0, True), swap(own, "gx", 1, True)
    c_rows, n_rows, u_rows, b_rows, v_row = call(
        pack_rows, [rows, rows, (2, count, width), rows, (count, width)], "pack_rows"
    )(level, tracers, uvel, vvel, tracer_bar)
    plan = Message(count)
    message = (plan.rows, width)
    first_msg, second_msg = call(join_rows, [message, message], "join_rows", [SMEM] + [VMEM] * 10)(
        parity, level, eta, own, first, second, c_rows, n_rows, u_rows, b_rows, v_row
    )
    first_row, second_row = swap(first_msg, "gy", 0, False), swap(second_msg, "gy", 1, False)
    ext = (height + 8, 2 * width)

    def surface(*refs):
        surface_kernel(*refs, count=count)

    basis, level_ext, sums = call(surface, [(3,) + ext, ext, (devices, width)], "surface", [SMEM] + [VMEM] * 6)(
        parity, level, eta, first, second, first_row, second_row
    )
    all_sums = lax.all_to_all(sums.reshape(devices, 1, width), ("gx", "gy"), 0, 0).reshape(devices, width)
    taller = (count, height + 8, width)
    base, flows = call(
        column_kernel,
        [(2,) + field, (4,) + field],
        "columns",
        [SMEM] + [VMEM] * 12,
        [
            pltpu.VMEM((4, 8 * count, width), F32),
            pltpu.VMEM((4, width, width), F32),
            pltpu.VMEM(taller, F32),
            pltpu.VMEM(taller, F32),
            pltpu.VMEM((4,) + taller, F32),
            pltpu.VMEM((2,) + field, F32),
        ],
        pl.CostEstimate(flops=400 * count * height * width, transcendentals=count * height * width, bytes_accessed=1 << 22),
    )(parity, tracers, uvel, vvel, tracer_bar, own, first, second, c_rows, v_row, first_row, second_row, level_ext)
    pieces = (count + chunk - 1) // chunk
    tracer_adj, eta_adj = call(
        final_kernel,
        [(2,) + field, tile],
        "finish",
        None,
        [pltpu.VMEM((2,) + field, F32), pltpu.VMEM(tile, F32), pltpu.SemaphoreType.DMA((pieces + 1,))],
        out_spec=HBM,
    )(all_sums, basis, level_ext, base, flows)
    return (tracer_adj, eta_adj)


def solution(mesh):
    return jax.shard_map(
        per_device,
        mesh=mesh,
        in_specs=(
            P(None, None, "gy", "gx"),
            P(None, "gy", "gx"),
            P(None, "gy", "gx"),
            P("gy", "gx"),
            P("gy", "gx"),
            P(None, None, "gy", "gx"),
            P("gy", "gx"),
        ),
        out_specs=(P(None, None, "gy", "gx"), P("gy", "gx")),
        check_vma=False,
    )
```

```python
import jax
import jax.numpy as jnp
from jax import lax
from jax.experimental import pallas as pl
from jax.experimental.pallas import tpu as pltpu
from jax.sharding import PartitionSpec as P

advect_rate = 0.25
mix_floor = 0.2
mix_boost = 2.0
mix_slope = 2.0
mix_rate = 1.0
surface_stiffness = 2.0
thermal_steric = 0.5
haline_steric = 0.5
sterics = (thermal_steric, -haline_steric)
spread = 4.0 * surface_stiffness
F32 = jnp.float32
VMEM = pl.BlockSpec(memory_space=pltpu.VMEM)
HBM = pl.BlockSpec(memory_space=pltpu.HBM)
vmem_grant = 8 << 20
chunk = 6
U_TILE, V_TILE, BAR_TILE, SURFACE_TILE = 2, 3, 4, 6


def lanes_of(shape):
    return lax.broadcasted_iota(jnp.int32, shape, 1)


def rows_of(shape):
    return lax.broadcasted_iota(jnp.int32, shape, 0)


def roll(cells, shift, axis):
    size = cells.shape[axis]
    shift = shift % size
    return cells if shift == 0 else pltpu.roll(cells, shift, axis)


def layer_rows(count, width):
    return rows_of((count, width)).astype(F32)


def pack_columns(
    mask_in, levels_in, eta_in, tracer_in, u_in, v_in, bar_in,
    out_ref, level_ref, eta_ref, tracer_ref, u_ref, v_ref, bar_ref,
    mask_ref, levels_ref, sems,
):
    pairs = (
        (tracer_in, tracer_ref), (u_in, u_ref), (v_in, v_ref), (bar_in, bar_ref),
        (mask_in, mask_ref), (levels_in, levels_ref), (eta_in, eta_ref),
    )
    copies = [pltpu.make_async_copy(source, target, sems.at[i]) for i, (source, target) in enumerate(pairs)]
    for copy in copies:
        copy.start()
    count, height, width = u_ref.shape
    lane = lanes_of((height, width))
    group = lane // 4
    fields = (
        (copies[0], tracer_ref.at[0]), (None, tracer_ref.at[1]), (copies[1], u_ref), (copies[2], v_ref),
        (copies[3], bar_ref.at[0]), (None, bar_ref.at[1]),
    )
    for index, (copy, field) in enumerate(fields):
        if copy is not None:
            copy.wait()
        tile = jnp.zeros((height, width), F32)
        for k in range(count):
            tile = jnp.where(group == k, roll(field[k], 4 * k + 2, 1), tile)
        out_ref[index] = tile
    for copy in copies[4:]:
        copy.wait()
    level = (mask_ref[...] * levels_ref[...]).astype(F32)
    level_ref[...] = level
    depth = jnp.where(lane < width // 2, roll(level, 3, 1), roll(level, -3, 1))
    out_ref[SURFACE_TILE] = jnp.where((lane < 3) | (lane >= width - 3), eta_ref[...], depth)


class Sides:
    def __init__(self, first_ref, second_ref, level):
        self.refs = (first_ref, second_ref)
        self.level = level
        self.shape = level.shape
        lane = lanes_of(self.shape)
        self.lane = lane
        self.layer = (lane // 4).astype(F32)
        self.eastern = lane % 4 == 1
        east, west = self.pick(SURFACE_TILE)
        half = lane < self.shape[1] // 2
        self.eta = jnp.where(half, east, west)
        self.depth = jnp.where(half, roll(self.eta, -3, 1), roll(self.eta, 3, 1))

    def pick(self, tile):
        first, second = (ref[tile] for ref in self.refs)
        even = is_even("gx", self.shape)
        return jnp.where(even, first, second), jnp.where(even, second, first)

    def inner(self, tile):
        east, west = self.pick(tile)
        return jnp.where(self.eastern, roll(east, -1, 1), roll(west, 1, 1))

    def outer(self, tile):
        east, west = self.pick(tile)
        return jnp.where(self.eastern, roll(east, -2, 1), roll(west, 2, 1))

    def columns(self, cells, east, west):
        return jnp.where(self.eastern, cells[:, east : east + 1], cells[:, west : west + 1])

    def edge_flow(self, own_ref, u_inner):
        width = self.shape[1]
        own_depth = self.columns(self.level, width - 1, 0)
        beyond = self.columns(self.depth, 0, width - 1)
        flow = jnp.where(self.eastern, own_ref[U_TILE], u_inner)
        return jnp.where(self.layer < jnp.minimum(own_depth, beyond), flow, 0.0)


def pack_rows(level_ref, tracer_ref, u_ref, v_ref, bar_ref, c_out, n_out, u_out, b_out, v_out):
    count, height, width = u_ref.shape
    level = level_ref[...]
    layer = layer_rows(count, width)
    for side, (row, inside, face) in enumerate(((height - 1, height - 2, height - 2), (0, 1, 0))):
        depth = jnp.minimum(level[row : row + 1, :], level[inside : inside + 1, :])
        flow = jnp.where(layer < depth, 0.5 * v_ref[:, face, :], 0.0)
        u_out[side] = u_ref[:, row, :]
        for f in range(2):
            part = slice(f * count, (f + 1) * count)
            c = tracer_ref[f, :, row, :]
            c_out[side, part, :] = c
            n_out[side, part, :] = flow * (c + tracer_ref[f, :, inside, :])
            b_out[side, part, :] = bar_ref[f, :, row, :]
    v_out[...] = jnp.where(layer < level[height - 1 :, :], v_ref[:, height - 1, :], 0.0)


class Message:
    def __init__(self, count):
        self.tracers = [slice(f * count, (f + 1) * count) for f in range(2)]
        self.summed = [slice(f * count, (f + 1) * count) for f in range(2, 4)]
        self.bars = [slice(f * count, (f + 1) * count) for f in range(4, 6)]
        self.v = slice(6 * count, 7 * count)
        self.surface = [slice(7 * count + 8 * i, 7 * count + 8 * i + 8) for i in range(2)]
        self.corner = slice(7 * count + 16, 7 * count + 24)
        self.rows = 7 * count + 24


def is_even(axis, shape):
    return jnp.full(shape, lax.rem(lax.axis_index(axis), 2), jnp.int32) == 0


def join_rows(
    level_ref, eta_ref, own_ref, first_ref, second_ref, c_ref, n_ref, u_ref, b_ref, v_ref,
    first_out, second_out,
):
    count, width = v_ref.shape
    level = level_ref[...]
    height = level.shape[0]
    plan = Message(count)
    sides = Sides(first_ref, second_ref, level)
    inner = [sides.inner(f) for f in range(2)]
    v_inner = sides.inner(V_TILE)
    flow = 0.5 * sides.edge_flow(own_ref, sides.inner(U_TILE))
    flux = [flow * (own_ref[f] + inner[f]) for f in range(2)]
    layer = layer_rows(count, width)
    lane = lanes_of((count, width))
    level_row = rows_of((count, width))
    row8 = rows_of((8, width))
    no_flow, pad = jnp.zeros((count, width), F32), jnp.zeros((8, width), F32)

    def put(part, north, south):
        even = is_even("gy", north.shape)
        first_out[part, :] = jnp.where(even, north, south)
        second_out[part, :] = jnp.where(even, south, north)

    def summed(side, f, row, sign):
        depth = level[row : row + 1, :]
        east_flow = jnp.where(layer < jnp.minimum(depth, roll(depth, -1, 1)), 0.5 * u_ref[side], 0.0)
        rate = jnp.where(layer < depth, advect_rate, 0.0)
        c = c_ref[side, plan.tracers[f], :]
        line = flux[f][row : row + 1, :]
        east_end, west_end = (
            jnp.sum(jnp.where(lane == 4 * level_row + m, line, 0.0), axis=1, keepdims=True) for m in (1, 2)
        )
        flux_e = jnp.where(lane == width - 1, east_end, east_flow * (c + roll(c, -1, 1)))
        flux_w = jnp.where(lane == 0, west_end, roll(flux_e, 1, 1))
        return c - rate * ((flux_e - flux_w) + sign * n_ref[side, plan.tracers[f], :])

    for f in range(2):
        part = plan.tracers[f]
        put(part, c_ref[0, part, :], c_ref[1, part, :])
        put(plan.summed[f], summed(0, f, height - 1, -1.0), summed(1, f, 0, 1.0))
        put(plan.bars[f], b_ref[0, part, :], b_ref[1, part, :])
    put(plan.v, v_ref[...], no_flow)
    for part, eta, depth in zip(plan.surface, (eta_ref[...], sides.eta), (level, sides.depth)):
        north = jnp.where(row8 < 4, roll(depth[height - 8 :, :], 4, 0), eta[height - 8 :, :])
        put(part, north, jnp.where(row8 < 4, eta[:8, :], roll(depth[:8, :], 4, 0)))
    lines = [inner[0], inner[1], v_inner]
    north = south = pad
    for index, cells in enumerate(lines):
        north = jnp.where(row8 == index, cells[height - 1 :, :], north)
        south = jnp.where(row8 == index, cells[:1, :], south)
    put(plan.corner, north, south)


def extended(own, side, north, south, turn):
    row8 = rows_of((8, own.shape[1]))
    parts = []
    for index, tile in enumerate((own, side)):
        up, down = (roll(msg[index], turn, 0) for msg in (north, south))
        parts.append(jnp.concatenate([tile, jnp.where(row8 < 4, up, down)], axis=0))
    return jnp.concatenate(parts, axis=1)


def surface_kernel(
    level_ref, eta_ref, first_ref, second_ref, first_row, second_row,
    basis_out, level_out, sums_out, *, count,
):
    level = level_ref[...]
    height, width = level.shape
    sides = Sides(first_ref, second_ref, level)
    north, south = [], []
    for part in Message(count).surface:
        even = is_even("gy", (8, width))
        north.append(jnp.where(even, first_row[part, :], second_row[part, :]))
        south.append(jnp.where(even, second_row[part, :], first_row[part, :]))
    eta_ext = extended(eta_ref[...], sides.eta, north, south, 0)
    level_ext = extended(level, sides.depth, north, south, 4)
    level_out[...] = level_ext
    depth = level_ext / count
    east_weight = (surface_stiffness / spread) * jnp.minimum(depth, roll(depth, -1, 1))
    north_weight = (surface_stiffness / spread) * jnp.minimum(depth, roll(depth, -1, 0))

    west_weight, south_weight = roll(east_weight, 1, 1), roll(north_weight, 1, 0)

    def scaled(field):
        along_x = east_weight * (field - roll(field, -1, 1)) + west_weight * (field - roll(field, 1, 1))
        along_y = north_weight * (field - roll(field, -1, 0)) + south_weight * (field - roll(field, 1, 0))
        return along_x + along_y

    first = scaled(eta_ext)
    second = scaled(first) - first
    third = scaled(second)
    basis_out[0] = eta_ext
    basis_out[1] = first
    basis_out[2] = second
    vectors = [x[:height, :width] for x in (eta_ext, first, second, third)]
    pairs = ((0, 0), (0, 1), (0, 2), (1, 1), (1, 2), (2, 2), (2, 3))
    row = rows_of((8, width))
    table = jnp.zeros((8, width), F32)
    for index, (a, b) in enumerate(pairs):
        table = jnp.where(row == index, jnp.sum(vectors[a] * vectors[b], axis=0, keepdims=True), table)
    totals = jnp.sum(table, axis=1, keepdims=True)
    line = jnp.sum(jnp.where(lanes_of((8, width)) == row, totals, 0.0), axis=0, keepdims=True)
    sums_out[...] = jnp.broadcast_to(line, sums_out.shape)


def galerkin(sums):
    d00, d01, d02, d11, d12, d22, d2q = [sums[:, i : i + 1] for i in range(7)]
    k00 = d00 + spread * d01
    k01 = d01 + spread * d11
    k02 = d02 + spread * d12
    k11 = d11 + spread * (d11 + d12)
    k12 = d12 + spread * (d12 + d22)
    k22 = d22 + spread * d2q
    i00 = 1.0 / k00
    s11 = k11 - k01 * k01 * i00
    s12 = k12 - k01 * k02 * i00
    s22 = k22 - k02 * k02 * i00
    g1 = spread * (d01 * d01 - d00 * d11) * i00
    g2 = spread * (d02 * d01 - d00 * d12) * i00
    i11 = 1.0 / s11
    c12 = s12 * i11
    last = s22 - s12 * c12
    y2 = jnp.where(last > 4e-7 * s22, (g2 - g1 * c12) / last, 0.0)
    y1 = (g1 - s12 * y2) * i11
    y0 = (d00 - k01 * y1 - k02 * y2) * i00
    return y0, y1, y2


def column_kernel(
    tracer_ref, u_ref, v_ref, bar_ref,
    own_ref, first_ref, second_ref, c_rows, v_row, first_row, second_row, level_ref,
    base_out, flow_out,
    side_ref, turn_ref, ratio_ref, slope_ref, value_ref, adjoint_ref,
):
    count, height, width = u_ref.shape
    level_ext = level_ref[...]
    level = level_ext[:height, :width]
    sides = Sides(first_ref, second_ref, level)
    lane, row = lanes_of((height, width)), rows_of((height, width))
    layer = layer_rows(count, width)
    last_row, last_lane = level_ext.shape[0] - 1, level_ext.shape[1] - 1
    plan = Message(count)

    def from_north(part):
        even = is_even("gy", (part.stop - part.start, width))
        return jnp.where(even, first_row[part, :], second_row[part, :])

    def from_south(part):
        even = is_even("gy", (part.stop - part.start, width))
        return jnp.where(even, second_row[part, :], first_row[part, :])


    inner = [sides.inner(f) for f in range(2)]
    u_inner, v_inner = sides.inner(U_TILE), sides.inner(V_TILE)
    edge_flow = sides.edge_flow(own_ref, u_inner)
    edge_flux = [0.5 * edge_flow * (own_ref[f] + inner[f]) for f in range(2)]
    depth_in = sides.columns(sides.depth, 0, width - 1)
    depth_out = sides.columns(sides.depth, 1, width - 2)
    far_flow = jnp.where(sides.eastern, u_inner, sides.outer(U_TILE))
    far_flow = jnp.where(sides.layer < jnp.minimum(depth_in, depth_out), far_flow, 0.0)
    corner_depth = [
        jnp.where(sides.eastern[:1], level_ext[r : r + 1, width : width + 1], level_ext[r : r + 1, last_lane:])
        for r in (height, last_row)
    ]
    corner_north, corner_south = from_north(plan.corner), from_south(plan.corner)
    depth_up = jnp.where(row == height - 1, corner_depth[0], roll(depth_in, -1, 0))
    up_flow = jnp.where(sides.layer < jnp.minimum(depth_in, depth_up), v_inner, 0.0)
    low_flow = jnp.where(
        sides.layer[:1] < jnp.minimum(depth_in[:1], corner_depth[1]), corner_south[2:3, :], 0.0
    )
    rate = jnp.where(sides.layer < depth_in, advect_rate, 0.0)
    outward = jnp.where(sides.eastern, 1.0, -1.0)
    beyond = []
    for f in range(2):
        c = inner[f]
        far_flux = 0.5 * far_flow * (c + sides.outer(f))
        c_up = jnp.where(row == height - 1, corner_north[f : f + 1, :], roll(c, -1, 0))
        flux_n = 0.5 * up_flow * (c + c_up)
        low_flux = 0.5 * low_flow * (corner_south[f : f + 1, :] + c[:1])
        flux_s = jnp.where(row == 0, low_flux, roll(flux_n, 1, 0))
        beyond.append(c - rate * (outward * (far_flux - edge_flux[f]) + (flux_n - flux_s)))
    beyond += [sides.inner(BAR_TILE), sides.inner(BAR_TILE + 1), depth_in]
    filler = jnp.zeros((width - height * len(beyond), width), F32)
    turned = jnp.transpose(jnp.concatenate(beyond + [filler], axis=0))

    south_flow = jnp.where(layer < level[:1, :], from_south(plan.v), 0.0)
    north_flow = jnp.where(layer < level_ext[height : height + 1, :width], v_row[...], 0.0)
    south_flux, north_flux = [], []
    side_ref[...] = jnp.zeros_like(side_ref)
    for f in range(2):
        part = plan.tracers[f]
        south_flux.append(0.5 * south_flow * (from_south(part) + c_rows[1, part, :]))
        north_flux.append(0.5 * north_flow * (c_rows[0, part, :] + from_north(part)))
        side_ref[f, pl.ds(4, count, stride=8), :] = from_south(plan.summed[f]) - advect_rate * south_flux[f]
        side_ref[f, pl.ds(5, count, stride=8), :] = from_north(plan.summed[f]) + advect_rate * north_flux[f]
        side_ref[2 + f, pl.ds(4, count, stride=8), :] = from_south(plan.bars[f])
        side_ref[2 + f, pl.ds(5, count, stride=8), :] = from_north(plan.bars[f])
    for f in range(4):
        turn_ref[f] = roll(turned, -height * f, 1)
        for m in (1, 2):
            side_ref[f, pl.ds(m, count, stride=8), :] = turn_ref[f, pl.ds(m, count, stride=4), :]
    row8 = rows_of((8, width))
    side_level = roll(turned[:8, :], -4 * height, 1)
    side_level = jnp.where((row8 == 1) | (row8 == 2), side_level, 0.0)
    side_level = jnp.where(row8 == 4, level_ext[last_row:, :width], side_level)
    side_level = jnp.where(row8 == 5, level_ext[height : height + 1, :width], side_level)
    level_all = jnp.concatenate([level, side_level], axis=0)

    east_depth = jnp.minimum(level_ext, roll(level_ext, -1, 1))[:height, :width]
    north_depth = jnp.minimum(level_ext, roll(level_ext, -1, 0))[:height, :width]

    def with_side(own, f, k):
        return jnp.concatenate([own, side_ref[f, 8 * k : 8 * k + 8, :]], axis=0)

    def advected(k):
        flow_e = jnp.where(east_depth > k, 0.5 * u_ref[k], 0.0)
        flow_n = jnp.where(north_depth > k, 0.5 * v_ref[k], 0.0)
        wet_rate = jnp.where(level > k, advect_rate, 0.0)
        result = []
        for f in range(2):
            c = tracer_ref[f, k]
            ends = roll(edge_flux[f], -(4 * k + 2), 1)
            flux_e = jnp.where(lane == width - 1, ends, flow_e * (c + roll(c, -1, 1)))
            flux_w = jnp.where(lane == 0, ends, roll(flux_e, 1, 1))
            flux_n = jnp.where(row == height - 1, north_flux[f][k : k + 1, :], flow_n * (c + roll(c, -1, 0)))
            flux_s = jnp.where(row == 0, south_flux[f][k : k + 1, :], roll(flux_n, 1, 0))
            result.append(with_side(c - wet_rate * ((flux_e - flux_w) + (flux_n - flux_s)), f, k))
        return result

    now = advected(0)
    kappa_up = ratio_up = values = None
    for k in range(count):
        diagonal = 1.0
        kappa = later = None
        if k < count - 1:
            later = advected(k + 1)
            step = (now[1] - now[0]) - (later[1] - later[0])
            gate = jax.nn.sigmoid(mix_slope * step)
            wet_below = level_all > k + 1
            kappa = jnp.where(wet_below, mix_floor + mix_boost * gate, 0.0)
            slope_ref[k] = jnp.where(wet_below, (mix_boost * mix_slope) * gate * (1.0 - gate), 0.0)
            diagonal = diagonal + mix_rate * kappa
        if k > 0:
            diagonal = diagonal + mix_rate * kappa_up * (1.0 - ratio_up)
        inverse = 1.0 / diagonal
        right = [now[0], now[1], with_side(bar_ref[0, k], 2, k), with_side(bar_ref[1, k], 3, k)]
        if k > 0:
            right = [cells + mix_rate * kappa_up * value for cells, value in zip(right, values)]
        values = [cells * inverse for cells in right]
        for f in range(4):
            value_ref[f, k] = values[f]
        if kappa is not None:
            ratio_up, kappa_up = mix_rate * kappa * inverse, kappa
            ratio_ref[k] = ratio_up
        now = later

    def emit(k, cells, change):
        for f, sign in ((0, -1.0), (1, 1.0)):
            full = cells[2 + f] + sign * change
            adjoint_ref[f, k] = full[:height, :]
            side_ref[f, 8 * k : 8 * k + 8, :] = full[height:, :]

    below = values
    pull_below = None
    for k in range(count - 2, -1, -1):
        here = [value_ref[f, k] + ratio_ref[k] * below[f] for f in range(4)]
        pull = (-mix_rate) * slope_ref[k] * (
            (here[2] - below[2]) * (here[0] - below[0]) + (here[3] - below[3]) * (here[1] - below[1])
        )
        emit(k + 1, below, -pull if pull_below is None else pull_below - pull)
        below, pull_below = here, pull
    emit(0, below, pull_below)

    for f in range(2):
        for m in (1, 2):
            turn_ref[f, pl.ds(m, count, stride=4), :] = side_ref[f, pl.ds(m, count, stride=8), :]
    wide = lanes_of((width, width)) < height
    back = jnp.transpose(jnp.where(wide, turn_ref[0], roll(turn_ref[1], height, 1)))
    ends_of = [back[f * height : (f + 1) * height, :] for f in range(2)]
    south_line = [side_ref[f, pl.ds(4, count, stride=8), :] for f in range(2)]
    north_line = [side_ref[f, pl.ds(5, count, stride=8), :] for f in range(2)]
    for k in range(count):
        flow_e = jnp.where(east_depth > k, u_ref[k], 0.0)
        flow_n = jnp.where(north_depth > k, v_ref[k], 0.0)
        ends_flow = roll(edge_flow, -(4 * k + 2), 1)
        low = south_flow[k : k + 1, :]
        flow_out[0, k] = flow_e
        flow_out[1, k] = jnp.where(lane == 0, ends_flow, roll(flow_e, 1, 1))
        flow_out[2, k] = flow_n
        flow_out[3, k] = jnp.where(row == 0, low, roll(flow_n, 1, 0))
        for f in range(2):
            y = adjoint_ref[f, k]
            ends = roll(ends_of[f], -(4 * k + 2), 1)
            y_east = jnp.where(lane == width - 1, ends, roll(y, -1, 1))
            y_north = jnp.where(row == height - 1, north_line[f][k : k + 1, :], roll(y, -1, 0))
            part_e = flow_e * (y - y_east)
            part_n = flow_n * (y - y_north)
            part_w = jnp.where(lane == 0, ends_flow * (ends - y), roll(part_e, 1, 1))
            part_s = jnp.where(row == 0, low * (south_line[f][k : k + 1, :] - y), roll(part_n, 1, 0))
            base_out[f, k] = y - (0.5 * advect_rate) * ((part_e + part_w) + (part_n + part_s))


def final_kernel(sums_ref, basis_ref, level_ref, base_ref, flow_ref, tracer_hbm, eta_hbm, tracer_out, eta_out, sems):
    _, count, height, width = base_ref.shape
    y0, y1, y2 = galerkin(jnp.sum(sums_ref[...], axis=0, keepdims=True))
    eta_ext = y0 * basis_ref[0] + (y1 * basis_ref[1] + y2 * basis_ref[2])
    eta = eta_ext[:height, :width]
    level = level_ref[:height, :width]
    eta_out[...] = eta
    copies = [pltpu.make_async_copy(eta_out, eta_hbm, sems.at[0])]
    copies[0].start()
    half = 0.5 * advect_rate
    east = half * (eta_ext - roll(eta_ext, -1, 1))
    north = half * (eta_ext - roll(eta_ext, -1, 0))
    west = roll(east, 1, 1)[:height, :width]
    south = roll(north, 1, 0)[:height, :width]
    east, north = east[:height, :width], north[:height, :width]
    for k in range(count):
        part = (flow_ref[0, k] * east + flow_ref[1, k] * west) + (flow_ref[2, k] * north + flow_ref[3, k] * south)
        share = jnp.where(level > k, eta, 0.0) - part
        for f in range(2):
            tracer_out[f, k] = base_ref[f, k] + sterics[f] * share
        if (k + 1) % chunk == 0 or k == count - 1:
            levels = pl.ds(k - k % chunk, k % chunk + 1)
            at = len(copies)
            copies.append(pltpu.make_async_copy(tracer_out.at[:, levels], tracer_hbm.at[:, levels], sems.at[at]))
            copies[-1].start()
    for copy in copies:
        copy.wait()


def call(kernel, outs, name, specs=None, scratch=(), cost=None, out_spec=VMEM):
    def run(*operands):
        return pl.pallas_call(
            kernel,
            out_shape=[jax.ShapeDtypeStruct(shape, F32) for shape in outs],
            in_specs=specs or [VMEM] * len(operands),
            out_specs=[out_spec] * len(outs),
            scratch_shapes=list(scratch),
            cost_estimate=cost,
            compiler_params=pltpu.CompilerParams(vmem_limit_bytes=vmem_grant),
            name=name,
        )(*operands)

    return run


def swap(cells, axis, first, wrap):
    count = lax.axis_size(axis)
    pairs = []
    for i in range(first, count, 2):
        if i + 1 < count or wrap:
            j = (i + 1) % count
            pairs += [(i, j), (j, i)]
    return lax.ppermute(cells, axis, pairs)


def per_device(tracers, uvel, vvel, sea_mask, levels, tracer_bar, eta_bar):
    _, count, height, width = tracers.shape
    devices = lax.axis_size("gx") * lax.axis_size("gy")
    tile = (height, width)
    rows = (2, 2 * count, width)
    field = (count,) + tile
    inputs = (sea_mask, levels, eta_bar, tracers, uvel, vvel, tracer_bar)
    own, level, eta, tracers, uvel, vvel, tracer_bar = call(
        pack_columns,
        [(SURFACE_TILE + 1,) + tile, tile, tile, (2,) + field, field, field, (2,) + field],
        "pack_columns",
        [HBM] * 7,
        [pltpu.VMEM(tile, jnp.int32), pltpu.VMEM(tile, jnp.int32), pltpu.SemaphoreType.DMA((7,))],
    )(*(pltpu.with_memory_space_constraint(x, pltpu.HBM) for x in inputs))
    first, second = swap(own, "gx", 0, True), swap(own, "gx", 1, True)
    c_rows, n_rows, u_rows, b_rows, v_row = call(
        pack_rows, [rows, rows, (2, count, width), rows, (count, width)], "pack_rows"
    )(level, tracers, uvel, vvel, tracer_bar)
    plan = Message(count)
    message = (plan.rows, width)
    first_msg, second_msg = call(join_rows, [message, message], "join_rows")(
        level, eta, own, first, second, c_rows, n_rows, u_rows, b_rows, v_row
    )
    first_row, second_row = swap(first_msg, "gy", 0, False), swap(second_msg, "gy", 1, False)
    ext = (height + 8, 2 * width)

    def surface(*refs):
        surface_kernel(*refs, count=count)

    basis, level_ext, sums = call(surface, [(3,) + ext, ext, (devices, width)], "surface")(
        level, eta, first, second, first_row, second_row
    )
    all_sums = lax.all_to_all(sums.reshape(devices, 1, width), ("gx", "gy"), 0, 0).reshape(devices, width)
    taller = (count, height + 8, width)
    base, flows = call(
        column_kernel,
        [(2,) + field, (4,) + field],
        "columns",
        None,
        [
            pltpu.VMEM((4, 8 * count, width), F32),
            pltpu.VMEM((4, width, width), F32),
            pltpu.VMEM(taller, F32),
            pltpu.VMEM(taller, F32),
            pltpu.VMEM((4,) + taller, F32),
            pltpu.VMEM((2,) + field, F32),
        ],
        pl.CostEstimate(flops=400 * count * height * width, transcendentals=count * height * width, bytes_accessed=1 << 22),
    )(tracers, uvel, vvel, tracer_bar, own, first, second, c_rows, v_row, first_row, second_row, level_ext)
    pieces = (count + chunk - 1) // chunk
    tracer_adj, eta_adj = call(
        final_kernel,
        [(2,) + field, tile],
        "finish",
        None,
        [pltpu.VMEM((2,) + field, F32), pltpu.VMEM(tile, F32), pltpu.SemaphoreType.DMA((pieces + 1,))],
        out_spec=HBM,
    )(all_sums, basis, level_ext, base, flows)
    return (tracer_adj, eta_adj)


def solution(mesh):
    return jax.shard_map(
        per_device,
        mesh=mesh,
        in_specs=(
            P(None, None, "gy", "gx"),
            P(None, "gy", "gx"),
            P(None, "gy", "gx"),
            P("gy", "gx"),
            P("gy", "gx"),
            P(None, None, "gy", "gx"),
            P("gy", "gx"),
        ),
        out_specs=(P(None, None, "gy", "gx"), P("gy", "gx")),
        check_vma=False,
    )
```

```python
import jax
import jax.numpy as jnp
from jax import lax
from jax.experimental import pallas as pl
from jax.experimental.pallas import tpu as pltpu
from jax.sharding import PartitionSpec as P

advect_rate = 0.25
mix_floor = 0.2
mix_boost = 2.0
mix_slope = 2.0
mix_rate = 1.0
surface_stiffness = 2.0
thermal_steric = 0.5
haline_steric = 0.5
sterics = (thermal_steric, -haline_steric)
spread = 4.0 * surface_stiffness
F32 = jnp.float32
VMEM = pl.BlockSpec(memory_space=pltpu.VMEM)
HBM = pl.BlockSpec(memory_space=pltpu.HBM)
vmem_grant = 8 << 20
chunk = 6
U_TILE, V_TILE, BAR_TILE, SURFACE_TILE = 2, 3, 4, 6


def lanes_of(shape):
    return lax.broadcasted_iota(jnp.int32, shape, 1)


def rows_of(shape):
    return lax.broadcasted_iota(jnp.int32, shape, 0)


def roll(cells, shift, axis):
    size = cells.shape[axis]
    shift = shift % size
    return cells if shift == 0 else pltpu.roll(cells, shift, axis)


def layer_rows(count, width):
    return rows_of((count, width)).astype(F32)


def pack_columns(
    mask_in, levels_in, eta_in, tracer_in, u_in, v_in, bar_in,
    out_ref, level_ref, eta_ref, tracer_ref, u_ref, v_ref, bar_ref,
    mask_ref, levels_ref, sems,
):
    pairs = (
        (tracer_in, tracer_ref), (u_in, u_ref), (v_in, v_ref), (bar_in, bar_ref),
        (mask_in, mask_ref), (levels_in, levels_ref), (eta_in, eta_ref),
    )
    copies = [pltpu.make_async_copy(source, target, sems.at[i]) for i, (source, target) in enumerate(pairs)]
    for copy in copies:
        copy.start()
    count, height, width = u_ref.shape
    lane = lanes_of((height, width))
    group = lane // 4
    fields = (
        (copies[0], tracer_ref.at[0]), (None, tracer_ref.at[1]), (copies[1], u_ref), (copies[2], v_ref),
        (copies[3], bar_ref.at[0]), (None, bar_ref.at[1]),
    )
    for index, (copy, field) in enumerate(fields):
        if copy is not None:
            copy.wait()
        tile = jnp.zeros((height, width), F32)
        for k in range(count):
            tile = jnp.where(group == k, roll(field[k], 4 * k + 2, 1), tile)
        out_ref[index] = tile
    for copy in copies[4:]:
        copy.wait()
    level = (mask_ref[...] * levels_ref[...]).astype(F32)
    level_ref[...] = level
    depth = jnp.where(lane < width // 2, roll(level, 3, 1), roll(level, -3, 1))
    out_ref[SURFACE_TILE] = jnp.where((lane < 3) | (lane >= width - 3), eta_ref[...], depth)


class Sides:
    def __init__(self, first_ref, second_ref, level):
        self.refs = (first_ref, second_ref)
        self.level = level
        self.shape = level.shape
        lane = lanes_of(self.shape)
        self.lane = lane
        self.layer = (lane // 4).astype(F32)
        self.eastern = lane % 4 == 1
        east, west = self.pick(SURFACE_TILE)
        half = lane < self.shape[1] // 2
        self.eta = jnp.where(half, east, west)
        self.depth = jnp.where(half, roll(self.eta, -3, 1), roll(self.eta, 3, 1))

    def pick(self, tile):
        first, second = (ref[tile] for ref in self.refs)
        even = is_even("gx", self.shape)
        return jnp.where(even, first, second), jnp.where(even, second, first)

    def inner(self, tile):
        east, west = self.pick(tile)
        return jnp.where(self.eastern, roll(east, -1, 1), roll(west, 1, 1))

    def outer(self, tile):
        east, west = self.pick(tile)
        return jnp.where(self.eastern, roll(east, -2, 1), roll(west, 2, 1))

    def columns(self, cells, east, west):
        return jnp.where(self.eastern, cells[:, east : east + 1], cells[:, west : west + 1])

    def edge_flow(self, own_ref, u_inner):
        width = self.shape[1]
        own_depth = self.columns(self.level, width - 1, 0)
        beyond = self.columns(self.depth, 0, width - 1)
        flow = jnp.where(self.eastern, own_ref[U_TILE], u_inner)
        return jnp.where(self.layer < jnp.minimum(own_depth, beyond), flow, 0.0)


def pack_rows(level_ref, tracer_ref, u_ref, v_ref, bar_ref, c_out, n_out, u_out, b_out, v_out):
    count, height, width = u_ref.shape
    level = level_ref[...]
    layer = layer_rows(count, width)
    for side, (row, inside, face) in enumerate(((height - 1, height - 2, height - 2), (0, 1, 0))):
        depth = jnp.minimum(level[row : row + 1, :], level[inside : inside + 1, :])
        flow = jnp.where(layer < depth, 0.5 * v_ref[:, face, :], 0.0)
        u_out[side] = u_ref[:, row, :]
        for f in range(2):
            part = slice(f * count, (f + 1) * count)
            c = tracer_ref[f, :, row, :]
            c_out[side, part, :] = c
            n_out[side, part, :] = flow * (c + tracer_ref[f, :, inside, :])
            b_out[side, part, :] = bar_ref[f, :, row, :]
    v_out[...] = jnp.where(layer < level[height - 1 :, :], v_ref[:, height - 1, :], 0.0)


class Message:
    def __init__(self, count):
        self.tracers = [slice(f * count, (f + 1) * count) for f in range(2)]
        self.summed = [slice(f * count, (f + 1) * count) for f in range(2, 4)]
        self.bars = [slice(f * count, (f + 1) * count) for f in range(4, 6)]
        self.v = slice(6 * count, 7 * count)
        self.surface = [slice(7 * count + 8 * i, 7 * count + 8 * i + 8) for i in range(2)]
        self.corner = slice(7 * count + 16, 7 * count + 24)
        self.rows = 7 * count + 24


def is_even(axis, shape):
    return jnp.full(shape, lax.rem(lax.axis_index(axis), 2), jnp.int32) == 0


def join_rows(
    level_ref, eta_ref, own_ref, first_ref, second_ref, c_ref, n_ref, u_ref, b_ref, v_ref,
    first_out, second_out,
):
    count, width = v_ref.shape
    level = level_ref[...]
    height = level.shape[0]
    plan = Message(count)
    sides = Sides(first_ref, second_ref, level)
    inner = [sides.inner(f) for f in range(2)]
    v_inner = sides.inner(V_TILE)
    flow = 0.5 * sides.edge_flow(own_ref, sides.inner(U_TILE))
    flux = [flow * (own_ref[f] + inner[f]) for f in range(2)]
    layer = layer_rows(count, width)
    lane = lanes_of((count, width))
    level_row = rows_of((count, width))
    row8 = rows_of((8, width))
    no_flow, pad = jnp.zeros((count, width), F32), jnp.zeros((8, width), F32)

    def put(part, north, south):
        even = is_even("gy", north.shape)
        first_out[part, :] = jnp.where(even, south, north)
        second_out[part, :] = jnp.where(even, north, south)

    def summed(side, f, row, sign):
        depth = level[row : row + 1, :]
        east_flow = jnp.where(layer < jnp.minimum(depth, roll(depth, -1, 1)), 0.5 * u_ref[side], 0.0)
        rate = jnp.where(layer < depth, advect_rate, 0.0)
        c = c_ref[side, plan.tracers[f], :]
        line = flux[f][row : row + 1, :]
        east_end, west_end = (
            jnp.sum(jnp.where(lane == 4 * level_row + m, line, 0.0), axis=1, keepdims=True) for m in (1, 2)
        )
        flux_e = jnp.where(lane == width - 1, east_end, east_flow * (c + roll(c, -1, 1)))
        flux_w = jnp.where(lane == 0, west_end, roll(flux_e, 1, 1))
        return c - rate * ((flux_e - flux_w) + sign * n_ref[side, plan.tracers[f], :])

    for f in range(2):
        part = plan.tracers[f]
        put(part, c_ref[0, part, :], c_ref[1, part, :])
        put(plan.summed[f], summed(0, f, height - 1, -1.0), summed(1, f, 0, 1.0))
        put(plan.bars[f], b_ref[0, part, :], b_ref[1, part, :])
    put(plan.v, v_ref[...], no_flow)
    for part, eta, depth in zip(plan.surface, (eta_ref[...], sides.eta), (level, sides.depth)):
        north = jnp.where(row8 < 4, roll(depth[height - 8 :, :], 4, 0), eta[height - 8 :, :])
        put(part, north, jnp.where(row8 < 4, eta[:8, :], roll(depth[:8, :], 4, 0)))
    lines = [inner[0], inner[1], v_inner]
    north = south = pad
    for index, cells in enumerate(lines):
        north = jnp.where(row8 == index, cells[height - 1 :, :], north)
        south = jnp.where(row8 == index, cells[:1, :], south)
    put(plan.corner, north, south)


def extended(own, side, north, south, turn):
    row8 = rows_of((8, own.shape[1]))
    parts = []
    for index, tile in enumerate((own, side)):
        up, down = (roll(msg[index], turn, 0) for msg in (north, south))
        parts.append(jnp.concatenate([tile, jnp.where(row8 < 4, up, down)], axis=0))
    return jnp.concatenate(parts, axis=1)


def surface_kernel(
    level_ref, eta_ref, first_ref, second_ref, first_row, second_row,
    basis_out, level_out, sums_out, *, count,
):
    level = level_ref[...]
    height, width = level.shape
    sides = Sides(first_ref, second_ref, level)
    north, south = [], []
    for part in Message(count).surface:
        even = is_even("gy", (8, width))
        north.append(jnp.where(even, second_row[part, :], first_row[part, :]))
        south.append(jnp.where(even, first_row[part, :], second_row[part, :]))
    eta_ext = extended(eta_ref[...], sides.eta, north, south, 0)
    level_ext = extended(level, sides.depth, north, south, 4)
    level_out[...] = level_ext
    depth = level_ext / count
    east_weight = (surface_stiffness / spread) * jnp.minimum(depth, roll(depth, -1, 1))
    north_weight = (surface_stiffness / spread) * jnp.minimum(depth, roll(depth, -1, 0))

    west_weight, south_weight = roll(east_weight, 1, 1), roll(north_weight, 1, 0)

    def scaled(field):
        along_x = east_weight * (field - roll(field, -1, 1)) + west_weight * (field - roll(field, 1, 1))
        along_y = north_weight * (field - roll(field, -1, 0)) + south_weight * (field - roll(field, 1, 0))
        return along_x + along_y

    first = scaled(eta_ext)
    second = scaled(first) - first
    third = scaled(second)
    basis_out[0] = eta_ext
    basis_out[1] = first
    basis_out[2] = second
    vectors = [x[:height, :width] for x in (eta_ext, first, second, third)]
    pairs = ((0, 0), (0, 1), (0, 2), (1, 1), (1, 2), (2, 2), (2, 3))
    row = rows_of((8, width))
    table = jnp.zeros((8, width), F32)
    for index, (a, b) in enumerate(pairs):
        table = jnp.where(row == index, jnp.sum(vectors[a] * vectors[b], axis=0, keepdims=True), table)
    totals = jnp.sum(table, axis=1, keepdims=True)
    line = jnp.sum(jnp.where(lanes_of((8, width)) == row, totals, 0.0), axis=0, keepdims=True)
    sums_out[...] = jnp.broadcast_to(line, sums_out.shape)


def galerkin(sums):
    d00, d01, d02, d11, d12, d22, d2q = [sums[:, i : i + 1] for i in range(7)]
    k00 = d00 + spread * d01
    k01 = d01 + spread * d11
    k02 = d02 + spread * d12
    k11 = d11 + spread * (d11 + d12)
    k12 = d12 + spread * (d12 + d22)
    k22 = d22 + spread * d2q
    i00 = 1.0 / k00
    s11 = k11 - k01 * k01 * i00
    s12 = k12 - k01 * k02 * i00
    s22 = k22 - k02 * k02 * i00
    g1 = spread * (d01 * d01 - d00 * d11) * i00
    g2 = spread * (d02 * d01 - d00 * d12) * i00
    i11 = 1.0 / s11
    c12 = s12 * i11
    last = s22 - s12 * c12
    y2 = jnp.where(last > 4e-7 * s22, (g2 - g1 * c12) / last, 0.0)
    y1 = (g1 - s12 * y2) * i11
    y0 = (d00 - k01 * y1 - k02 * y2) * i00
    return y0, y1, y2


def column_kernel(
    tracer_ref, u_ref, v_ref, bar_ref,
    own_ref, first_ref, second_ref, c_rows, v_row, first_row, second_row, level_ref, basis_ref,
    base_out, share_out,
    side_ref, turn_ref, ratio_ref, slope_ref, value_ref, adjoint_ref,
):
    count, height, width = u_ref.shape
    level_ext = level_ref[...]
    level = level_ext[:height, :width]
    sides = Sides(first_ref, second_ref, level)
    lane, row = lanes_of((height, width)), rows_of((height, width))
    layer = layer_rows(count, width)
    last_row, last_lane = level_ext.shape[0] - 1, level_ext.shape[1] - 1
    plan = Message(count)

    def from_north(part):
        even = is_even("gy", (part.stop - part.start, width))
        return jnp.where(even, second_row[part, :], first_row[part, :])

    def from_south(part):
        even = is_even("gy", (part.stop - part.start, width))
        return jnp.where(even, first_row[part, :], second_row[part, :])


    inner = [sides.inner(f) for f in range(2)]
    u_inner, v_inner = sides.inner(U_TILE), sides.inner(V_TILE)
    edge_flow = sides.edge_flow(own_ref, u_inner)
    edge_flux = [0.5 * edge_flow * (own_ref[f] + inner[f]) for f in range(2)]
    depth_in = sides.columns(sides.depth, 0, width - 1)
    depth_out = sides.columns(sides.depth, 1, width - 2)
    far_flow = jnp.where(sides.eastern, u_inner, sides.outer(U_TILE))
    far_flow = jnp.where(sides.layer < jnp.minimum(depth_in, depth_out), far_flow, 0.0)
    corner_depth = [
        jnp.where(sides.eastern[:1], level_ext[r : r + 1, width : width + 1], level_ext[r : r + 1, last_lane:])
        for r in (height, last_row)
    ]
    corner_north, corner_south = from_north(plan.corner), from_south(plan.corner)
    depth_up = jnp.where(row == height - 1, corner_depth[0], roll(depth_in, -1, 0))
    up_flow = jnp.where(sides.layer < jnp.minimum(depth_in, depth_up), v_inner, 0.0)
    low_flow = jnp.where(
        sides.layer[:1] < jnp.minimum(depth_in[:1], corner_depth[1]), corner_south[2:3, :], 0.0
    )
    rate = jnp.where(sides.layer < depth_in, advect_rate, 0.0)
    outward = jnp.where(sides.eastern, 1.0, -1.0)
    beyond = []
    for f in range(2):
        c = inner[f]
        far_flux = 0.5 * far_flow * (c + sides.outer(f))
        c_up = jnp.where(row == height - 1, corner_north[f : f + 1, :], roll(c, -1, 0))
        flux_n = 0.5 * up_flow * (c + c_up)
        low_flux = 0.5 * low_flow * (corner_south[f : f + 1, :] + c[:1])
        flux_s = jnp.where(row == 0, low_flux, roll(flux_n, 1, 0))
        beyond.append(c - rate * (outward * (far_flux - edge_flux[f]) + (flux_n - flux_s)))
    beyond += [sides.inner(BAR_TILE), sides.inner(BAR_TILE + 1), depth_in]
    filler = jnp.zeros((width - height * len(beyond), width), F32)
    turned = jnp.transpose(jnp.concatenate(beyond + [filler], axis=0))

    south_flow = jnp.where(layer < level[:1, :], from_south(plan.v), 0.0)
    north_flow = jnp.where(layer < level_ext[height : height + 1, :width], v_row[...], 0.0)
    south_flux, north_flux = [], []
    side_ref[...] = jnp.zeros_like(side_ref)
    for f in range(2):
        part = plan.tracers[f]
        south_flux.append(0.5 * south_flow * (from_south(part) + c_rows[1, part, :]))
        north_flux.append(0.5 * north_flow * (c_rows[0, part, :] + from_north(part)))
        side_ref[f, pl.ds(4, count, stride=8), :] = from_south(plan.summed[f]) - advect_rate * south_flux[f]
        side_ref[f, pl.ds(5, count, stride=8), :] = from_north(plan.summed[f]) + advect_rate * north_flux[f]
        side_ref[2 + f, pl.ds(4, count, stride=8), :] = from_south(plan.bars[f])
        side_ref[2 + f, pl.ds(5, count, stride=8), :] = from_north(plan.bars[f])
    for f in range(4):
        turn_ref[f] = roll(turned, -height * f, 1)
        for m in (1, 2):
            side_ref[f, pl.ds(m, count, stride=8), :] = turn_ref[f, pl.ds(m, count, stride=4), :]
    row8 = rows_of((8, width))
    side_level = roll(turned[:8, :], -4 * height, 1)
    side_level = jnp.where((row8 == 1) | (row8 == 2), side_level, 0.0)
    side_level = jnp.where(row8 == 4, level_ext[last_row:, :width], side_level)
    side_level = jnp.where(row8 == 5, level_ext[height : height + 1, :width], side_level)
    level_all = jnp.concatenate([level, side_level], axis=0)

    east_depth = jnp.minimum(level_ext, roll(level_ext, -1, 1))[:height, :width]
    north_depth = jnp.minimum(level_ext, roll(level_ext, -1, 0))[:height, :width]

    def with_side(own, f, k):
        return jnp.concatenate([own, side_ref[f, 8 * k : 8 * k + 8, :]], axis=0)

    def advected(k):
        flow_e = jnp.where(east_depth > k, 0.5 * u_ref[k], 0.0)
        flow_n = jnp.where(north_depth > k, 0.5 * v_ref[k], 0.0)
        wet_rate = jnp.where(level > k, advect_rate, 0.0)
        result = []
        for f in range(2):
            c = tracer_ref[f, k]
            ends = roll(edge_flux[f], -(4 * k + 2), 1)
            flux_e = jnp.where(lane == width - 1, ends, flow_e * (c + roll(c, -1, 1)))
            flux_w = jnp.where(lane == 0, ends, roll(flux_e, 1, 1))
            flux_n = jnp.where(row == height - 1, north_flux[f][k : k + 1, :], flow_n * (c + roll(c, -1, 0)))
            flux_s = jnp.where(row == 0, south_flux[f][k : k + 1, :], roll(flux_n, 1, 0))
            result.append(with_side(c - wet_rate * ((flux_e - flux_w) + (flux_n - flux_s)), f, k))
        return result

    now = advected(0)
    kappa_up = ratio_up = values = None
    for k in range(count):
        diagonal = 1.0
        kappa = later = None
        if k < count - 1:
            later = advected(k + 1)
            step = (now[1] - now[0]) - (later[1] - later[0])
            gate = jax.nn.sigmoid(mix_slope * step)
            wet_below = level_all > k + 1
            kappa = jnp.where(wet_below, mix_floor + mix_boost * gate, 0.0)
            slope_ref[k] = jnp.where(wet_below, (mix_boost * mix_slope) * gate * (1.0 - gate), 0.0)
            diagonal = diagonal + mix_rate * kappa
        if k > 0:
            diagonal = diagonal + mix_rate * kappa_up * (1.0 - ratio_up)
        inverse = 1.0 / diagonal
        right = [now[0], now[1], with_side(bar_ref[0, k], 2, k), with_side(bar_ref[1, k], 3, k)]
        if k > 0:
            right = [cells + mix_rate * kappa_up * value for cells, value in zip(right, values)]
        values = [cells * inverse for cells in right]
        for f in range(4):
            value_ref[f, k] = values[f]
        if kappa is not None:
            ratio_up, kappa_up = mix_rate * kappa * inverse, kappa
            ratio_ref[k] = ratio_up
        now = later

    def emit(k, cells, change):
        for f, sign in ((0, -1.0), (1, 1.0)):
            full = cells[2 + f] + sign * change
            adjoint_ref[f, k] = full[:height, :]
            side_ref[f, 8 * k : 8 * k + 8, :] = full[height:, :]

    below = values
    pull_below = None
    for k in range(count - 2, -1, -1):
        here = [value_ref[f, k] + ratio_ref[k] * below[f] for f in range(4)]
        pull = (-mix_rate) * slope_ref[k] * (
            (here[2] - below[2]) * (here[0] - below[0]) + (here[3] - below[3]) * (here[1] - below[1])
        )
        emit(k + 1, below, -pull if pull_below is None else pull_below - pull)
        below, pull_below = here, pull
    emit(0, below, pull_below)

    for f in range(2):
        for m in (1, 2):
            turn_ref[f, pl.ds(m, count, stride=4), :] = side_ref[f, pl.ds(m, count, stride=8), :]
    wide = lanes_of((width, width)) < height
    back = jnp.transpose(jnp.where(wide, turn_ref[0], roll(turn_ref[1], height, 1)))
    ends_of = [back[f * height : (f + 1) * height, :] for f in range(2)]
    south_line = [side_ref[f, pl.ds(4, count, stride=8), :] for f in range(2)]
    north_line = [side_ref[f, pl.ds(5, count, stride=8), :] for f in range(2)]
    steps = []
    for b in range(3):
        field = basis_ref[b]
        east = (0.5 * advect_rate) * (field - roll(field, -1, 1))
        north = (0.5 * advect_rate) * (field - roll(field, -1, 0))
        around = (field, east, roll(east, 1, 1), north, roll(north, 1, 0))
        steps.append([cells[:height, :width] for cells in around])
    for k in range(count):
        flow_e = jnp.where(east_depth > k, u_ref[k], 0.0)
        flow_n = jnp.where(north_depth > k, v_ref[k], 0.0)
        ends_flow = roll(edge_flow, -(4 * k + 2), 1)
        low = south_flow[k : k + 1, :]
        flow_w = jnp.where(lane == 0, ends_flow, roll(flow_e, 1, 1))
        flow_s = jnp.where(row == 0, low, roll(flow_n, 1, 0))
        for b, (field, east, west, north, south) in enumerate(steps):
            part = (flow_e * east + flow_w * west) + (flow_n * north + flow_s * south)
            share_out[b, k] = jnp.where(level > k, field, 0.0) - part
        for f in range(2):
            y = adjoint_ref[f, k]
            ends = roll(ends_of[f], -(4 * k + 2), 1)
            y_east = jnp.where(lane == width - 1, ends, roll(y, -1, 1))
            y_north = jnp.where(row == height - 1, north_line[f][k : k + 1, :], roll(y, -1, 0))
            part_e = flow_e * (y - y_east)
            part_n = flow_n * (y - y_north)
            part_w = jnp.where(lane == 0, ends_flow * (ends - y), roll(part_e, 1, 1))
            part_s = jnp.where(row == 0, low * (south_line[f][k : k + 1, :] - y), roll(part_n, 1, 0))
            base_out[f, k] = y - (0.5 * advect_rate) * ((part_e + part_w) + (part_n + part_s))


def final_kernel(sums_ref, basis_ref, base_ref, share_ref, tracer_hbm, eta_hbm, tracer_out, eta_out, sems):
    _, count, height, width = base_ref.shape
    y0, y1, y2 = galerkin(jnp.sum(sums_ref[...], axis=0, keepdims=True))

    def combined(fields):
        return y0 * fields[0] + (y1 * fields[1] + y2 * fields[2])

    eta_out[...] = combined([basis_ref[b, :height, :width] for b in range(3)])
    copies = [pltpu.make_async_copy(eta_out, eta_hbm, sems.at[0])]
    copies[0].start()
    for k in range(count):
        share = combined([share_ref[b, k] for b in range(3)])
        for f in range(2):
            tracer_out[f, k] = base_ref[f, k] + sterics[f] * share
        if (k + 1) % chunk == 0 or k == count - 1:
            levels = pl.ds(k - k % chunk, k % chunk + 1)
            at = len(copies)
            copies.append(pltpu.make_async_copy(tracer_out.at[:, levels], tracer_hbm.at[:, levels], sems.at[at]))
            copies[-1].start()
    for copy in copies:
        copy.wait()


def call(kernel, outs, name, specs=None, scratch=(), cost=None, out_spec=VMEM):
    def run(*operands):
        return pl.pallas_call(
            kernel,
            out_shape=[jax.ShapeDtypeStruct(shape, F32) for shape in outs],
            in_specs=specs or [VMEM] * len(operands),
            out_specs=[out_spec] * len(outs),
            scratch_shapes=list(scratch),
            cost_estimate=cost,
            compiler_params=pltpu.CompilerParams(vmem_limit_bytes=vmem_grant),
            name=name,
        )(*operands)

    return run


def swap(cells, axis, first, wrap):
    count = lax.axis_size(axis)
    pairs = []
    for i in range(first, count, 2):
        if i + 1 < count or wrap:
            j = (i + 1) % count
            pairs += [(i, j), (j, i)]
    return lax.ppermute(cells, axis, pairs)


def per_device(tracers, uvel, vvel, sea_mask, levels, tracer_bar, eta_bar):
    _, count, height, width = tracers.shape
    devices = lax.axis_size("gx") * lax.axis_size("gy")
    tile = (height, width)
    rows = (2, 2 * count, width)
    field = (count,) + tile
    inputs = (sea_mask, levels, eta_bar, tracers, uvel, vvel, tracer_bar)
    own, level, eta, tracers, uvel, vvel, tracer_bar = call(
        pack_columns,
        [(SURFACE_TILE + 1,) + tile, tile, tile, (2,) + field, field, field, (2,) + field],
        "pack_columns",
        [HBM] * 7,
        [pltpu.VMEM(tile, jnp.int32), pltpu.VMEM(tile, jnp.int32), pltpu.SemaphoreType.DMA((7,))],
    )(*(pltpu.with_memory_space_constraint(x, pltpu.HBM) for x in inputs))
    first, second = swap(own, "gx", 0, True), swap(own, "gx", 1, True)
    c_rows, n_rows, u_rows, b_rows, v_row = call(
        pack_rows, [rows, rows, (2, count, width), rows, (count, width)], "pack_rows"
    )(level, tracers, uvel, vvel, tracer_bar)
    plan = Message(count)
    message = (plan.rows, width)
    first_msg, second_msg = call(join_rows, [message, message], "join_rows")(
        level, eta, own, first, second, c_rows, n_rows, u_rows, b_rows, v_row
    )
    first_row, second_row = swap(first_msg, "gy", 1, False), swap(second_msg, "gy", 0, False)
    ext = (height + 8, 2 * width)

    def surface(*refs):
        surface_kernel(*refs, count=count)

    basis, level_ext, sums = call(surface, [(3,) + ext, ext, (devices, width)], "surface")(
        level, eta, first, second, first_row, second_row
    )
    all_sums = lax.all_to_all(sums.reshape(devices, 1, width), ("gx", "gy"), 0, 0).reshape(devices, width)
    taller = (count, height + 8, width)
    base, shares = call(
        column_kernel,
        [(2,) + field, (3,) + field],
        "columns",
        None,
        [
            pltpu.VMEM((4, 8 * count, width), F32),
            pltpu.VMEM((4, width, width), F32),
            pltpu.VMEM(taller, F32),
            pltpu.VMEM(taller, F32),
            pltpu.VMEM((4,) + taller, F32),
            pltpu.VMEM((2,) + field, F32),
        ],
        pl.CostEstimate(flops=400 * count * height * width, transcendentals=count * height * width, bytes_accessed=1 << 22),
    )(tracers, uvel, vvel, tracer_bar, own, first, second, c_rows, v_row, first_row, second_row, level_ext, basis)
    pieces = (count + chunk - 1) // chunk
    tracer_adj, eta_adj = call(
        final_kernel,
        [(2,) + field, tile],
        "finish",
        None,
        [pltpu.VMEM((2,) + field, F32), pltpu.VMEM(tile, F32), pltpu.SemaphoreType.DMA((pieces + 1,))],
        out_spec=HBM,
    )(all_sums, basis, base, shares)
    return (tracer_adj, eta_adj)


def solution(mesh):
    return jax.shard_map(
        per_device,
        mesh=mesh,
        in_specs=(
            P(None, None, "gy", "gx"),
            P(None, "gy", "gx"),
            P(None, "gy", "gx"),
            P("gy", "gx"),
            P("gy", "gx"),
            P(None, None, "gy", "gx"),
            P("gy", "gx"),
        ),
        out_specs=(P(None, None, "gy", "gx"), P("gy", "gx")),
        check_vma=False,
    )
```

```python
import jax
import jax.numpy as jnp
from jax import lax
from jax.experimental import pallas as pl
from jax.experimental.pallas import tpu as pltpu
from jax.sharding import PartitionSpec as P

advect_rate = 0.25
mix_floor = 0.2
mix_boost = 2.0
mix_slope = 2.0
mix_rate = 1.0
surface_stiffness = 2.0
thermal_steric = 0.5
haline_steric = 0.5
sterics = (thermal_steric, -haline_steric)
spread = 4.0 * surface_stiffness
F32 = jnp.float32
VMEM = pl.BlockSpec(memory_space=pltpu.VMEM)
HBM = pl.BlockSpec(memory_space=pltpu.HBM)
vmem_grant = 8 << 20
chunk = 6
U_TILE, V_TILE, LAST_TILE = 2, 3, 4
surface_turn = 18


def lanes_of(shape):
    return lax.broadcasted_iota(jnp.int32, shape, 1)


def rows_of(shape):
    return lax.broadcasted_iota(jnp.int32, shape, 0)


def roll(cells, shift, axis):
    size = cells.shape[axis]
    shift = shift % size
    return cells if shift == 0 else pltpu.roll(cells, shift, axis)


def layer_rows(count, width):
    return rows_of((count, width)).astype(F32)


def pack_columns(
    mask_in, levels_in, eta_in, tracer_in, u_in, v_in, bar_in,
    out_ref, level_ref, eta_ref, tracer_ref, u_ref, v_ref, bar_ref,
    mask_ref, levels_ref, sems,
):
    pairs = (
        (tracer_in, tracer_ref), (u_in, u_ref), (v_in, v_ref), (bar_in, bar_ref),
        (mask_in, mask_ref), (levels_in, levels_ref), (eta_in, eta_ref),
    )
    copies = [pltpu.make_async_copy(source, target, sems.at[i]) for i, (source, target) in enumerate(pairs)]
    for copy in copies:
        copy.start()
    count, height, width = u_ref.shape
    lane = lanes_of((height, width))
    group = lane // 4
    middle = jnp.where((lane % 4 == 1) | (lane % 4 == 2), group, -1)
    beside = jnp.where((lane + 1) % 4 < 2, (lane + 1) // 4 - 1, -1)

    def gathered(field, place, turn, tile):
        for k in range(count):
            tile = jnp.where(place == k, roll(field[k], 4 * k + turn, 1), tile)
        return tile

    empty = jnp.zeros((height, width), F32)
    copies[0].wait()
    for f in range(2):
        out_ref[f] = gathered(tracer_ref.at[f], group, 2, empty)
    copies[1].wait()
    out_ref[U_TILE] = gathered(u_ref, group, 2, empty)
    copies[2].wait()
    v_tile = gathered(v_ref, middle, 2, empty)
    copies[3].wait()
    out_ref[V_TILE] = gathered(bar_ref.at[0], beside, 4, v_tile)
    last = gathered(bar_ref.at[1], middle, 2, empty)
    for copy in copies[4:]:
        copy.wait()
    level = (mask_ref[...] * levels_ref[...]).astype(F32)
    level_ref[...] = level
    depth = jnp.where(lane < width // 2, roll(level, 3, 1), roll(level, -3, 1))
    surface = roll(jnp.where((lane < 3) | (lane >= width - 3), eta_ref[...], depth), -surface_turn, 1)
    start = width - 6 - surface_turn
    out_ref[LAST_TILE] = jnp.where((lane >= start) & (lane < start + 12), surface, last)


class Sides:
    def __init__(self, first_ref, second_ref, level):
        self.refs = (first_ref, second_ref)
        self.level = level
        self.shape = level.shape
        lane = lanes_of(self.shape)
        self.lane = lane
        self.layer = (lane // 4).astype(F32)
        self.eastern = lane % 4 == 1
        east, west = (roll(tile, surface_turn, 1) for tile in self.pick(LAST_TILE))
        half = lane < self.shape[1] // 2
        self.eta = jnp.where(half, east, west)
        self.depth = jnp.where(half, roll(self.eta, -3, 1), roll(self.eta, 3, 1))

    def pick(self, tile):
        first, second = (ref[tile] for ref in self.refs)
        even = is_even("gx", self.shape)
        return jnp.where(even, first, second), jnp.where(even, second, first)

    def inner(self, tile):
        east, west = self.pick(tile)
        return jnp.where(self.eastern, roll(east, -1, 1), roll(west, 1, 1))

    def bars(self):
        east, west = self.pick(V_TILE)
        return [jnp.where(self.eastern, roll(east, -3, 1), roll(west, -1, 1)), self.inner(LAST_TILE)]

    def outer(self, tile):
        east, west = self.pick(tile)
        return jnp.where(self.eastern, roll(east, -2, 1), roll(west, 2, 1))

    def columns(self, cells, east, west):
        return jnp.where(self.eastern, cells[:, east : east + 1], cells[:, west : west + 1])

    def edge_flow(self, own_ref, u_inner):
        width = self.shape[1]
        own_depth = self.columns(self.level, width - 1, 0)
        beyond = self.columns(self.depth, 0, width - 1)
        flow = jnp.where(self.eastern, own_ref[U_TILE], u_inner)
        return jnp.where(self.layer < jnp.minimum(own_depth, beyond), flow, 0.0)


def pack_rows(level_ref, tracer_ref, u_ref, v_ref, bar_ref, c_out, n_out, u_out, b_out, v_out):
    count, height, width = u_ref.shape
    level = level_ref[...]
    layer = layer_rows(count, width)
    for side, (row, inside, face) in enumerate(((height - 1, height - 2, height - 2), (0, 1, 0))):
        depth = jnp.minimum(level[row : row + 1, :], level[inside : inside + 1, :])
        flow = jnp.where(layer < depth, 0.5 * v_ref[:, face, :], 0.0)
        u_out[side] = u_ref[:, row, :]
        for f in range(2):
            part = slice(f * count, (f + 1) * count)
            c = tracer_ref[f, :, row, :]
            c_out[side, part, :] = c
            n_out[side, part, :] = flow * (c + tracer_ref[f, :, inside, :])
            b_out[side, part, :] = bar_ref[f, :, row, :]
    v_out[...] = jnp.where(layer < level[height - 1 :, :], v_ref[:, height - 1, :], 0.0)


class Message:
    def __init__(self, count):
        self.tracers = [slice(f * count, (f + 1) * count) for f in range(2)]
        self.summed = [slice(f * count, (f + 1) * count) for f in range(2, 4)]
        self.bars = [slice(f * count, (f + 1) * count) for f in range(4, 6)]
        self.v = slice(6 * count, 7 * count)
        self.surface = [slice(7 * count + 8 * i, 7 * count + 8 * i + 8) for i in range(2)]
        self.corner = slice(7 * count + 16, 7 * count + 24)
        self.rows = 7 * count + 24


def is_even(axis, shape):
    return jnp.full(shape, lax.rem(lax.axis_index(axis), 2), jnp.int32) == 0


def join_rows(
    level_ref, eta_ref, own_ref, first_ref, second_ref, c_ref, n_ref, u_ref, b_ref, v_ref,
    first_out, second_out,
):
    count, width = v_ref.shape
    level = level_ref[...]
    height = level.shape[0]
    plan = Message(count)
    sides = Sides(first_ref, second_ref, level)
    inner = [sides.inner(f) for f in range(2)]
    v_inner = sides.inner(V_TILE)
    flow = 0.5 * sides.edge_flow(own_ref, sides.inner(U_TILE))
    flux = [flow * (own_ref[f] + inner[f]) for f in range(2)]
    layer = layer_rows(count, width)
    lane = lanes_of((count, width))
    level_row = rows_of((count, width))
    row8 = rows_of((8, width))
    no_flow, pad = jnp.zeros((count, width), F32), jnp.zeros((8, width), F32)

    def put(part, north, south):
        even = is_even("gy", north.shape)
        first_out[part, :] = jnp.where(even, south, north)
        second_out[part, :] = jnp.where(even, north, south)

    def summed(side, f, row, sign):
        depth = level[row : row + 1, :]
        east_flow = jnp.where(layer < jnp.minimum(depth, roll(depth, -1, 1)), 0.5 * u_ref[side], 0.0)
        rate = jnp.where(layer < depth, advect_rate, 0.0)
        c = c_ref[side, plan.tracers[f], :]
        line = flux[f][row : row + 1, :]
        east_end, west_end = (
            jnp.sum(jnp.where(lane == 4 * level_row + m, line, 0.0), axis=1, keepdims=True) for m in (1, 2)
        )
        flux_e = jnp.where(lane == width - 1, east_end, east_flow * (c + roll(c, -1, 1)))
        flux_w = jnp.where(lane == 0, west_end, roll(flux_e, 1, 1))
        return c - rate * ((flux_e - flux_w) + sign * n_ref[side, plan.tracers[f], :])

    for f in range(2):
        part = plan.tracers[f]
        put(part, c_ref[0, part, :], c_ref[1, part, :])
        put(plan.summed[f], summed(0, f, height - 1, -1.0), summed(1, f, 0, 1.0))
        put(plan.bars[f], b_ref[0, part, :], b_ref[1, part, :])
    put(plan.v, v_ref[...], no_flow)
    for part, eta, depth in zip(plan.surface, (eta_ref[...], sides.eta), (level, sides.depth)):
        north = jnp.where(row8 < 4, roll(depth[height - 8 :, :], 4, 0), eta[height - 8 :, :])
        put(part, north, jnp.where(row8 < 4, eta[:8, :], roll(depth[:8, :], 4, 0)))
    lines = [inner[0], inner[1], v_inner]
    north = south = pad
    for index, cells in enumerate(lines):
        north = jnp.where(row8 == index, cells[height - 1 :, :], north)
        south = jnp.where(row8 == index, cells[:1, :], south)
    put(plan.corner, north, south)


def extended(own, side, north, south, turn):
    row8 = rows_of((8, own.shape[1]))
    parts = []
    for index, tile in enumerate((own, side)):
        up, down = (roll(msg[index], turn, 0) for msg in (north, south))
        parts.append(jnp.concatenate([tile, jnp.where(row8 < 4, up, down)], axis=0))
    return jnp.concatenate(parts, axis=1)


def surface_kernel(
    level_ref, eta_ref, first_ref, second_ref, first_row, second_row,
    basis_out, level_out, sums_out, *, count,
):
    level = level_ref[...]
    height, width = level.shape
    sides = Sides(first_ref, second_ref, level)
    north, south = [], []
    for part in Message(count).surface:
        even = is_even("gy", (8, width))
        north.append(jnp.where(even, second_row[part, :], first_row[part, :]))
        south.append(jnp.where(even, first_row[part, :], second_row[part, :]))
    eta_ext = extended(eta_ref[...], sides.eta, north, south, 0)
    level_ext = extended(level, sides.depth, north, south, 4)
    level_out[...] = level_ext
    depth = level_ext / count
    east_weight = (surface_stiffness / spread) * jnp.minimum(depth, roll(depth, -1, 1))
    north_weight = (surface_stiffness / spread) * jnp.minimum(depth, roll(depth, -1, 0))

    west_weight, south_weight = roll(east_weight, 1, 1), roll(north_weight, 1, 0)

    def scaled(field):
        along_x = east_weight * (field - roll(field, -1, 1)) + west_weight * (field - roll(field, 1, 1))
        along_y = north_weight * (field - roll(field, -1, 0)) + south_weight * (field - roll(field, 1, 0))
        return along_x + along_y

    first = scaled(eta_ext)
    second = scaled(first) - first
    third = scaled(second)
    basis_out[0] = eta_ext
    basis_out[1] = first
    basis_out[2] = second
    vectors = [x[:height, :width] for x in (eta_ext, first, second, third)]
    pairs = ((0, 0), (0, 1), (0, 2), (1, 1), (1, 2), (2, 2), (2, 3))
    row = rows_of((8, width))
    table = jnp.zeros((8, width), F32)
    for index, (a, b) in enumerate(pairs):
        table = jnp.where(row == index, jnp.sum(vectors[a] * vectors[b], axis=0, keepdims=True), table)
    totals = jnp.sum(table, axis=1, keepdims=True)
    line = jnp.sum(jnp.where(lanes_of((8, width)) == row, totals, 0.0), axis=0, keepdims=True)
    sums_out[...] = jnp.broadcast_to(line, sums_out.shape)


def galerkin(sums):
    d00, d01, d02, d11, d12, d22, d2q = [sums[:, i : i + 1] for i in range(7)]
    k00 = d00 + spread * d01
    k01 = d01 + spread * d11
    k02 = d02 + spread * d12
    k11 = d11 + spread * (d11 + d12)
    k12 = d12 + spread * (d12 + d22)
    k22 = d22 + spread * d2q
    i00 = 1.0 / k00
    s11 = k11 - k01 * k01 * i00
    s12 = k12 - k01 * k02 * i00
    s22 = k22 - k02 * k02 * i00
    g1 = spread * (d01 * d01 - d00 * d11) * i00
    g2 = spread * (d02 * d01 - d00 * d12) * i00
    product = s11 * s22
    det = product - s12 * s12
    full = det > 4e-7 * product
    inverse = 1.0 / det
    y2 = jnp.where(full, (s11 * g2 - s12 * g1) * inverse, 0.0)
    y1 = jnp.where(full, (s22 * g1 - s12 * g2) * inverse, g1 / s11)
    y0 = (d00 - k01 * y1 - k02 * y2) * i00
    return y0, y1, y2


def column_kernel(
    tracer_ref, u_ref, v_ref, bar_ref,
    own_ref, first_ref, second_ref, c_rows, v_row, first_row, second_row, level_ref, basis_ref,
    base_out, share_out,
    side_ref, turn_ref, ratio_ref, slope_ref, value_ref, adjoint_ref,
):
    count, height, width = u_ref.shape
    level_ext = level_ref[...]
    level = level_ext[:height, :width]
    sides = Sides(first_ref, second_ref, level)
    lane, row = lanes_of((height, width)), rows_of((height, width))
    layer = layer_rows(count, width)
    last_row, last_lane = level_ext.shape[0] - 1, level_ext.shape[1] - 1
    plan = Message(count)

    def from_north(part):
        even = is_even("gy", (part.stop - part.start, width))
        return jnp.where(even, second_row[part, :], first_row[part, :])

    def from_south(part):
        even = is_even("gy", (part.stop - part.start, width))
        return jnp.where(even, first_row[part, :], second_row[part, :])


    inner = [sides.inner(f) for f in range(2)]
    u_inner, v_inner = sides.inner(U_TILE), sides.inner(V_TILE)
    edge_flow = sides.edge_flow(own_ref, u_inner)
    edge_flux = [0.5 * edge_flow * (own_ref[f] + inner[f]) for f in range(2)]
    depth_in = sides.columns(sides.depth, 0, width - 1)
    depth_out = sides.columns(sides.depth, 1, width - 2)
    far_flow = jnp.where(sides.eastern, u_inner, sides.outer(U_TILE))
    far_flow = jnp.where(sides.layer < jnp.minimum(depth_in, depth_out), far_flow, 0.0)
    corner_depth = [
        jnp.where(sides.eastern[:1], level_ext[r : r + 1, width : width + 1], level_ext[r : r + 1, last_lane:])
        for r in (height, last_row)
    ]
    corner_north, corner_south = from_north(plan.corner), from_south(plan.corner)
    depth_up = jnp.where(row == height - 1, corner_depth[0], roll(depth_in, -1, 0))
    up_flow = jnp.where(sides.layer < jnp.minimum(depth_in, depth_up), v_inner, 0.0)
    low_flow = jnp.where(
        sides.layer[:1] < jnp.minimum(depth_in[:1], corner_depth[1]), corner_south[2:3, :], 0.0
    )
    rate = jnp.where(sides.layer < depth_in, advect_rate, 0.0)
    outward = jnp.where(sides.eastern, 1.0, -1.0)
    beyond = []
    for f in range(2):
        c = inner[f]
        far_flux = 0.5 * far_flow * (c + sides.outer(f))
        c_up = jnp.where(row == height - 1, corner_north[f : f + 1, :], roll(c, -1, 0))
        flux_n = 0.5 * up_flow * (c + c_up)
        low_flux = 0.5 * low_flow * (corner_south[f : f + 1, :] + c[:1])
        flux_s = jnp.where(row == 0, low_flux, roll(flux_n, 1, 0))
        beyond.append(c - rate * (outward * (far_flux - edge_flux[f]) + (flux_n - flux_s)))
    beyond += sides.bars() + [depth_in]
    filler = jnp.zeros((width - height * len(beyond), width), F32)
    turned = jnp.transpose(jnp.concatenate(beyond + [filler], axis=0))

    south_flow = jnp.where(layer < level[:1, :], from_south(plan.v), 0.0)
    north_flow = jnp.where(layer < level_ext[height : height + 1, :width], v_row[...], 0.0)
    south_flux, north_flux = [], []
    side_ref[...] = jnp.zeros_like(side_ref)
    for f in range(2):
        part = plan.tracers[f]
        south_flux.append(0.5 * south_flow * (from_south(part) + c_rows[1, part, :]))
        north_flux.append(0.5 * north_flow * (c_rows[0, part, :] + from_north(part)))
        side_ref[f, pl.ds(4, count, stride=8), :] = from_south(plan.summed[f]) - advect_rate * south_flux[f]
        side_ref[f, pl.ds(5, count, stride=8), :] = from_north(plan.summed[f]) + advect_rate * north_flux[f]
        side_ref[2 + f, pl.ds(4, count, stride=8), :] = from_south(plan.bars[f])
        side_ref[2 + f, pl.ds(5, count, stride=8), :] = from_north(plan.bars[f])
    for f in range(4):
        turn_ref[f] = roll(turned, -height * f, 1)
        for m in (1, 2):
            side_ref[f, pl.ds(m, count, stride=8), :] = turn_ref[f, pl.ds(m, count, stride=4), :]
    row8 = rows_of((8, width))
    side_level = roll(turned[:8, :], -4 * height, 1)
    side_level = jnp.where((row8 == 1) | (row8 == 2), side_level, 0.0)
    side_level = jnp.where(row8 == 4, level_ext[last_row:, :width], side_level)
    side_level = jnp.where(row8 == 5, level_ext[height : height + 1, :width], side_level)
    level_all = jnp.concatenate([level, side_level], axis=0)

    east_depth = jnp.minimum(level_ext, roll(level_ext, -1, 1))[:height, :width]
    north_depth = jnp.minimum(level_ext, roll(level_ext, -1, 0))[:height, :width]

    def with_side(own, f, k):
        return jnp.concatenate([own, side_ref[f, 8 * k : 8 * k + 8, :]], axis=0)

    def advected(k):
        flow_e = jnp.where(east_depth > k, 0.5 * u_ref[k], 0.0)
        flow_n = jnp.where(north_depth > k, 0.5 * v_ref[k], 0.0)
        wet_rate = jnp.where(level > k, advect_rate, 0.0)
        result = []
        for f in range(2):
            c = tracer_ref[f, k]
            ends = roll(edge_flux[f], -(4 * k + 2), 1)
            flux_e = jnp.where(lane == width - 1, ends, flow_e * (c + roll(c, -1, 1)))
            flux_w = jnp.where(lane == 0, ends, roll(flux_e, 1, 1))
            flux_n = jnp.where(row == height - 1, north_flux[f][k : k + 1, :], flow_n * (c + roll(c, -1, 0)))
            flux_s = jnp.where(row == 0, south_flux[f][k : k + 1, :], roll(flux_n, 1, 0))
            result.append(with_side(c - wet_rate * ((flux_e - flux_w) + (flux_n - flux_s)), f, k))
        return result

    now = advected(0)
    kappa_up = ratio_up = values = None
    for k in range(count):
        diagonal = 1.0
        kappa = later = None
        if k < count - 1:
            later = advected(k + 1)
            step = (now[1] - now[0]) - (later[1] - later[0])
            gate = jax.nn.sigmoid(mix_slope * step)
            wet_below = level_all > k + 1
            kappa = jnp.where(wet_below, mix_floor + mix_boost * gate, 0.0)
            slope_ref[k] = jnp.where(wet_below, (mix_boost * mix_slope) * gate * (1.0 - gate), 0.0)
            diagonal = diagonal + mix_rate * kappa
        if k > 0:
            diagonal = diagonal + mix_rate * kappa_up * (1.0 - ratio_up)
        inverse = 1.0 / diagonal
        right = [now[0], now[1], with_side(bar_ref[0, k], 2, k), with_side(bar_ref[1, k], 3, k)]
        if k > 0:
            right = [cells + mix_rate * kappa_up * value for cells, value in zip(right, values)]
        values = [cells * inverse for cells in right]
        for f in range(4):
            value_ref[f, k] = values[f]
        if kappa is not None:
            ratio_up, kappa_up = mix_rate * kappa * inverse, kappa
            ratio_ref[k] = ratio_up
        now = later

    def emit(k, cells, change):
        for f, sign in ((0, -1.0), (1, 1.0)):
            full = cells[2 + f] + sign * change
            adjoint_ref[f, k] = full[:height, :]
            side_ref[f, 8 * k : 8 * k + 8, :] = full[height:, :]

    below = values
    pull_below = None
    for k in range(count - 2, -1, -1):
        here = [value_ref[f, k] + ratio_ref[k] * below[f] for f in range(4)]
        pull = (-mix_rate) * slope_ref[k] * (
            (here[2] - below[2]) * (here[0] - below[0]) + (here[3] - below[3]) * (here[1] - below[1])
        )
        emit(k + 1, below, -pull if pull_below is None else pull_below - pull)
        below, pull_below = here, pull
    emit(0, below, pull_below)

    for f in range(2):
        for m in (1, 2):
            turn_ref[f, pl.ds(m, count, stride=4), :] = side_ref[f, pl.ds(m, count, stride=8), :]
    wide = lanes_of((width, width)) < height
    back = jnp.transpose(jnp.where(wide, turn_ref[0], roll(turn_ref[1], height, 1)))
    ends_of = [back[f * height : (f + 1) * height, :] for f in range(2)]
    south_line = [side_ref[f, pl.ds(4, count, stride=8), :] for f in range(2)]
    north_line = [side_ref[f, pl.ds(5, count, stride=8), :] for f in range(2)]
    steps = []
    for b in range(3):
        field = basis_ref[b]
        east = (0.5 * advect_rate) * (field - roll(field, -1, 1))
        north = (0.5 * advect_rate) * (field - roll(field, -1, 0))
        around = (field, east, roll(east, 1, 1), north, roll(north, 1, 0))
        steps.append([cells[:height, :width] for cells in around])
    for k in range(count):
        flow_e = jnp.where(east_depth > k, u_ref[k], 0.0)
        flow_n = jnp.where(north_depth > k, v_ref[k], 0.0)
        ends_flow = roll(edge_flow, -(4 * k + 2), 1)
        low = south_flow[k : k + 1, :]
        flow_w = jnp.where(lane == 0, ends_flow, roll(flow_e, 1, 1))
        flow_s = jnp.where(row == 0, low, roll(flow_n, 1, 0))
        for b, (field, east, west, north, south) in enumerate(steps):
            part = (flow_e * east + flow_w * west) + (flow_n * north + flow_s * south)
            share_out[b, k] = jnp.where(level > k, field, 0.0) - part
        for f in range(2):
            y = adjoint_ref[f, k]
            ends = roll(ends_of[f], -(4 * k + 2), 1)
            y_east = jnp.where(lane == width - 1, ends, roll(y, -1, 1))
            y_north = jnp.where(row == height - 1, north_line[f][k : k + 1, :], roll(y, -1, 0))
            part_e = flow_e * (y - y_east)
            part_n = flow_n * (y - y_north)
            part_w = jnp.where(lane == 0, ends_flow * (ends - y), roll(part_e, 1, 1))
            part_s = jnp.where(row == 0, low * (south_line[f][k : k + 1, :] - y), roll(part_n, 1, 0))
            base_out[f, k] = y - (0.5 * advect_rate) * ((part_e + part_w) + (part_n + part_s))


def final_kernel(sums_ref, basis_ref, base_ref, share_ref, tracer_hbm, eta_hbm, tracer_out, eta_out, sems):
    _, count, height, width = base_ref.shape
    y0, y1, y2 = galerkin(jnp.sum(sums_ref[...], axis=0, keepdims=True))

    def combined(fields):
        return y0 * fields[0] + (y1 * fields[1] + y2 * fields[2])

    eta_out[...] = combined([basis_ref[b, :height, :width] for b in range(3)])
    copies = [pltpu.make_async_copy(eta_out, eta_hbm, sems.at[0])]
    copies[0].start()
    for k in range(count):
        share = combined([share_ref[b, k] for b in range(3)])
        for f in range(2):
            tracer_out[f, k] = base_ref[f, k] + sterics[f] * share
        if (k + 1) % chunk == 0 or k == count - 1:
            levels = pl.ds(k - k % chunk, k % chunk + 1)
            at = len(copies)
            copies.append(pltpu.make_async_copy(tracer_out.at[:, levels], tracer_hbm.at[:, levels], sems.at[at]))
            copies[-1].start()
    for copy in copies:
        copy.wait()


def call(kernel, outs, name, specs=None, scratch=(), cost=None, out_spec=VMEM):
    def run(*operands):
        return pl.pallas_call(
            kernel,
            out_shape=[jax.ShapeDtypeStruct(shape, F32) for shape in outs],
            in_specs=specs or [VMEM] * len(operands),
            out_specs=[out_spec] * len(outs),
            scratch_shapes=list(scratch),
            cost_estimate=cost,
            compiler_params=pltpu.CompilerParams(vmem_limit_bytes=vmem_grant),
            name=name,
        )(*operands)

    return run


def swap(cells, axis, first, wrap):
    count = lax.axis_size(axis)
    pairs = []
    for i in range(first, count, 2):
        if i + 1 < count or wrap:
            j = (i + 1) % count
            pairs += [(i, j), (j, i)]
    return lax.ppermute(cells, axis, pairs)


def per_device(tracers, uvel, vvel, sea_mask, levels, tracer_bar, eta_bar):
    _, count, height, width = tracers.shape
    devices = lax.axis_size("gx") * lax.axis_size("gy")
    tile = (height, width)
    rows = (2, 2 * count, width)
    field = (count,) + tile
    inputs = (sea_mask, levels, eta_bar, tracers, uvel, vvel, tracer_bar)
    own, level, eta, tracers, uvel, vvel, tracer_bar = call(
        pack_columns,
        [(LAST_TILE + 1,) + tile, tile, tile, (2,) + field, field, field, (2,) + field],
        "pack_columns",
        [HBM] * 7,
        [pltpu.VMEM(tile, jnp.int32), pltpu.VMEM(tile, jnp.int32), pltpu.SemaphoreType.DMA((7,))],
    )(*(pltpu.with_memory_space_constraint(x, pltpu.HBM) for x in inputs))
    first, second = swap(own, "gx", 0, True), swap(own, "gx", 1, True)
    c_rows, n_rows, u_rows, b_rows, v_row = call(
        pack_rows, [rows, rows, (2, count, width), rows, (count, width)], "pack_rows"
    )(level, tracers, uvel, vvel, tracer_bar)
    plan = Message(count)
    message = (plan.rows, width)
    first_msg, second_msg = call(join_rows, [message, message], "join_rows")(
        level, eta, own, first, second, c_rows, n_rows, u_rows, b_rows, v_row
    )
    first_row, second_row = swap(first_msg, "gy", 1, False), swap(second_msg, "gy", 0, False)
    ext = (height + 8, 2 * width)

    def surface(*refs):
        surface_kernel(*refs, count=count)

    basis, level_ext, sums = call(surface, [(3,) + ext, ext, (devices, width)], "surface")(
        level, eta, first, second, first_row, second_row
    )
    all_sums = lax.all_to_all(sums.reshape(devices, 1, width), ("gx", "gy"), 0, 0).reshape(devices, width)
    taller = (count, height + 8, width)
    base, shares = call(
        column_kernel,
        [(2,) + field, (3,) + field],
        "columns",
        None,
        [
            pltpu.VMEM((4, 8 * count, width), F32),
            pltpu.VMEM((4, width, width), F32),
            pltpu.VMEM(taller, F32),
            pltpu.VMEM(taller, F32),
            pltpu.VMEM((4,) + taller, F32),
            pltpu.VMEM((2,) + field, F32),
        ],
        pl.CostEstimate(flops=400 * count * height * width, transcendentals=count * height * width, bytes_accessed=1 << 22),
    )(tracers, uvel, vvel, tracer_bar, own, first, second, c_rows, v_row, first_row, second_row, level_ext, basis)
    pieces = (count + chunk - 1) // chunk
    tracer_adj, eta_adj = call(
        final_kernel,
        [(2,) + field, tile],
        "finish",
        None,
        [pltpu.VMEM((2,) + field, F32), pltpu.VMEM(tile, F32), pltpu.SemaphoreType.DMA((pieces + 1,))],
        out_spec=HBM,
    )(all_sums, basis, base, shares)
    return (tracer_adj, eta_adj)


def solution(mesh):
    return jax.shard_map(
        per_device,
        mesh=mesh,
        in_specs=(
            P(None, None, "gy", "gx"),
            P(None, "gy", "gx"),
            P(None, "gy", "gx"),
            P("gy", "gx"),
            P("gy", "gx"),
            P(None, None, "gy", "gx"),
            P("gy", "gx"),
        ),
        out_specs=(P(None, None, "gy", "gx"), P("gy", "gx")),
        check_vma=False,
    )
```

```python
import jax
import jax.numpy as jnp
from jax import lax
from jax.experimental import pallas as pl
from jax.experimental.pallas import tpu as pltpu
from jax.sharding import PartitionSpec as P

advect_rate = 0.25
mix_floor = 0.2
mix_boost = 2.0
mix_slope = 2.0
mix_rate = 1.0
surface_stiffness = 2.0
thermal_steric = 0.5
haline_steric = 0.5
sterics = (thermal_steric, -haline_steric)
spread = 4.0 * surface_stiffness
F32 = jnp.float32
VMEM = pl.BlockSpec(memory_space=pltpu.VMEM)
HBM = pl.BlockSpec(memory_space=pltpu.HBM)
vmem_grant = 8 << 20
chunk = 6
U_TILE, V_TILE, LAST_TILE = 2, 3, 4
surface_turn = 18


def lanes_of(shape):
    return lax.broadcasted_iota(jnp.int32, shape, 1)


def rows_of(shape):
    return lax.broadcasted_iota(jnp.int32, shape, 0)


def roll(cells, shift, axis):
    size = cells.shape[axis]
    shift = shift % size
    return cells if shift == 0 else pltpu.roll(cells, shift, axis)


def layer_rows(count, width):
    return rows_of((count, width)).astype(F32)


def pack_columns(
    mask_in, levels_in, eta_in, tracer_in, u_in, v_in, bar_in,
    out_ref, level_ref, eta_ref, tracer_ref, u_ref, v_ref, bar_ref,
    mask_ref, levels_ref, sems,
):
    pairs = (
        (tracer_in, tracer_ref), (u_in, u_ref), (v_in, v_ref), (bar_in, bar_ref),
        (mask_in, mask_ref), (levels_in, levels_ref), (eta_in, eta_ref),
    )
    copies = [pltpu.make_async_copy(source, target, sems.at[i]) for i, (source, target) in enumerate(pairs)]
    for copy in copies:
        copy.start()
    count, height, width = u_ref.shape
    lane = lanes_of((height, width))
    group = lane // 4
    middle = jnp.where((lane % 4 == 1) | (lane % 4 == 2), group, -1)
    beside = jnp.where((lane + 1) % 4 < 2, (lane + 1) // 4 - 1, -1)

    def gathered(field, place, turn, tile):
        for k in range(count):
            tile = jnp.where(place == k, roll(field[k], 4 * k + turn, 1), tile)
        return tile

    empty = jnp.zeros((height, width), F32)
    copies[0].wait()
    for f in range(2):
        out_ref[f] = gathered(tracer_ref.at[f], group, 2, empty)
    copies[1].wait()
    out_ref[U_TILE] = gathered(u_ref, group, 2, empty)
    copies[2].wait()
    v_tile = gathered(v_ref, middle, 2, empty)
    copies[3].wait()
    out_ref[V_TILE] = gathered(bar_ref.at[0], beside, 4, v_tile)
    last = gathered(bar_ref.at[1], middle, 2, empty)
    for copy in copies[4:]:
        copy.wait()
    level = (mask_ref[...] * levels_ref[...]).astype(F32)
    level_ref[...] = level
    depth = jnp.where(lane < width // 2, roll(level, 3, 1), roll(level, -3, 1))
    surface = roll(jnp.where((lane < 3) | (lane >= width - 3), eta_ref[...], depth), -surface_turn, 1)
    start = width - 6 - surface_turn
    out_ref[LAST_TILE] = jnp.where((lane >= start) & (lane < start + 12), surface, last)


class Sides:
    def __init__(self, first_ref, second_ref, level):
        self.refs = (first_ref, second_ref)
        self.level = level
        self.shape = level.shape
        lane = lanes_of(self.shape)
        self.lane = lane
        self.layer = (lane // 4).astype(F32)
        self.eastern = lane % 4 == 1
        east, west = (roll(tile, surface_turn, 1) for tile in self.pick(LAST_TILE))
        half = lane < self.shape[1] // 2
        self.eta = jnp.where(half, east, west)
        self.depth = jnp.where(half, roll(self.eta, -3, 1), roll(self.eta, 3, 1))

    def pick(self, tile):
        first, second = (ref[tile] for ref in self.refs)
        even = is_even("gx", self.shape)
        return jnp.where(even, first, second), jnp.where(even, second, first)

    def inner(self, tile):
        east, west = self.pick(tile)
        return jnp.where(self.eastern, roll(east, -1, 1), roll(west, 1, 1))

    def bars(self):
        east, west = self.pick(V_TILE)
        return [jnp.where(self.eastern, roll(east, -3, 1), roll(west, -1, 1)), self.inner(LAST_TILE)]

    def outer(self, tile):
        east, west = self.pick(tile)
        return jnp.where(self.eastern, roll(east, -2, 1), roll(west, 2, 1))

    def columns(self, cells, east, west):
        return jnp.where(self.eastern, cells[:, east : east + 1], cells[:, west : west + 1])

    def edge_flow(self, own_ref, u_inner):
        width = self.shape[1]
        own_depth = self.columns(self.level, width - 1, 0)
        beyond = self.columns(self.depth, 0, width - 1)
        flow = jnp.where(self.eastern, own_ref[U_TILE], u_inner)
        return jnp.where(self.layer < jnp.minimum(own_depth, beyond), flow, 0.0)


def pack_rows(level_ref, tracer_ref, u_ref, v_ref, bar_ref, c_out, n_out, u_out, b_out, v_out):
    count, height, width = u_ref.shape
    level = level_ref[...]
    layer = layer_rows(count, width)
    for side, (row, inside, face) in enumerate(((height - 1, height - 2, height - 2), (0, 1, 0))):
        depth = jnp.minimum(level[row : row + 1, :], level[inside : inside + 1, :])
        flow = jnp.where(layer < depth, 0.5 * v_ref[:, face, :], 0.0)
        u_out[side] = u_ref[:, row, :]
        for f in range(2):
            part = slice(f * count, (f + 1) * count)
            c = tracer_ref[f, :, row, :]
            c_out[side, part, :] = c
            n_out[side, part, :] = flow * (c + tracer_ref[f, :, inside, :])
            b_out[side, part, :] = bar_ref[f, :, row, :]
    v_out[...] = jnp.where(layer < level[height - 1 :, :], v_ref[:, height - 1, :], 0.0)


class Message:
    def __init__(self, count):
        self.tracers = [slice(f * count, (f + 1) * count) for f in range(2)]
        self.summed = [slice(f * count, (f + 1) * count) for f in range(2, 4)]
        self.bars = [slice(f * count, (f + 1) * count) for f in range(4, 6)]
        self.v = slice(6 * count, 7 * count)
        self.surface = [slice(7 * count + 8 * i, 7 * count + 8 * i + 8) for i in range(2)]
        self.corner = slice(7 * count + 16, 7 * count + 24)
        self.rows = 7 * count + 24


def is_even(axis, shape):
    return jnp.full(shape, lax.rem(lax.axis_index(axis), 2), jnp.int32) == 0


def join_rows(
    level_ref, eta_ref, own_ref, first_ref, second_ref, c_ref, n_ref, u_ref, b_ref, v_ref,
    first_out, second_out,
):
    count, width = v_ref.shape
    level = level_ref[...]
    height = level.shape[0]
    plan = Message(count)
    sides = Sides(first_ref, second_ref, level)
    inner = [sides.inner(f) for f in range(2)]
    v_inner = sides.inner(V_TILE)
    flow = 0.5 * sides.edge_flow(own_ref, sides.inner(U_TILE))
    flux = [flow * (own_ref[f] + inner[f]) for f in range(2)]
    layer = layer_rows(count, width)
    lane = lanes_of((count, width))
    level_row = rows_of((count, width))
    row8 = rows_of((8, width))
    no_flow, pad = jnp.zeros((count, width), F32), jnp.zeros((8, width), F32)

    def put(part, north, south):
        even = is_even("gy", north.shape)
        first_out[part, :] = jnp.where(even, south, north)
        second_out[part, :] = jnp.where(even, north, south)

    def summed(side, f, row, sign):
        depth = level[row : row + 1, :]
        east_flow = jnp.where(layer < jnp.minimum(depth, roll(depth, -1, 1)), 0.5 * u_ref[side], 0.0)
        rate = jnp.where(layer < depth, advect_rate, 0.0)
        c = c_ref[side, plan.tracers[f], :]
        line = flux[f][row : row + 1, :]
        east_end, west_end = (
            jnp.sum(jnp.where(lane == 4 * level_row + m, line, 0.0), axis=1, keepdims=True) for m in (1, 2)
        )
        flux_e = jnp.where(lane == width - 1, east_end, east_flow * (c + roll(c, -1, 1)))
        flux_w = jnp.where(lane == 0, west_end, roll(flux_e, 1, 1))
        return c - rate * ((flux_e - flux_w) + sign * n_ref[side, plan.tracers[f], :])

    for f in range(2):
        part = plan.tracers[f]
        put(part, c_ref[0, part, :], c_ref[1, part, :])
        put(plan.summed[f], summed(0, f, height - 1, -1.0), summed(1, f, 0, 1.0))
        put(plan.bars[f], b_ref[0, part, :], b_ref[1, part, :])
    put(plan.v, v_ref[...], no_flow)
    for part, eta, depth in zip(plan.surface, (eta_ref[...], sides.eta), (level, sides.depth)):
        north = jnp.where(row8 < 4, roll(depth[height - 8 :, :], 4, 0), eta[height - 8 :, :])
        put(part, north, jnp.where(row8 < 4, eta[:8, :], roll(depth[:8, :], 4, 0)))
    lines = [inner[0], inner[1], v_inner]
    north = south = pad
    for index, cells in enumerate(lines):
        north = jnp.where(row8 == index, cells[height - 1 :, :], north)
        south = jnp.where(row8 == index, cells[:1, :], south)
    put(plan.corner, north, south)


def extended(own, side, north, south, turn):
    row8 = rows_of((8, own.shape[1]))
    parts = []
    for index, tile in enumerate((own, side)):
        up, down = (roll(msg[index], turn, 0) for msg in (north, south))
        parts.append(jnp.concatenate([tile, jnp.where(row8 < 4, up, down)], axis=0))
    return jnp.concatenate(parts, axis=1)


pairs = ((0, 0), (0, 1), (0, 2), (1, 1), (1, 2), (2, 2), (2, 3))
centers = ((0.0, 0.25), (1.0, 0.25), (2.0, -0.25))


def surface_kernel(
    level_ref, eta_ref, first_ref, second_ref, first_row, second_row,
    basis_out, level_out, sums_out, *, count,
):
    level = level_ref[...]
    height, width = level.shape
    sides = Sides(first_ref, second_ref, level)
    north, south = [], []
    for part in Message(count).surface:
        even = is_even("gy", (8, width))
        north.append(jnp.where(even, second_row[part, :], first_row[part, :]))
        south.append(jnp.where(even, first_row[part, :], second_row[part, :]))
    eta_ext = extended(eta_ref[...], sides.eta, north, south, 0)
    level_ext = extended(level, sides.depth, north, south, 4)
    level_out[...] = level_ext
    depth = level_ext / count
    east_weight = (surface_stiffness / spread) * jnp.minimum(depth, roll(depth, -1, 1))
    north_weight = (surface_stiffness / spread) * jnp.minimum(depth, roll(depth, -1, 0))

    west_weight, south_weight = roll(east_weight, 1, 1), roll(north_weight, 1, 0)

    def scaled(field):
        along_x = east_weight * (field - roll(field, -1, 1)) + west_weight * (field - roll(field, 1, 1))
        along_y = north_weight * (field - roll(field, -1, 0)) + south_weight * (field - roll(field, 1, 0))
        return along_x + along_y

    powers = [eta_ext]
    for _ in range(3):
        powers.append(scaled(powers[-1]))
    for index in range(3):
        basis_out[index] = powers[index]
    powers = [x[:height, :width] for x in powers]
    table = []
    row = rows_of((8, width))
    for center, tilt in centers:
        one, two, three = powers[1:]
        if center:
            moved = [x - center * y for x, y in zip(powers[1:], powers)]
            twice = [x - center * y for x, y in zip(moved[1:], moved)]
            one, two, three = moved[0], twice[0], twice[1] - center * twice[0]
        vectors = (powers[0], one, two - tilt * one, three - tilt * two)
        part = jnp.zeros((8, width), F32)
        for index, (i, j) in enumerate(pairs):
            part = jnp.where(row == index, jnp.sum(vectors[i] * vectors[j], axis=0, keepdims=True), part)
        table.append(part)
    table = jnp.concatenate(table, axis=0)
    totals = jnp.sum(table, axis=1, keepdims=True)
    place = lanes_of(table.shape) == rows_of(table.shape)
    line = jnp.sum(jnp.where(place, totals, 0.0), axis=0, keepdims=True)
    sums_out[...] = jnp.broadcast_to(line, sums_out.shape)


def galerkin(sums):
    mean, square = sums[:, 1:2], sums[:, 0:1]
    center = jnp.zeros_like(mean)
    tilt = jnp.full_like(mean, centers[0][1])
    chosen = sums
    for index in range(1, len(centers)):
        here = mean > 0.5 * (centers[index - 1][0] + centers[index][0]) * square
        center = jnp.where(here, centers[index][0], center)
        tilt = jnp.where(here, centers[index][1], tilt)
        chosen = jnp.where(here, roll(sums, -8 * index, 1), chosen)
    d00, d01, d02, d11, d12, d22, d2q = [chosen[:, i : i + 1] for i in range(7)]
    base = 1.0 + spread * center
    k00 = base * d00 + spread * d01
    k01 = base * d01 + spread * d11
    k02 = base * d02 + spread * d12
    k11 = base * d11 + spread * (tilt * d11 + d12)
    k12 = base * d12 + spread * (tilt * d12 + d22)
    k22 = base * d22 + spread * d2q
    i00 = 1.0 / k00
    s11 = k11 - k01 * k01 * i00
    s12 = k12 - k01 * k02 * i00
    s22 = k22 - k02 * k02 * i00
    g1 = spread * (d01 * d01 - d00 * d11) * i00
    g2 = spread * (d02 * d01 - d00 * d12) * i00
    second = s11 > 1e-7 * k11
    i11 = jnp.where(second, 1.0 / s11, 0.0)
    c12 = s12 * i11
    last = s22 - s12 * c12
    third = second & (last > 4e-7 * s22)
    y2 = jnp.where(third, (g2 - g1 * c12) / last, 0.0)
    y1 = (g1 - s12 * y2) * i11
    y0 = (d00 - k01 * y1 - k02 * y2) * i00
    inner = center + tilt
    return y0 - center * y1 + center * inner * y2, y1 - (center + inner) * y2, y2


def column_kernel(
    tracer_ref, u_ref, v_ref, bar_ref,
    own_ref, first_ref, second_ref, c_rows, v_row, first_row, second_row, level_ref, basis_ref,
    base_out, share_out,
    side_ref, turn_ref, ratio_ref, slope_ref, value_ref, adjoint_ref,
):
    count, height, width = u_ref.shape
    level_ext = level_ref[...]
    level = level_ext[:height, :width]
    sides = Sides(first_ref, second_ref, level)
    lane, row = lanes_of((height, width)), rows_of((height, width))
    layer = layer_rows(count, width)
    last_row, last_lane = level_ext.shape[0] - 1, level_ext.shape[1] - 1
    plan = Message(count)

    def from_north(part):
        even = is_even("gy", (part.stop - part.start, width))
        return jnp.where(even, second_row[part, :], first_row[part, :])

    def from_south(part):
        even = is_even("gy", (part.stop - part.start, width))
        return jnp.where(even, first_row[part, :], second_row[part, :])


    inner = [sides.inner(f) for f in range(2)]
    u_inner, v_inner = sides.inner(U_TILE), sides.inner(V_TILE)
    edge_flow = sides.edge_flow(own_ref, u_inner)
    edge_flux = [0.5 * edge_flow * (own_ref[f] + inner[f]) for f in range(2)]
    depth_in = sides.columns(sides.depth, 0, width - 1)
    depth_out = sides.columns(sides.depth, 1, width - 2)
    far_flow = jnp.where(sides.eastern, u_inner, sides.outer(U_TILE))
    far_flow = jnp.where(sides.layer < jnp.minimum(depth_in, depth_out), far_flow, 0.0)
    corner_depth = [
        jnp.where(sides.eastern[:1], level_ext[r : r + 1, width : width + 1], level_ext[r : r + 1, last_lane:])
        for r in (height, last_row)
    ]
    corner_north, corner_south = from_north(plan.corner), from_south(plan.corner)
    depth_up = jnp.where(row == height - 1, corner_depth[0], roll(depth_in, -1, 0))
    up_flow = jnp.where(sides.layer < jnp.minimum(depth_in, depth_up), v_inner, 0.0)
    low_flow = jnp.where(
        sides.layer[:1] < jnp.minimum(depth_in[:1], corner_depth[1]), corner_south[2:3, :], 0.0
    )
    rate = jnp.where(sides.layer < depth_in, advect_rate, 0.0)
    outward = jnp.where(sides.eastern, 1.0, -1.0)
    beyond = []
    for f in range(2):
        c = inner[f]
        far_flux = 0.5 * far_flow * (c + sides.outer(f))
        c_up = jnp.where(row == height - 1, corner_north[f : f + 1, :], roll(c, -1, 0))
        flux_n = 0.5 * up_flow * (c + c_up)
        low_flux = 0.5 * low_flow * (corner_south[f : f + 1, :] + c[:1])
        flux_s = jnp.where(row == 0, low_flux, roll(flux_n, 1, 0))
        beyond.append(c - rate * (outward * (far_flux - edge_flux[f]) + (flux_n - flux_s)))
    beyond += sides.bars() + [depth_in]
    filler = jnp.zeros((width - height * len(beyond), width), F32)
    turned = jnp.transpose(jnp.concatenate(beyond + [filler], axis=0))

    south_flow = jnp.where(layer < level[:1, :], from_south(plan.v), 0.0)
    north_flow = jnp.where(layer < level_ext[height : height + 1, :width], v_row[...], 0.0)
    south_flux, north_flux = [], []
    side_ref[...] = jnp.zeros_like(side_ref)
    for f in range(2):
        part = plan.tracers[f]
        south_flux.append(0.5 * south_flow * (from_south(part) + c_rows[1, part, :]))
        north_flux.append(0.5 * north_flow * (c_rows[0, part, :] + from_north(part)))
        side_ref[f, pl.ds(4, count, stride=8), :] = from_south(plan.summed[f]) - advect_rate * south_flux[f]
        side_ref[f, pl.ds(5, count, stride=8), :] = from_north(plan.summed[f]) + advect_rate * north_flux[f]
        side_ref[2 + f, pl.ds(4, count, stride=8), :] = from_south(plan.bars[f])
        side_ref[2 + f, pl.ds(5, count, stride=8), :] = from_north(plan.bars[f])
    for f in range(4):
        turn_ref[f] = roll(turned, -height * f, 1)
        for m in (1, 2):
            side_ref[f, pl.ds(m, count, stride=8), :] = turn_ref[f, pl.ds(m, count, stride=4), :]
    row8 = rows_of((8, width))
    side_level = roll(turned[:8, :], -4 * height, 1)
    side_level = jnp.where((row8 == 1) | (row8 == 2), side_level, 0.0)
    side_level = jnp.where(row8 == 4, level_ext[last_row:, :width], side_level)
    side_level = jnp.where(row8 == 5, level_ext[height : height + 1, :width], side_level)
    level_all = jnp.concatenate([level, side_level], axis=0)

    east_depth = jnp.minimum(level_ext, roll(level_ext, -1, 1))[:height, :width]
    north_depth = jnp.minimum(level_ext, roll(level_ext, -1, 0))[:height, :width]

    def with_side(own, f, k):
        return jnp.concatenate([own, side_ref[f, 8 * k : 8 * k + 8, :]], axis=0)

    def advected(k):
        flow_e = jnp.where(east_depth > k, 0.5 * u_ref[k], 0.0)
        flow_n = jnp.where(north_depth > k, 0.5 * v_ref[k], 0.0)
        wet_rate = jnp.where(level > k, advect_rate, 0.0)
        result = []
        for f in range(2):
            c = tracer_ref[f, k]
            ends = roll(edge_flux[f], -(4 * k + 2), 1)
            flux_e = jnp.where(lane == width - 1, ends, flow_e * (c + roll(c, -1, 1)))
            flux_w = jnp.where(lane == 0, ends, roll(flux_e, 1, 1))
            flux_n = jnp.where(row == height - 1, north_flux[f][k : k + 1, :], flow_n * (c + roll(c, -1, 0)))
            flux_s = jnp.where(row == 0, south_flux[f][k : k + 1, :], roll(flux_n, 1, 0))
            result.append(with_side(c - wet_rate * ((flux_e - flux_w) + (flux_n - flux_s)), f, k))
        return result

    now = advected(0)
    kappa_up = ratio_up = values = None
    for k in range(count):
        diagonal = 1.0
        kappa = later = None
        if k < count - 1:
            later = advected(k + 1)
            step = (now[1] - now[0]) - (later[1] - later[0])
            gate = jax.nn.sigmoid(mix_slope * step)
            wet_below = level_all > k + 1
            kappa = jnp.where(wet_below, mix_floor + mix_boost * gate, 0.0)
            slope_ref[k] = jnp.where(wet_below, (mix_boost * mix_slope) * gate * (1.0 - gate), 0.0)
            diagonal = diagonal + mix_rate * kappa
        if k > 0:
            diagonal = diagonal + mix_rate * kappa_up * (1.0 - ratio_up)
        inverse = 1.0 / diagonal
        right = [now[0], now[1], with_side(bar_ref[0, k], 2, k), with_side(bar_ref[1, k], 3, k)]
        if k > 0:
            right = [cells + mix_rate * kappa_up * value for cells, value in zip(right, values)]
        values = [cells * inverse for cells in right]
        for f in range(4):
            value_ref[f, k] = values[f]
        if kappa is not None:
            ratio_up, kappa_up = mix_rate * kappa * inverse, kappa
            ratio_ref[k] = ratio_up
        now = later

    def emit(k, cells, change):
        for f, sign in ((0, -1.0), (1, 1.0)):
            full = cells[2 + f] + sign * change
            adjoint_ref[f, k] = full[:height, :]
            side_ref[f, 8 * k : 8 * k + 8, :] = full[height:, :]

    below = values
    pull_below = None
    for k in range(count - 2, -1, -1):
        here = [value_ref[f, k] + ratio_ref[k] * below[f] for f in range(4)]
        pull = (-mix_rate) * slope_ref[k] * (
            (here[2] - below[2]) * (here[0] - below[0]) + (here[3] - below[3]) * (here[1] - below[1])
        )
        emit(k + 1, below, -pull if pull_below is None else pull_below - pull)
        below, pull_below = here, pull
    emit(0, below, pull_below)

    for f in range(2):
        for m in (1, 2):
            turn_ref[f, pl.ds(m, count, stride=4), :] = side_ref[f, pl.ds(m, count, stride=8), :]
    wide = lanes_of((width, width)) < height
    back = jnp.transpose(jnp.where(wide, turn_ref[0], roll(turn_ref[1], height, 1)))
    ends_of = [back[f * height : (f + 1) * height, :] for f in range(2)]
    south_line = [side_ref[f, pl.ds(4, count, stride=8), :] for f in range(2)]
    north_line = [side_ref[f, pl.ds(5, count, stride=8), :] for f in range(2)]
    steps = []
    for b in range(3):
        field = basis_ref[b]
        east = (0.5 * advect_rate) * (field - roll(field, -1, 1))
        north = (0.5 * advect_rate) * (field - roll(field, -1, 0))
        around = (field, east, roll(east, 1, 1), north, roll(north, 1, 0))
        steps.append([cells[:height, :width] for cells in around])
    for k in range(count):
        flow_e = jnp.where(east_depth > k, u_ref[k], 0.0)
        flow_n = jnp.where(north_depth > k, v_ref[k], 0.0)
        ends_flow = roll(edge_flow, -(4 * k + 2), 1)
        low = south_flow[k : k + 1, :]
        flow_w = jnp.where(lane == 0, ends_flow, roll(flow_e, 1, 1))
        flow_s = jnp.where(row == 0, low, roll(flow_n, 1, 0))
        for b, (field, east, west, north, south) in enumerate(steps):
            part = (flow_e * east + flow_w * west) + (flow_n * north + flow_s * south)
            share_out[b, k] = jnp.where(level > k, field, 0.0) - part
        for f in range(2):
            y = adjoint_ref[f, k]
            ends = roll(ends_of[f], -(4 * k + 2), 1)
            y_east = jnp.where(lane == width - 1, ends, roll(y, -1, 1))
            y_north = jnp.where(row == height - 1, north_line[f][k : k + 1, :], roll(y, -1, 0))
            part_e = flow_e * (y - y_east)
            part_n = flow_n * (y - y_north)
            part_w = jnp.where(lane == 0, ends_flow * (ends - y), roll(part_e, 1, 1))
            part_s = jnp.where(row == 0, low * (south_line[f][k : k + 1, :] - y), roll(part_n, 1, 0))
            base_out[f, k] = y - (0.5 * advect_rate) * ((part_e + part_w) + (part_n + part_s))


def final_kernel(sums_ref, basis_ref, base_ref, share_ref, tracer_hbm, eta_hbm, tracer_out, eta_out, sems):
    _, count, height, width = base_ref.shape
    y0, y1, y2 = galerkin(jnp.sum(sums_ref[...], axis=0, keepdims=True))

    def combined(fields):
        return y0 * fields[0] + (y1 * fields[1] + y2 * fields[2])

    eta_out[...] = combined([basis_ref[b, :height, :width] for b in range(3)])
    copies = [pltpu.make_async_copy(eta_out, eta_hbm, sems.at[0])]
    copies[0].start()
    for k in range(count):
        share = combined([share_ref[b, k] for b in range(3)])
        for f in range(2):
            tracer_out[f, k] = base_ref[f, k] + sterics[f] * share
        if (k + 1) % chunk == 0 or k == count - 1:
            levels = pl.ds(k - k % chunk, k % chunk + 1)
            at = len(copies)
            copies.append(pltpu.make_async_copy(tracer_out.at[:, levels], tracer_hbm.at[:, levels], sems.at[at]))
            copies[-1].start()
    for copy in copies:
        copy.wait()


def call(kernel, outs, name, specs=None, scratch=(), cost=None, out_spec=VMEM):
    def run(*operands):
        return pl.pallas_call(
            kernel,
            out_shape=[jax.ShapeDtypeStruct(shape, F32) for shape in outs],
            in_specs=specs or [VMEM] * len(operands),
            out_specs=[out_spec] * len(outs),
            scratch_shapes=list(scratch),
            cost_estimate=cost,
            compiler_params=pltpu.CompilerParams(vmem_limit_bytes=vmem_grant),
            name=name,
        )(*operands)

    return run


def swap(cells, axis, first, wrap):
    count = lax.axis_size(axis)
    pairs = []
    for i in range(first, count, 2):
        if i + 1 < count or wrap:
            j = (i + 1) % count
            pairs += [(i, j), (j, i)]
    return lax.ppermute(cells, axis, pairs)


def per_device(tracers, uvel, vvel, sea_mask, levels, tracer_bar, eta_bar):
    _, count, height, width = tracers.shape
    devices = lax.axis_size("gx") * lax.axis_size("gy")
    tile = (height, width)
    rows = (2, 2 * count, width)
    field = (count,) + tile
    inputs = (sea_mask, levels, eta_bar, tracers, uvel, vvel, tracer_bar)
    own, level, eta, tracers, uvel, vvel, tracer_bar = call(
        pack_columns,
        [(LAST_TILE + 1,) + tile, tile, tile, (2,) + field, field, field, (2,) + field],
        "pack_columns",
        [HBM] * 7,
        [pltpu.VMEM(tile, jnp.int32), pltpu.VMEM(tile, jnp.int32), pltpu.SemaphoreType.DMA((7,))],
    )(*(pltpu.with_memory_space_constraint(x, pltpu.HBM) for x in inputs))
    first, second = swap(own, "gx", 0, True), swap(own, "gx", 1, True)
    c_rows, n_rows, u_rows, b_rows, v_row = call(
        pack_rows, [rows, rows, (2, count, width), rows, (count, width)], "pack_rows"
    )(level, tracers, uvel, vvel, tracer_bar)
    plan = Message(count)
    message = (plan.rows, width)
    first_msg, second_msg = call(join_rows, [message, message], "join_rows")(
        level, eta, own, first, second, c_rows, n_rows, u_rows, b_rows, v_row
    )
    first_row, second_row = swap(first_msg, "gy", 1, False), swap(second_msg, "gy", 0, False)
    ext = (height + 8, 2 * width)

    def surface(*refs):
        surface_kernel(*refs, count=count)

    basis, level_ext, sums = call(surface, [(3,) + ext, ext, (devices, width)], "surface")(
        level, eta, first, second, first_row, second_row
    )
    all_sums = lax.all_to_all(sums.reshape(devices, 1, width), ("gx", "gy"), 0, 0).reshape(devices, width)
    taller = (count, height + 8, width)
    base, shares = call(
        column_kernel,
        [(2,) + field, (3,) + field],
        "columns",
        None,
        [
            pltpu.VMEM((4, 8 * count, width), F32),
            pltpu.VMEM((4, width, width), F32),
            pltpu.VMEM(taller, F32),
            pltpu.VMEM(taller, F32),
            pltpu.VMEM((4,) + taller, F32),
            pltpu.VMEM((2,) + field, F32),
        ],
        pl.CostEstimate(flops=400 * count * height * width, transcendentals=count * height * width, bytes_accessed=1 << 22),
    )(tracers, uvel, vvel, tracer_bar, own, first, second, c_rows, v_row, first_row, second_row, level_ext, basis)
    pieces = (count + chunk - 1) // chunk
    tracer_adj, eta_adj = call(
        final_kernel,
        [(2,) + field, tile],
        "finish",
        None,
        [pltpu.VMEM((2,) + field, F32), pltpu.VMEM(tile, F32), pltpu.SemaphoreType.DMA((pieces + 1,))],
        out_spec=HBM,
    )(all_sums, basis, base, shares)
    return (tracer_adj, eta_adj)


def solution(mesh):
    return jax.shard_map(
        per_device,
        mesh=mesh,
        in_specs=(
            P(None, None, "gy", "gx"),
            P(None, "gy", "gx"),
            P(None, "gy", "gx"),
            P("gy", "gx"),
            P("gy", "gx"),
            P(None, None, "gy", "gx"),
            P("gy", "gx"),
        ),
        out_specs=(P(None, None, "gy", "gx"), P("gy", "gx")),
        check_vma=False,
    )
```

```python
import jax
import jax.numpy as jnp
from jax import lax
from jax.experimental import pallas as pl
from jax.experimental.pallas import tpu as pltpu
from jax.sharding import PartitionSpec as P

advect_rate = 0.25
mix_floor = 0.2
mix_boost = 2.0
mix_slope = 2.0
mix_rate = 1.0
surface_stiffness = 2.0
thermal_steric = 0.5
haline_steric = 0.5
sterics = (thermal_steric, -haline_steric)
spread = 4.0 * surface_stiffness
F32 = jnp.float32
VMEM = pl.BlockSpec(memory_space=pltpu.VMEM)
HBM = pl.BlockSpec(memory_space=pltpu.HBM)
vmem_grant = 8 << 20
chunk = 6
U_TILE, V_TILE, LAST_TILE = 2, 3, 4
surface_turn = 18


def lanes_of(shape):
    return lax.broadcasted_iota(jnp.int32, shape, 1)


def rows_of(shape):
    return lax.broadcasted_iota(jnp.int32, shape, 0)


def roll(cells, shift, axis):
    size = cells.shape[axis]
    shift = shift % size
    return cells if shift == 0 else pltpu.roll(cells, shift, axis)


def layer_rows(count, width):
    return rows_of((count, width)).astype(F32)


def pack_columns(
    mask_in, levels_in, eta_in, tracer_in, u_in, v_in, bar_in,
    out_ref, level_ref, eta_ref, tracer_ref, u_ref, v_ref, bar_ref,
    mask_ref, levels_ref, sems,
):
    pairs = (
        (tracer_in, tracer_ref), (u_in, u_ref), (v_in, v_ref), (bar_in, bar_ref),
        (mask_in, mask_ref), (levels_in, levels_ref), (eta_in, eta_ref),
    )
    copies = [pltpu.make_async_copy(source, target, sems.at[i]) for i, (source, target) in enumerate(pairs)]
    for copy in copies:
        copy.start()
    count, height, width = u_ref.shape
    lane = lanes_of((height, width))
    group = lane // 4
    middle = jnp.where((lane % 4 == 1) | (lane % 4 == 2), group, -1)
    beside = jnp.where((lane + 1) % 4 < 2, (lane + 1) // 4 - 1, -1)

    def gathered(field, place, turn, tile):
        for k in range(count):
            tile = jnp.where(place == k, roll(field[k], 4 * k + turn, 1), tile)
        return tile

    empty = jnp.zeros((height, width), F32)
    copies[0].wait()
    for f in range(2):
        out_ref[f] = gathered(tracer_ref.at[f], group, 2, empty)
    copies[1].wait()
    out_ref[U_TILE] = gathered(u_ref, group, 2, empty)
    copies[2].wait()
    v_tile = gathered(v_ref, middle, 2, empty)
    copies[3].wait()
    out_ref[V_TILE] = gathered(bar_ref.at[0], beside, 4, v_tile)
    last = gathered(bar_ref.at[1], middle, 2, empty)
    for copy in copies[4:]:
        copy.wait()
    level = (mask_ref[...] * levels_ref[...]).astype(F32)
    level_ref[...] = level
    depth = jnp.where(lane < width // 2, roll(level, 3, 1), roll(level, -3, 1))
    surface = roll(jnp.where((lane < 3) | (lane >= width - 3), eta_ref[...], depth), -surface_turn, 1)
    start = width - 6 - surface_turn
    out_ref[LAST_TILE] = jnp.where((lane >= start) & (lane < start + 12), surface, last)


class Sides:
    def __init__(self, first_ref, second_ref, level):
        self.refs = (first_ref, second_ref)
        self.level = level
        self.shape = level.shape
        lane = lanes_of(self.shape)
        self.lane = lane
        self.layer = (lane // 4).astype(F32)
        self.eastern = lane % 4 == 1
        east, west = (roll(tile, surface_turn, 1) for tile in self.pick(LAST_TILE))
        half = lane < self.shape[1] // 2
        self.eta = jnp.where(half, east, west)
        self.depth = jnp.where(half, roll(self.eta, -3, 1), roll(self.eta, 3, 1))

    def pick(self, tile):
        first, second = (ref[tile] for ref in self.refs)
        even = is_even("gx", self.shape)
        return jnp.where(even, first, second), jnp.where(even, second, first)

    def inner(self, tile):
        east, west = self.pick(tile)
        return jnp.where(self.eastern, roll(east, -1, 1), roll(west, 1, 1))

    def bars(self):
        east, west = self.pick(V_TILE)
        return [jnp.where(self.eastern, roll(east, -3, 1), roll(west, -1, 1)), self.inner(LAST_TILE)]

    def outer(self, tile):
        east, west = self.pick(tile)
        return jnp.where(self.eastern, roll(east, -2, 1), roll(west, 2, 1))

    def columns(self, cells, east, west):
        return jnp.where(self.eastern, cells[:, east : east + 1], cells[:, west : west + 1])

    def edge_flow(self, own_ref, u_inner):
        width = self.shape[1]
        own_depth = self.columns(self.level, width - 1, 0)
        beyond = self.columns(self.depth, 0, width - 1)
        flow = jnp.where(self.eastern, own_ref[U_TILE], u_inner)
        return jnp.where(self.layer < jnp.minimum(own_depth, beyond), flow, 0.0)


def pack_rows(level_ref, tracer_ref, u_ref, v_ref, bar_ref, c_out, n_out, u_out, b_out, v_out):
    count, height, width = u_ref.shape
    level = level_ref[...]
    layer = layer_rows(count, width)
    for side, (row, inside, face) in enumerate(((height - 1, height - 2, height - 2), (0, 1, 0))):
        depth = jnp.minimum(level[row : row + 1, :], level[inside : inside + 1, :])
        flow = jnp.where(layer < depth, 0.5 * v_ref[:, face, :], 0.0)
        u_out[side] = u_ref[:, row, :]
        for f in range(2):
            part = slice(f * count, (f + 1) * count)
            c = tracer_ref[f, :, row, :]
            c_out[side, part, :] = c
            n_out[side, part, :] = flow * (c + tracer_ref[f, :, inside, :])
            b_out[side, part, :] = bar_ref[f, :, row, :]
    v_out[...] = jnp.where(layer < level[height - 1 :, :], v_ref[:, height - 1, :], 0.0)


class Message:
    def __init__(self, count):
        self.tracers = [slice(f * count, (f + 1) * count) for f in range(2)]
        self.summed = [slice(f * count, (f + 1) * count) for f in range(2, 4)]
        self.bars = [slice(f * count, (f + 1) * count) for f in range(4, 6)]
        self.v = slice(6 * count, 7 * count)
        self.surface = [slice(7 * count + 8 * i, 7 * count + 8 * i + 8) for i in range(2)]
        self.corner = slice(7 * count + 16, 7 * count + 24)
        self.rows = 7 * count + 24


def is_even(axis, shape):
    return jnp.full(shape, lax.rem(lax.axis_index(axis), 2), jnp.int32) == 0


def join_rows(
    level_ref, eta_ref, own_ref, first_ref, second_ref, c_ref, n_ref, u_ref, b_ref, v_ref,
    first_out, second_out,
):
    count, width = v_ref.shape
    level = level_ref[...]
    height = level.shape[0]
    plan = Message(count)
    sides = Sides(first_ref, second_ref, level)
    inner = [sides.inner(f) for f in range(2)]
    v_inner = sides.inner(V_TILE)
    flow = 0.5 * sides.edge_flow(own_ref, sides.inner(U_TILE))
    flux = [flow * (own_ref[f] + inner[f]) for f in range(2)]
    layer = layer_rows(count, width)
    lane = lanes_of((count, width))
    level_row = rows_of((count, width))
    row8 = rows_of((8, width))
    no_flow, pad = jnp.zeros((count, width), F32), jnp.zeros((8, width), F32)

    def put(part, north, south):
        even = is_even("gy", north.shape)
        first_out[part, :] = jnp.where(even, south, north)
        second_out[part, :] = jnp.where(even, north, south)

    def summed(side, f, row, sign):
        depth = level[row : row + 1, :]
        east_flow = jnp.where(layer < jnp.minimum(depth, roll(depth, -1, 1)), 0.5 * u_ref[side], 0.0)
        rate = jnp.where(layer < depth, advect_rate, 0.0)
        c = c_ref[side, plan.tracers[f], :]
        line = flux[f][row : row + 1, :]
        east_end, west_end = (
            jnp.sum(jnp.where(lane == 4 * level_row + m, line, 0.0), axis=1, keepdims=True) for m in (1, 2)
        )
        flux_e = jnp.where(lane == width - 1, east_end, east_flow * (c + roll(c, -1, 1)))
        flux_w = jnp.where(lane == 0, west_end, roll(flux_e, 1, 1))
        return c - rate * ((flux_e - flux_w) + sign * n_ref[side, plan.tracers[f], :])

    for f in range(2):
        part = plan.tracers[f]
        put(part, c_ref[0, part, :], c_ref[1, part, :])
        put(plan.summed[f], summed(0, f, height - 1, -1.0), summed(1, f, 0, 1.0))
        put(plan.bars[f], b_ref[0, part, :], b_ref[1, part, :])
    put(plan.v, v_ref[...], no_flow)
    for part, eta, depth in zip(plan.surface, (eta_ref[...], sides.eta), (level, sides.depth)):
        north = jnp.where(row8 < 4, roll(depth[height - 8 :, :], 4, 0), eta[height - 8 :, :])
        put(part, north, jnp.where(row8 < 4, eta[:8, :], roll(depth[:8, :], 4, 0)))
    lines = [inner[0], inner[1], v_inner]
    north = south = pad
    for index, cells in enumerate(lines):
        north = jnp.where(row8 == index, cells[height - 1 :, :], north)
        south = jnp.where(row8 == index, cells[:1, :], south)
    put(plan.corner, north, south)


def extended(own, side, north, south, turn):
    row8 = rows_of((8, own.shape[1]))
    parts = []
    for index, tile in enumerate((own, side)):
        up, down = (roll(msg[index], turn, 0) for msg in (north, south))
        parts.append(jnp.concatenate([tile, jnp.where(row8 < 4, up, down)], axis=0))
    return jnp.concatenate(parts, axis=1)


pairs = ((0, 0), (0, 1), (0, 2), (1, 1), (1, 2), (2, 2), (2, 3))
centers = ((0.0, 0.25), (1.0, 0.25), (2.0, -0.25))


def surface_kernel(
    level_ref, eta_ref, first_ref, second_ref, first_row, second_row,
    basis_out, level_out, sums_out, *, count,
):
    level = level_ref[...]
    height, width = level.shape
    sides = Sides(first_ref, second_ref, level)
    north, south = [], []
    for part in Message(count).surface:
        even = is_even("gy", (8, width))
        north.append(jnp.where(even, second_row[part, :], first_row[part, :]))
        south.append(jnp.where(even, first_row[part, :], second_row[part, :]))
    eta_ext = extended(eta_ref[...], sides.eta, north, south, 0)
    level_ext = extended(level, sides.depth, north, south, 4)
    level_out[...] = level_ext
    depth = level_ext / count
    east_weight = (surface_stiffness / spread) * jnp.minimum(depth, roll(depth, -1, 1))
    north_weight = (surface_stiffness / spread) * jnp.minimum(depth, roll(depth, -1, 0))

    west_weight, south_weight = roll(east_weight, 1, 1), roll(north_weight, 1, 0)

    def scaled(field):
        along_x = east_weight * (field - roll(field, -1, 1)) + west_weight * (field - roll(field, 1, 1))
        along_y = north_weight * (field - roll(field, -1, 0)) + south_weight * (field - roll(field, 1, 0))
        return along_x + along_y

    powers = [eta_ext]
    for _ in range(3):
        powers.append(scaled(powers[-1]))
    for index in range(3):
        basis_out[index] = powers[index]
    powers = [x[:height, :width] for x in powers]
    table = []
    row = rows_of((8, width))
    for center, tilt in centers:
        one, two, three = powers[1:]
        if center:
            moved = [x - center * y for x, y in zip(powers[1:], powers)]
            twice = [x - center * y for x, y in zip(moved[1:], moved)]
            one, two, three = moved[0], twice[0], twice[1] - center * twice[0]
        vectors = (powers[0], one, two - tilt * one, three - tilt * two)
        part = jnp.zeros((8, width), F32)
        for index, (i, j) in enumerate(pairs):
            part = jnp.where(row == index, jnp.sum(vectors[i] * vectors[j], axis=0, keepdims=True), part)
        table.append(part)
    table = jnp.concatenate(table, axis=0)
    totals = jnp.sum(table, axis=1, keepdims=True)
    place = lanes_of(table.shape) == rows_of(table.shape)
    line = jnp.sum(jnp.where(place, totals, 0.0), axis=0, keepdims=True)
    sums_out[...] = jnp.broadcast_to(line, sums_out.shape)


def galerkin(sums):
    lane = lanes_of(sums.shape)
    d00, d01, d02, d11, d12, d22, d2q = [roll(sums, -i, 1) for i in range(7)]
    mean, square = d01[:, :1], d00[:, :1]
    place = jnp.zeros(mean.shape, jnp.int32)
    center = jnp.full(sums.shape, centers[0][0], F32)
    tilt = jnp.full(sums.shape, centers[0][1], F32)
    for index in range(1, len(centers)):
        place = jnp.where(mean > 0.5 * (centers[index - 1][0] + centers[index][0]) * square, 8 * index, place)
        center = jnp.where(lane == 8 * index, centers[index][0], center)
        tilt = jnp.where(lane == 8 * index, centers[index][1], tilt)
    base = 1.0 + spread * center
    k00 = base * d00 + spread * d01
    k01 = base * d01 + spread * d11
    k02 = base * d02 + spread * d12
    k11 = base * d11 + spread * (tilt * d11 + d12)
    k12 = base * d12 + spread * (tilt * d12 + d22)
    k22 = base * d22 + spread * d2q
    i00 = 1.0 / k00
    s11 = k11 - k01 * k01 * i00
    s12 = k12 - k01 * k02 * i00
    s22 = k22 - k02 * k02 * i00
    g1 = spread * (d01 * d01 - d00 * d11) * i00
    g2 = spread * (d02 * d01 - d00 * d12) * i00
    second = s11 > 1e-7 * k11
    i11 = jnp.where(second, 1.0 / s11, 0.0)
    c12 = s12 * i11
    last = s22 - s12 * c12
    third = second & (last > 4e-7 * s22)
    y2 = jnp.where(third, (g2 - g1 * c12) / last, 0.0)
    y1 = (g1 - s12 * y2) * i11
    y0 = (d00 - k01 * y1 - k02 * y2) * i00
    inner = center + tilt
    results = (y0 - center * y1 + center * inner * y2, y1 - (center + inner) * y2, y2)
    return [jnp.sum(jnp.where(lane == place, y, 0.0), axis=1, keepdims=True) for y in results]


def column_kernel(
    tracer_ref, u_ref, v_ref, bar_ref,
    own_ref, first_ref, second_ref, c_rows, v_row, first_row, second_row, level_ref, basis_ref,
    base_out, share_out,
    side_ref, turn_ref, ratio_ref, slope_ref, value_ref, adjoint_ref,
):
    count, height, width = u_ref.shape
    level_ext = level_ref[...]
    level = level_ext[:height, :width]
    sides = Sides(first_ref, second_ref, level)
    lane, row = lanes_of((height, width)), rows_of((height, width))
    layer = layer_rows(count, width)
    last_row, last_lane = level_ext.shape[0] - 1, level_ext.shape[1] - 1
    plan = Message(count)

    def from_north(part):
        even = is_even("gy", (part.stop - part.start, width))
        return jnp.where(even, second_row[part, :], first_row[part, :])

    def from_south(part):
        even = is_even("gy", (part.stop - part.start, width))
        return jnp.where(even, first_row[part, :], second_row[part, :])


    inner = [sides.inner(f) for f in range(2)]
    u_inner, v_inner = sides.inner(U_TILE), sides.inner(V_TILE)
    edge_flow = sides.edge_flow(own_ref, u_inner)
    edge_flux = [0.5 * edge_flow * (own_ref[f] + inner[f]) for f in range(2)]
    depth_in = sides.columns(sides.depth, 0, width - 1)
    depth_out = sides.columns(sides.depth, 1, width - 2)
    far_flow = jnp.where(sides.eastern, u_inner, sides.outer(U_TILE))
    far_flow = jnp.where(sides.layer < jnp.minimum(depth_in, depth_out), far_flow, 0.0)
    corner_depth = [
        jnp.where(sides.eastern[:1], level_ext[r : r + 1, width : width + 1], level_ext[r : r + 1, last_lane:])
        for r in (height, last_row)
    ]
    corner_north, corner_south = from_north(plan.corner), from_south(plan.corner)
    depth_up = jnp.where(row == height - 1, corner_depth[0], roll(depth_in, -1, 0))
    up_flow = jnp.where(sides.layer < jnp.minimum(depth_in, depth_up), v_inner, 0.0)
    low_flow = jnp.where(
        sides.layer[:1] < jnp.minimum(depth_in[:1], corner_depth[1]), corner_south[2:3, :], 0.0
    )
    rate = jnp.where(sides.layer < depth_in, advect_rate, 0.0)
    outward = jnp.where(sides.eastern, 1.0, -1.0)
    beyond = []
    for f in range(2):
        c = inner[f]
        far_flux = 0.5 * far_flow * (c + sides.outer(f))
        c_up = jnp.where(row == height - 1, corner_north[f : f + 1, :], roll(c, -1, 0))
        flux_n = 0.5 * up_flow * (c + c_up)
        low_flux = 0.5 * low_flow * (corner_south[f : f + 1, :] + c[:1])
        flux_s = jnp.where(row == 0, low_flux, roll(flux_n, 1, 0))
        beyond.append(c - rate * (outward * (far_flux - edge_flux[f]) + (flux_n - flux_s)))
    beyond += sides.bars() + [depth_in]
    filler = jnp.zeros((width - height * len(beyond), width), F32)
    turned = jnp.transpose(jnp.concatenate(beyond + [filler], axis=0))

    south_flow = jnp.where(layer < level[:1, :], from_south(plan.v), 0.0)
    north_flow = jnp.where(layer < level_ext[height : height + 1, :width], v_row[...], 0.0)
    south_flux, north_flux = [], []
    side_ref[...] = jnp.zeros_like(side_ref)
    for f in range(2):
        part = plan.tracers[f]
        south_flux.append(0.5 * south_flow * (from_south(part) + c_rows[1, part, :]))
        north_flux.append(0.5 * north_flow * (c_rows[0, part, :] + from_north(part)))
        side_ref[f, pl.ds(4, count, stride=8), :] = from_south(plan.summed[f]) - advect_rate * south_flux[f]
        side_ref[f, pl.ds(5, count, stride=8), :] = from_north(plan.summed[f]) + advect_rate * north_flux[f]
        side_ref[2 + f, pl.ds(4, count, stride=8), :] = from_south(plan.bars[f])
        side_ref[2 + f, pl.ds(5, count, stride=8), :] = from_north(plan.bars[f])
    for f in range(4):
        turn_ref[f] = roll(turned, -height * f, 1)
        for m in (1, 2):
            side_ref[f, pl.ds(m, count, stride=8), :] = turn_ref[f, pl.ds(m, count, stride=4), :]
    row8 = rows_of((8, width))
    side_level = roll(turned[:8, :], -4 * height, 1)
    side_level = jnp.where((row8 == 1) | (row8 == 2), side_level, 0.0)
    side_level = jnp.where(row8 == 4, level_ext[last_row:, :width], side_level)
    side_level = jnp.where(row8 == 5, level_ext[height : height + 1, :width], side_level)
    level_all = jnp.concatenate([level, side_level], axis=0)

    east_depth = jnp.minimum(level_ext, roll(level_ext, -1, 1))[:height, :width]
    north_depth = jnp.minimum(level_ext, roll(level_ext, -1, 0))[:height, :width]

    def with_side(own, f, k):
        return jnp.concatenate([own, side_ref[f, 8 * k : 8 * k + 8, :]], axis=0)

    def advected(k):
        flow_e = jnp.where(east_depth > k, 0.5 * u_ref[k], 0.0)
        flow_n = jnp.where(north_depth > k, 0.5 * v_ref[k], 0.0)
        wet_rate = jnp.where(level > k, advect_rate, 0.0)
        result = []
        for f in range(2):
            c = tracer_ref[f, k]
            ends = roll(edge_flux[f], -(4 * k + 2), 1)
            flux_e = jnp.where(lane == width - 1, ends, flow_e * (c + roll(c, -1, 1)))
            flux_w = jnp.where(lane == 0, ends, roll(flux_e, 1, 1))
            flux_n = jnp.where(row == height - 1, north_flux[f][k : k + 1, :], flow_n * (c + roll(c, -1, 0)))
            flux_s = jnp.where(row == 0, south_flux[f][k : k + 1, :], roll(flux_n, 1, 0))
            result.append(with_side(c - wet_rate * ((flux_e - flux_w) + (flux_n - flux_s)), f, k))
        return result

    now = advected(0)
    kappa_up = ratio_up = values = None
    for k in range(count):
        diagonal = 1.0
        kappa = later = None
        if k < count - 1:
            later = advected(k + 1)
            step = (now[1] - now[0]) - (later[1] - later[0])
            gate = jax.nn.sigmoid(mix_slope * step)
            wet_below = level_all > k + 1
            kappa = jnp.where(wet_below, mix_floor + mix_boost * gate, 0.0)
            slope_ref[k] = jnp.where(wet_below, (mix_boost * mix_slope) * gate * (1.0 - gate), 0.0)
            diagonal = diagonal + mix_rate * kappa
        if k > 0:
            diagonal = diagonal + mix_rate * kappa_up * (1.0 - ratio_up)
        inverse = 1.0 / diagonal
        right = [now[0], now[1], with_side(bar_ref[0, k], 2, k), with_side(bar_ref[1, k], 3, k)]
        if k > 0:
            right = [cells + mix_rate * kappa_up * value for cells, value in zip(right, values)]
        values = [cells * inverse for cells in right]
        for f in range(4):
            value_ref[f, k] = values[f]
        if kappa is not None:
            ratio_up, kappa_up = mix_rate * kappa * inverse, kappa
            ratio_ref[k] = ratio_up
        now = later

    def emit(k, cells, change):
        for f, sign in ((0, -1.0), (1, 1.0)):
            full = cells[2 + f] + sign * change
            adjoint_ref[f, k] = full[:height, :]
            side_ref[f, 8 * k : 8 * k + 8, :] = full[height:, :]

    below = values
    pull_below = None
    for k in range(count - 2, -1, -1):
        here = [value_ref[f, k] + ratio_ref[k] * below[f] for f in range(4)]
        pull = (-mix_rate) * slope_ref[k] * (
            (here[2] - below[2]) * (here[0] - below[0]) + (here[3] - below[3]) * (here[1] - below[1])
        )
        emit(k + 1, below, -pull if pull_below is None else pull_below - pull)
        below, pull_below = here, pull
    emit(0, below, pull_below)

    for f in range(2):
        for m in (1, 2):
            turn_ref[f, pl.ds(m, count, stride=4), :] = side_ref[f, pl.ds(m, count, stride=8), :]
    wide = lanes_of((width, width)) < height
    back = jnp.transpose(jnp.where(wide, turn_ref[0], roll(turn_ref[1], height, 1)))
    ends_of = [back[f * height : (f + 1) * height, :] for f in range(2)]
    south_line = [side_ref[f, pl.ds(4, count, stride=8), :] for f in range(2)]
    north_line = [side_ref[f, pl.ds(5, count, stride=8), :] for f in range(2)]
    steps = []
    for b in range(3):
        field = basis_ref[b]
        east = (0.5 * advect_rate) * (field - roll(field, -1, 1))
        north = (0.5 * advect_rate) * (field - roll(field, -1, 0))
        around = (field, east, roll(east, 1, 1), north, roll(north, 1, 0))
        steps.append([cells[:height, :width] for cells in around])
    for k in range(count):
        flow_e = jnp.where(east_depth > k, u_ref[k], 0.0)
        flow_n = jnp.where(north_depth > k, v_ref[k], 0.0)
        ends_flow = roll(edge_flow, -(4 * k + 2), 1)
        low = south_flow[k : k + 1, :]
        flow_w = jnp.where(lane == 0, ends_flow, roll(flow_e, 1, 1))
        flow_s = jnp.where(row == 0, low, roll(flow_n, 1, 0))
        for b, (field, east, west, north, south) in enumerate(steps):
            part = (flow_e * east + flow_w * west) + (flow_n * north + flow_s * south)
            share_out[b, k] = jnp.where(level > k, field, 0.0) - part
        for f in range(2):
            y = adjoint_ref[f, k]
            ends = roll(ends_of[f], -(4 * k + 2), 1)
            y_east = jnp.where(lane == width - 1, ends, roll(y, -1, 1))
            y_north = jnp.where(row == height - 1, north_line[f][k : k + 1, :], roll(y, -1, 0))
            part_e = flow_e * (y - y_east)
            part_n = flow_n * (y - y_north)
            part_w = jnp.where(lane == 0, ends_flow * (ends - y), roll(part_e, 1, 1))
            part_s = jnp.where(row == 0, low * (south_line[f][k : k + 1, :] - y), roll(part_n, 1, 0))
            base_out[f, k] = y - (0.5 * advect_rate) * ((part_e + part_w) + (part_n + part_s))


def final_kernel(sums_ref, basis_ref, base_ref, share_ref, tracer_hbm, eta_hbm, tracer_out, eta_out, sems):
    _, count, height, width = base_ref.shape
    y0, y1, y2 = galerkin(jnp.sum(sums_ref[...], axis=0, keepdims=True))

    def combined(fields):
        return y0 * fields[0] + (y1 * fields[1] + y2 * fields[2])

    eta_out[...] = combined([basis_ref[b, :height, :width] for b in range(3)])
    copies = [pltpu.make_async_copy(eta_out, eta_hbm, sems.at[0])]
    copies[0].start()
    for k in range(count):
        share = combined([share_ref[b, k] for b in range(3)])
        for f in range(2):
            tracer_out[f, k] = base_ref[f, k] + sterics[f] * share
        if (k + 1) % chunk == 0 or k == count - 1:
            levels = pl.ds(k - k % chunk, k % chunk + 1)
            at = len(copies)
            copies.append(pltpu.make_async_copy(tracer_out.at[:, levels], tracer_hbm.at[:, levels], sems.at[at]))
            copies[-1].start()
    for copy in copies:
        copy.wait()


def call(kernel, outs, name, specs=None, scratch=(), cost=None, out_spec=VMEM):
    def run(*operands):
        return pl.pallas_call(
            kernel,
            out_shape=[jax.ShapeDtypeStruct(shape, F32) for shape in outs],
            in_specs=specs or [VMEM] * len(operands),
            out_specs=[out_spec] * len(outs),
            scratch_shapes=list(scratch),
            cost_estimate=cost,
            compiler_params=pltpu.CompilerParams(vmem_limit_bytes=vmem_grant),
            name=name,
        )(*operands)

    return run


def swap(cells, axis, first, wrap):
    count = lax.axis_size(axis)
    pairs = []
    for i in range(first, count, 2):
        if i + 1 < count or wrap:
            j = (i + 1) % count
            pairs += [(i, j), (j, i)]
    return lax.ppermute(cells, axis, pairs)


def per_device(tracers, uvel, vvel, sea_mask, levels, tracer_bar, eta_bar):
    _, count, height, width = tracers.shape
    devices = lax.axis_size("gx") * lax.axis_size("gy")
    tile = (height, width)
    rows = (2, 2 * count, width)
    field = (count,) + tile
    inputs = (sea_mask, levels, eta_bar, tracers, uvel, vvel, tracer_bar)
    own, level, eta, tracers, uvel, vvel, tracer_bar = call(
        pack_columns,
        [(LAST_TILE + 1,) + tile, tile, tile, (2,) + field, field, field, (2,) + field],
        "pack_columns",
        [HBM] * 7,
        [pltpu.VMEM(tile, jnp.int32), pltpu.VMEM(tile, jnp.int32), pltpu.SemaphoreType.DMA((7,))],
    )(*(pltpu.with_memory_space_constraint(x, pltpu.HBM) for x in inputs))
    first, second = swap(own, "gx", 0, True), swap(own, "gx", 1, True)
    c_rows, n_rows, u_rows, b_rows, v_row = call(
        pack_rows, [rows, rows, (2, count, width), rows, (count, width)], "pack_rows"
    )(level, tracers, uvel, vvel, tracer_bar)
    plan = Message(count)
    message = (plan.rows, width)
    first_msg, second_msg = call(join_rows, [message, message], "join_rows")(
        level, eta, own, first, second, c_rows, n_rows, u_rows, b_rows, v_row
    )
    first_row, second_row = swap(first_msg, "gy", 1, False), swap(second_msg, "gy", 0, False)
    ext = (height + 8, 2 * width)

    def surface(*refs):
        surface_kernel(*refs, count=count)

    basis, level_ext, sums = call(surface, [(3,) + ext, ext, (devices, width)], "surface")(
        level, eta, first, second, first_row, second_row
    )
    all_sums = lax.all_to_all(sums.reshape(devices, 1, width), ("gx", "gy"), 0, 0).reshape(devices, width)
    taller = (count, height + 8, width)
    base, shares = call(
        column_kernel,
        [(2,) + field, (3,) + field],
        "columns",
        None,
        [
            pltpu.VMEM((4, 8 * count, width), F32),
            pltpu.VMEM((4, width, width), F32),
            pltpu.VMEM(taller, F32),
            pltpu.VMEM(taller, F32),
            pltpu.VMEM((4,) + taller, F32),
            pltpu.VMEM((2,) + field, F32),
        ],
        pl.CostEstimate(flops=400 * count * height * width, transcendentals=count * height * width, bytes_accessed=1 << 22),
    )(tracers, uvel, vvel, tracer_bar, own, first, second, c_rows, v_row, first_row, second_row, level_ext, basis)
    pieces = (count + chunk - 1) // chunk
    tracer_adj, eta_adj = call(
        final_kernel,
        [(2,) + field, tile],
        "finish",
        None,
        [pltpu.VMEM((2,) + field, F32), pltpu.VMEM(tile, F32), pltpu.SemaphoreType.DMA((pieces + 1,))],
        out_spec=HBM,
    )(all_sums, basis, base, shares)
    return (tracer_adj, eta_adj)


def solution(mesh):
    return jax.shard_map(
        per_device,
        mesh=mesh,
        in_specs=(
            P(None, None, "gy", "gx"),
            P(None, "gy", "gx"),
            P(None, "gy", "gx"),
            P("gy", "gx"),
            P("gy", "gx"),
            P(None, None, "gy", "gx"),
            P("gy", "gx"),
        ),
        out_specs=(P(None, None, "gy", "gx"), P("gy", "gx")),
        check_vma=False,
    )
```

```python
import jax
import jax.numpy as jnp
from jax import lax
from jax.experimental import pallas as pl
from jax.experimental.pallas import tpu as pltpu
from jax.sharding import PartitionSpec as P

advect_rate = 0.25
mix_floor = 0.2
mix_boost = 2.0
mix_slope = 2.0
mix_rate = 1.0
surface_stiffness = 2.0
thermal_steric = 0.5
haline_steric = 0.5
sterics = (thermal_steric, -haline_steric)
spread = 4.0 * surface_stiffness
F32 = jnp.float32
VMEM = pl.BlockSpec(memory_space=pltpu.VMEM)
HBM = pl.BlockSpec(memory_space=pltpu.HBM)
vmem_grant = 8 << 20
chunk = 6
U_TILE, V_TILE, LAST_TILE = 2, 3, 4
surface_turn = 18


def lanes_of(shape):
    return lax.broadcasted_iota(jnp.int32, shape, 1)


def rows_of(shape):
    return lax.broadcasted_iota(jnp.int32, shape, 0)


def roll(cells, shift, axis):
    size = cells.shape[axis]
    shift = shift % size
    return cells if shift == 0 else pltpu.roll(cells, shift, axis)


def layer_rows(count, width):
    return rows_of((count, width)).astype(F32)


def pack_columns(
    mask_in, levels_in, eta_in, tracer_in, u_in, v_in, bar_in,
    out_ref, level_ref, eta_ref, tracer_ref, u_ref, v_ref, bar_ref,
    mask_ref, levels_ref, sems,
):
    pairs = (
        (tracer_in, tracer_ref), (u_in, u_ref), (v_in, v_ref), (bar_in, bar_ref),
        (mask_in, mask_ref), (levels_in, levels_ref), (eta_in, eta_ref),
    )
    copies = [pltpu.make_async_copy(source, target, sems.at[i]) for i, (source, target) in enumerate(pairs)]
    for copy in copies:
        copy.start()
    count, height, width = u_ref.shape
    lane = lanes_of((height, width))
    group = lane // 4
    middle = jnp.where((lane % 4 == 1) | (lane % 4 == 2), group, -1)
    beside = jnp.where((lane + 1) % 4 < 2, (lane + 1) // 4 - 1, -1)

    def gathered(field, place, turn, tile):
        for k in range(count):
            tile = jnp.where(place == k, roll(field[k], 4 * k + turn, 1), tile)
        return tile

    empty = jnp.zeros((height, width), F32)
    copies[0].wait()
    for f in range(2):
        out_ref[f] = gathered(tracer_ref.at[f], group, 2, empty)
    copies[1].wait()
    out_ref[U_TILE] = gathered(u_ref, group, 2, empty)
    copies[2].wait()
    v_tile = gathered(v_ref, middle, 2, empty)
    copies[3].wait()
    out_ref[V_TILE] = gathered(bar_ref.at[0], beside, 4, v_tile)
    last = gathered(bar_ref.at[1], middle, 2, empty)
    for copy in copies[4:]:
        copy.wait()
    level = (mask_ref[...] * levels_ref[...]).astype(F32)
    level_ref[...] = level
    depth = jnp.where(lane < width // 2, roll(level, 3, 1), roll(level, -3, 1))
    surface = roll(jnp.where((lane < 3) | (lane >= width - 3), eta_ref[...], depth), -surface_turn, 1)
    start = width - 6 - surface_turn
    out_ref[LAST_TILE] = jnp.where((lane >= start) & (lane < start + 12), surface, last)


class Sides:
    def __init__(self, first_ref, second_ref, level):
        self.refs = (first_ref, second_ref)
        self.level = level
        self.shape = level.shape
        lane = lanes_of(self.shape)
        self.lane = lane
        self.layer = (lane // 4).astype(F32)
        self.eastern = lane % 4 == 1
        east, west = (roll(tile, surface_turn, 1) for tile in self.pick(LAST_TILE))
        half = lane < self.shape[1] // 2
        self.eta = jnp.where(half, east, west)
        self.depth = jnp.where(half, roll(self.eta, -3, 1), roll(self.eta, 3, 1))

    def pick(self, tile):
        first, second = (ref[tile] for ref in self.refs)
        even = is_even("gx", self.shape)
        return jnp.where(even, first, second), jnp.where(even, second, first)

    def inner(self, tile):
        east, west = self.pick(tile)
        return jnp.where(self.eastern, roll(east, -1, 1), roll(west, 1, 1))

    def bars(self):
        east, west = self.pick(V_TILE)
        return [jnp.where(self.eastern, roll(east, -3, 1), roll(west, -1, 1)), self.inner(LAST_TILE)]

    def outer(self, tile):
        east, west = self.pick(tile)
        return jnp.where(self.eastern, roll(east, -2, 1), roll(west, 2, 1))

    def columns(self, cells, east, west):
        return jnp.where(self.eastern, cells[:, east : east + 1], cells[:, west : west + 1])

    def edge_flow(self, own_ref, u_inner):
        width = self.shape[1]
        own_depth = self.columns(self.level, width - 1, 0)
        beyond = self.columns(self.depth, 0, width - 1)
        flow = jnp.where(self.eastern, own_ref[U_TILE], u_inner)
        return jnp.where(self.layer < jnp.minimum(own_depth, beyond), flow, 0.0)


def pack_rows(level_ref, tracer_ref, u_ref, v_ref, bar_ref, c_out, n_out, u_out, b_out, v_out):
    count, height, width = u_ref.shape
    level = level_ref[...]
    layer = layer_rows(count, width)
    for side, (row, inside, face) in enumerate(((height - 1, height - 2, height - 2), (0, 1, 0))):
        depth = jnp.minimum(level[row : row + 1, :], level[inside : inside + 1, :])
        flow = jnp.where(layer < depth, 0.5 * v_ref[:, face, :], 0.0)
        u_out[side] = u_ref[:, row, :]
        for f in range(2):
            part = slice(f * count, (f + 1) * count)
            c = tracer_ref[f, :, row, :]
            c_out[side, part, :] = c
            n_out[side, part, :] = flow * (c + tracer_ref[f, :, inside, :])
            b_out[side, part, :] = bar_ref[f, :, row, :]
    v_out[...] = jnp.where(layer < level[height - 1 :, :], v_ref[:, height - 1, :], 0.0)


class Message:
    def __init__(self, count):
        self.tracers = [slice(f * count, (f + 1) * count) for f in range(2)]
        self.summed = [slice(f * count, (f + 1) * count) for f in range(2, 4)]
        self.bars = [slice(f * count, (f + 1) * count) for f in range(4, 6)]
        self.v = slice(6 * count, 7 * count)
        self.surface = [slice(7 * count + 8 * i, 7 * count + 8 * i + 8) for i in range(2)]
        self.corner = slice(7 * count + 16, 7 * count + 24)
        self.rows = 7 * count + 24


def is_even(axis, shape):
    return jnp.full(shape, lax.rem(lax.axis_index(axis), 2), jnp.int32) == 0


def join_rows(
    level_ref, eta_ref, own_ref, first_ref, second_ref, c_ref, n_ref, u_ref, b_ref, v_ref,
    first_out, second_out,
):
    count, width = v_ref.shape
    level = level_ref[...]
    height = level.shape[0]
    plan = Message(count)
    sides = Sides(first_ref, second_ref, level)
    inner = [sides.inner(f) for f in range(2)]
    v_inner = sides.inner(V_TILE)
    flow = 0.5 * sides.edge_flow(own_ref, sides.inner(U_TILE))
    flux = [flow * (own_ref[f] + inner[f]) for f in range(2)]
    layer = layer_rows(count, width)
    lane = lanes_of((count, width))
    level_row = rows_of((count, width))
    row8 = rows_of((8, width))
    no_flow, pad = jnp.zeros((count, width), F32), jnp.zeros((8, width), F32)

    def put(part, north, south):
        even = is_even("gy", north.shape)
        first_out[part, :] = jnp.where(even, south, north)
        second_out[part, :] = jnp.where(even, north, south)

    def summed(side, f, row, sign):
        depth = level[row : row + 1, :]
        east_flow = jnp.where(layer < jnp.minimum(depth, roll(depth, -1, 1)), 0.5 * u_ref[side], 0.0)
        rate = jnp.where(layer < depth, advect_rate, 0.0)
        c = c_ref[side, plan.tracers[f], :]
        line = flux[f][row : row + 1, :]
        east_end, west_end = (
            jnp.sum(jnp.where(lane == 4 * level_row + m, line, 0.0), axis=1, keepdims=True) for m in (1, 2)
        )
        flux_e = jnp.where(lane == width - 1, east_end, east_flow * (c + roll(c, -1, 1)))
        flux_w = jnp.where(lane == 0, west_end, roll(flux_e, 1, 1))
        return c - rate * ((flux_e - flux_w) + sign * n_ref[side, plan.tracers[f], :])

    for f in range(2):
        part = plan.tracers[f]
        put(part, c_ref[0, part, :], c_ref[1, part, :])
        put(plan.summed[f], summed(0, f, height - 1, -1.0), summed(1, f, 0, 1.0))
        put(plan.bars[f], b_ref[0, part, :], b_ref[1, part, :])
    put(plan.v, v_ref[...], no_flow)
    for part, eta, depth in zip(plan.surface, (eta_ref[...], sides.eta), (level, sides.depth)):
        north = jnp.where(row8 < 4, roll(depth[height - 8 :, :], 4, 0), eta[height - 8 :, :])
        put(part, north, jnp.where(row8 < 4, eta[:8, :], roll(depth[:8, :], 4, 0)))
    lines = [inner[0], inner[1], v_inner]
    north = south = pad
    for index, cells in enumerate(lines):
        north = jnp.where(row8 == index, cells[height - 1 :, :], north)
        south = jnp.where(row8 == index, cells[:1, :], south)
    put(plan.corner, north, south)


def extended(own, side, north, south, turn):
    row8 = rows_of((8, own.shape[1]))
    parts = []
    for index, tile in enumerate((own, side)):
        up, down = (roll(msg[index], turn, 0) for msg in (north, south))
        parts.append(jnp.concatenate([tile, jnp.where(row8 < 4, up, down)], axis=0))
    return jnp.concatenate(parts, axis=1)


pairs = ((0, 0), (0, 1), (0, 2), (1, 1), (1, 2), (2, 2), (2, 3))
centers = ((0.0, 0.25), (1.0, 0.25), (2.0, -0.25))


def surface_kernel(
    level_ref, eta_ref, first_ref, second_ref, first_row, second_row,
    basis_out, level_out, sums_out, *, count,
):
    level = level_ref[...]
    height, width = level.shape
    sides = Sides(first_ref, second_ref, level)
    north, south = [], []
    for part in Message(count).surface:
        even = is_even("gy", (8, width))
        north.append(jnp.where(even, second_row[part, :], first_row[part, :]))
        south.append(jnp.where(even, first_row[part, :], second_row[part, :]))
    eta_ext = extended(eta_ref[...], sides.eta, north, south, 0)
    level_ext = extended(level, sides.depth, north, south, 4)
    level_out[...] = level_ext
    rate = surface_stiffness / (spread * count)
    east_weight, west_weight = (rate * jnp.minimum(level_ext, roll(level_ext, step, 1)) for step in (-1, 1))
    north_weight, south_weight = (rate * jnp.minimum(level_ext, roll(level_ext, step, 0)) for step in (-1, 1))

    def scaled(field):
        along_x = east_weight * (field - roll(field, -1, 1)) + west_weight * (field - roll(field, 1, 1))
        along_y = north_weight * (field - roll(field, -1, 0)) + south_weight * (field - roll(field, 1, 0))
        return along_x + along_y

    powers = [eta_ext]
    for _ in range(3):
        powers.append(scaled(powers[-1]))
    for index in range(3):
        basis_out[index] = powers[index]
    powers = [x[:height, :width] for x in powers]
    table = []
    row = rows_of((8, width))
    for center, tilt in centers:
        one, two, three = powers[1:]
        if center:
            moved = [x - center * y for x, y in zip(powers[1:], powers)]
            twice = [x - center * y for x, y in zip(moved[1:], moved)]
            one, two, three = moved[0], twice[0], twice[1] - center * twice[0]
        vectors = (powers[0], one, two - tilt * one, three - tilt * two)
        part = jnp.zeros((8, width), F32)
        for index, (i, j) in enumerate(pairs):
            part = jnp.where(row == index, jnp.sum(vectors[i] * vectors[j], axis=0, keepdims=True), part)
        table.append(part)
    table = jnp.concatenate(table, axis=0)
    totals = jnp.sum(table, axis=1, keepdims=True)
    place = lanes_of(table.shape) == rows_of(table.shape)
    line = jnp.sum(jnp.where(place, totals, 0.0), axis=0, keepdims=True)
    sums_out[...] = jnp.broadcast_to(line, sums_out.shape)


def galerkin(sums):
    lane = lanes_of(sums.shape)
    d00, d01, d02, d11, d12, d22, d2q = [roll(sums, -i, 1) for i in range(7)]
    mean, square = d01[:, :1], d00[:, :1]
    place = jnp.zeros(mean.shape, jnp.int32)
    center = jnp.full(sums.shape, centers[0][0], F32)
    tilt = jnp.full(sums.shape, centers[0][1], F32)
    for index in range(1, len(centers)):
        place = jnp.where(mean > 0.5 * (centers[index - 1][0] + centers[index][0]) * square, 8 * index, place)
        center = jnp.where(lane == 8 * index, centers[index][0], center)
        tilt = jnp.where(lane == 8 * index, centers[index][1], tilt)
    base = 1.0 + spread * center
    k00 = base * d00 + spread * d01
    k01 = base * d01 + spread * d11
    k02 = base * d02 + spread * d12
    k11 = base * d11 + spread * (tilt * d11 + d12)
    k12 = base * d12 + spread * (tilt * d12 + d22)
    k22 = base * d22 + spread * d2q
    i00 = 1.0 / k00
    s11 = k11 - k01 * k01 * i00
    s12 = k12 - k01 * k02 * i00
    s22 = k22 - k02 * k02 * i00
    g1 = spread * (d01 * d01 - d00 * d11) * i00
    g2 = spread * (d02 * d01 - d00 * d12) * i00
    second = s11 > 1e-7 * k11
    i11 = jnp.where(second, 1.0 / s11, 0.0)
    c12 = s12 * i11
    last = s22 - s12 * c12
    third = second & (last > 4e-7 * s22)
    y2 = jnp.where(third, (g2 - g1 * c12) / last, 0.0)
    y1 = (g1 - s12 * y2) * i11
    y0 = (d00 - k01 * y1 - k02 * y2) * i00
    inner = center + tilt
    results = (y0 - center * y1 + center * inner * y2, y1 - (center + inner) * y2, y2)
    return [jnp.sum(jnp.where(lane == place, y, 0.0), axis=1, keepdims=True) for y in results]


def column_kernel(
    tracer_ref, u_ref, v_ref, bar_ref,
    own_ref, first_ref, second_ref, c_rows, v_row, first_row, second_row, level_ref, basis_ref,
    base_out, share_out,
    side_ref, turn_ref, ratio_ref, slope_ref, value_ref, adjoint_ref,
):
    count, height, width = u_ref.shape
    level_ext = level_ref[...]
    level = level_ext[:height, :width]
    sides = Sides(first_ref, second_ref, level)
    lane, row = lanes_of((height, width)), rows_of((height, width))
    layer = layer_rows(count, width)
    last_row, last_lane = level_ext.shape[0] - 1, level_ext.shape[1] - 1
    plan = Message(count)

    def from_north(part):
        even = is_even("gy", (part.stop - part.start, width))
        return jnp.where(even, second_row[part, :], first_row[part, :])

    def from_south(part):
        even = is_even("gy", (part.stop - part.start, width))
        return jnp.where(even, first_row[part, :], second_row[part, :])


    inner = [sides.inner(f) for f in range(2)]
    u_inner, v_inner = sides.inner(U_TILE), sides.inner(V_TILE)
    edge_flow = sides.edge_flow(own_ref, u_inner)
    edge_flux = [0.5 * edge_flow * (own_ref[f] + inner[f]) for f in range(2)]
    depth_in = sides.columns(sides.depth, 0, width - 1)
    depth_out = sides.columns(sides.depth, 1, width - 2)
    far_flow = jnp.where(sides.eastern, u_inner, sides.outer(U_TILE))
    far_flow = jnp.where(sides.layer < jnp.minimum(depth_in, depth_out), far_flow, 0.0)
    corner_depth = [
        jnp.where(sides.eastern[:1], level_ext[r : r + 1, width : width + 1], level_ext[r : r + 1, last_lane:])
        for r in (height, last_row)
    ]
    corner_north, corner_south = from_north(plan.corner), from_south(plan.corner)
    depth_up = jnp.where(row == height - 1, corner_depth[0], roll(depth_in, -1, 0))
    up_flow = jnp.where(sides.layer < jnp.minimum(depth_in, depth_up), v_inner, 0.0)
    low_flow = jnp.where(
        sides.layer[:1] < jnp.minimum(depth_in[:1], corner_depth[1]), corner_south[2:3, :], 0.0
    )
    rate = jnp.where(sides.layer < depth_in, advect_rate, 0.0)
    outward = jnp.where(sides.eastern, 1.0, -1.0)
    beyond = []
    for f in range(2):
        c = inner[f]
        far_flux = 0.5 * far_flow * (c + sides.outer(f))
        c_up = jnp.where(row == height - 1, corner_north[f : f + 1, :], roll(c, -1, 0))
        flux_n = 0.5 * up_flow * (c + c_up)
        low_flux = 0.5 * low_flow * (corner_south[f : f + 1, :] + c[:1])
        flux_s = jnp.where(row == 0, low_flux, roll(flux_n, 1, 0))
        beyond.append(c - rate * (outward * (far_flux - edge_flux[f]) + (flux_n - flux_s)))
    beyond += sides.bars() + [depth_in]
    filler = jnp.zeros((width - height * len(beyond), width), F32)
    turned = jnp.transpose(jnp.concatenate(beyond + [filler], axis=0))

    south_flow = jnp.where(layer < level[:1, :], from_south(plan.v), 0.0)
    north_flow = jnp.where(layer < level_ext[height : height + 1, :width], v_row[...], 0.0)
    south_flux, north_flux = [], []
    side_ref[...] = jnp.zeros_like(side_ref)
    for f in range(2):
        part = plan.tracers[f]
        south_flux.append(0.5 * south_flow * (from_south(part) + c_rows[1, part, :]))
        north_flux.append(0.5 * north_flow * (c_rows[0, part, :] + from_north(part)))
        side_ref[f, pl.ds(4, count, stride=8), :] = from_south(plan.summed[f]) - advect_rate * south_flux[f]
        side_ref[f, pl.ds(5, count, stride=8), :] = from_north(plan.summed[f]) + advect_rate * north_flux[f]
        side_ref[2 + f, pl.ds(4, count, stride=8), :] = from_south(plan.bars[f])
        side_ref[2 + f, pl.ds(5, count, stride=8), :] = from_north(plan.bars[f])
    for f in range(4):
        turn_ref[f] = roll(turned, -height * f, 1)
        for m in (1, 2):
            side_ref[f, pl.ds(m, count, stride=8), :] = turn_ref[f, pl.ds(m, count, stride=4), :]
    row8 = rows_of((8, width))
    side_level = roll(turned[:8, :], -4 * height, 1)
    side_level = jnp.where((row8 == 1) | (row8 == 2), side_level, 0.0)
    side_level = jnp.where(row8 == 4, level_ext[last_row:, :width], side_level)
    side_level = jnp.where(row8 == 5, level_ext[height : height + 1, :width], side_level)
    level_all = jnp.concatenate([level, side_level], axis=0)

    east_depth = jnp.minimum(level_ext, roll(level_ext, -1, 1))[:height, :width]
    north_depth = jnp.minimum(level_ext, roll(level_ext, -1, 0))[:height, :width]

    def with_side(own, f, k):
        return jnp.concatenate([own, side_ref[f, 8 * k : 8 * k + 8, :]], axis=0)

    def advected(k):
        flow_e = jnp.where(east_depth > k, 0.5 * u_ref[k], 0.0)
        flow_n = jnp.where(north_depth > k, 0.5 * v_ref[k], 0.0)
        wet_rate = jnp.where(level > k, advect_rate, 0.0)
        result = []
        for f in range(2):
            c = tracer_ref[f, k]
            ends = roll(edge_flux[f], -(4 * k + 2), 1)
            flux_e = jnp.where(lane == width - 1, ends, flow_e * (c + roll(c, -1, 1)))
            flux_w = jnp.where(lane == 0, ends, roll(flux_e, 1, 1))
            flux_n = jnp.where(row == height - 1, north_flux[f][k : k + 1, :], flow_n * (c + roll(c, -1, 0)))
            flux_s = jnp.where(row == 0, south_flux[f][k : k + 1, :], roll(flux_n, 1, 0))
            result.append(with_side(c - wet_rate * ((flux_e - flux_w) + (flux_n - flux_s)), f, k))
        return result

    now = advected(0)
    kappa_up = ratio_up = values = None
    for k in range(count):
        diagonal = 1.0
        kappa = later = None
        if k < count - 1:
            later = advected(k + 1)
            step = (now[1] - now[0]) - (later[1] - later[0])
            gate = jax.nn.sigmoid(mix_slope * step)
            wet_below = level_all > k + 1
            kappa = jnp.where(wet_below, mix_floor + mix_boost * gate, 0.0)
            slope_ref[k] = jnp.where(wet_below, (mix_boost * mix_slope) * gate * (1.0 - gate), 0.0)
            diagonal = diagonal + mix_rate * kappa
        if k > 0:
            diagonal = diagonal + mix_rate * kappa_up * (1.0 - ratio_up)
        inverse = 1.0 / diagonal
        right = [now[0], now[1], with_side(bar_ref[0, k], 2, k), with_side(bar_ref[1, k], 3, k)]
        if k > 0:
            right = [cells + mix_rate * kappa_up * value for cells, value in zip(right, values)]
        values = [cells * inverse for cells in right]
        for f in range(4):
            value_ref[f, k] = values[f]
        if kappa is not None:
            ratio_up, kappa_up = mix_rate * kappa * inverse, kappa
            ratio_ref[k] = ratio_up
        now = later

    def emit(k, cells, change):
        for f, sign in ((0, -1.0), (1, 1.0)):
            full = cells[2 + f] + sign * change
            adjoint_ref[f, k] = full[:height, :]
            side_ref[f, 8 * k : 8 * k + 8, :] = full[height:, :]

    below = values
    pull_below = None
    for k in range(count - 2, -1, -1):
        here = [value_ref[f, k] + ratio_ref[k] * below[f] for f in range(4)]
        pull = (-mix_rate) * slope_ref[k] * (
            (here[2] - below[2]) * (here[0] - below[0]) + (here[3] - below[3]) * (here[1] - below[1])
        )
        emit(k + 1, below, -pull if pull_below is None else pull_below - pull)
        below, pull_below = here, pull
    emit(0, below, pull_below)

    for f in range(2):
        for m in (1, 2):
            turn_ref[f, pl.ds(m, count, stride=4), :] = side_ref[f, pl.ds(m, count, stride=8), :]
    wide = lanes_of((width, width)) < height
    back = jnp.transpose(jnp.where(wide, turn_ref[0], roll(turn_ref[1], height, 1)))
    ends_of = [back[f * height : (f + 1) * height, :] for f in range(2)]
    south_line = [side_ref[f, pl.ds(4, count, stride=8), :] for f in range(2)]
    north_line = [side_ref[f, pl.ds(5, count, stride=8), :] for f in range(2)]
    steps = []
    for b in range(3):
        field = basis_ref[b]
        east = (0.5 * advect_rate) * (field - roll(field, -1, 1))
        north = (0.5 * advect_rate) * (field - roll(field, -1, 0))
        around = (field, east, roll(east, 1, 1), north, roll(north, 1, 0))
        steps.append([cells[:height, :width] for cells in around])
    for k in range(count):
        flow_e = jnp.where(east_depth > k, u_ref[k], 0.0)
        flow_n = jnp.where(north_depth > k, v_ref[k], 0.0)
        ends_flow = roll(edge_flow, -(4 * k + 2), 1)
        low = south_flow[k : k + 1, :]
        flow_w = jnp.where(lane == 0, ends_flow, roll(flow_e, 1, 1))
        flow_s = jnp.where(row == 0, low, roll(flow_n, 1, 0))
        for b, (field, east, west, north, south) in enumerate(steps):
            part = (flow_e * east + flow_w * west) + (flow_n * north + flow_s * south)
            share_out[b, k] = jnp.where(level > k, field, 0.0) - part
        for f in range(2):
            y = adjoint_ref[f, k]
            ends = roll(ends_of[f], -(4 * k + 2), 1)
            y_east = jnp.where(lane == width - 1, ends, roll(y, -1, 1))
            y_north = jnp.where(row == height - 1, north_line[f][k : k + 1, :], roll(y, -1, 0))
            part_e = flow_e * (y - y_east)
            part_n = flow_n * (y - y_north)
            part_w = jnp.where(lane == 0, ends_flow * (ends - y), roll(part_e, 1, 1))
            part_s = jnp.where(row == 0, low * (south_line[f][k : k + 1, :] - y), roll(part_n, 1, 0))
            base_out[f, k] = y - (0.5 * advect_rate) * ((part_e + part_w) + (part_n + part_s))


def final_kernel(sums_ref, basis_ref, base_ref, share_ref, tracer_hbm, eta_hbm, tracer_out, eta_out, sems):
    _, count, height, width = base_ref.shape
    y0, y1, y2 = galerkin(jnp.sum(sums_ref[...], axis=0, keepdims=True))

    def combined(fields):
        return y0 * fields[0] + (y1 * fields[1] + y2 * fields[2])

    eta_out[...] = combined([basis_ref[b, :height, :width] for b in range(3)])
    copies = [pltpu.make_async_copy(eta_out, eta_hbm, sems.at[0])]
    copies[0].start()
    for k in range(count):
        share = combined([share_ref[b, k] for b in range(3)])
        for f in range(2):
            tracer_out[f, k] = base_ref[f, k] + sterics[f] * share
        if (k + 1) % chunk == 0 or k == count - 1:
            levels = pl.ds(k - k % chunk, k % chunk + 1)
            at = len(copies)
            copies.append(pltpu.make_async_copy(tracer_out.at[:, levels], tracer_hbm.at[:, levels], sems.at[at]))
            copies[-1].start()
    for copy in copies:
        copy.wait()


def call(kernel, outs, name, specs=None, scratch=(), cost=None, out_spec=VMEM):
    def run(*operands):
        return pl.pallas_call(
            kernel,
            out_shape=[jax.ShapeDtypeStruct(shape, F32) for shape in outs],
            in_specs=specs or [VMEM] * len(operands),
            out_specs=[out_spec] * len(outs),
            scratch_shapes=list(scratch),
            cost_estimate=cost,
            compiler_params=pltpu.CompilerParams(vmem_limit_bytes=vmem_grant),
            name=name,
        )(*operands)

    return run


def swap(cells, axis, first, wrap):
    count = lax.axis_size(axis)
    pairs = []
    for i in range(first, count, 2):
        if i + 1 < count or wrap:
            j = (i + 1) % count
            pairs += [(i, j), (j, i)]
    return lax.ppermute(cells, axis, pairs)


def per_device(tracers, uvel, vvel, sea_mask, levels, tracer_bar, eta_bar):
    _, count, height, width = tracers.shape
    devices = lax.axis_size("gx") * lax.axis_size("gy")
    tile = (height, width)
    rows = (2, 2 * count, width)
    field = (count,) + tile
    inputs = (sea_mask, levels, eta_bar, tracers, uvel, vvel, tracer_bar)
    own, level, eta, tracers, uvel, vvel, tracer_bar = call(
        pack_columns,
        [(LAST_TILE + 1,) + tile, tile, tile, (2,) + field, field, field, (2,) + field],
        "pack_columns",
        [HBM] * 7,
        [pltpu.VMEM(tile, jnp.int32), pltpu.VMEM(tile, jnp.int32), pltpu.SemaphoreType.DMA((7,))],
    )(*(pltpu.with_memory_space_constraint(x, pltpu.HBM) for x in inputs))
    first, second = swap(own, "gx", 0, True), swap(own, "gx", 1, True)
    c_rows, n_rows, u_rows, b_rows, v_row = call(
        pack_rows, [rows, rows, (2, count, width), rows, (count, width)], "pack_rows"
    )(level, tracers, uvel, vvel, tracer_bar)
    plan = Message(count)
    message = (plan.rows, width)
    first_msg, second_msg = call(join_rows, [message, message], "join_rows")(
        level, eta, own, first, second, c_rows, n_rows, u_rows, b_rows, v_row
    )
    first_row, second_row = swap(first_msg, "gy", 1, False), swap(second_msg, "gy", 0, False)
    ext = (height + 8, 2 * width)

    def surface(*refs):
        surface_kernel(*refs, count=count)

    basis, level_ext, sums = call(surface, [(3,) + ext, ext, (devices, width)], "surface")(
        level, eta, first, second, first_row, second_row
    )
    all_sums = lax.all_to_all(sums.reshape(devices, 1, width), ("gx", "gy"), 0, 0).reshape(devices, width)
    taller = (count, height + 8, width)
    base, shares = call(
        column_kernel,
        [(2,) + field, (3,) + field],
        "columns",
        None,
        [
            pltpu.VMEM((4, 8 * count, width), F32),
            pltpu.VMEM((4, width, width), F32),
            pltpu.VMEM(taller, F32),
            pltpu.VMEM(taller, F32),
            pltpu.VMEM((4,) + taller, F32),
            pltpu.VMEM((2,) + field, F32),
        ],
        pl.CostEstimate(flops=400 * count * height * width, transcendentals=count * height * width, bytes_accessed=1 << 22),
    )(tracers, uvel, vvel, tracer_bar, own, first, second, c_rows, v_row, first_row, second_row, level_ext, basis)
    pieces = (count + chunk - 1) // chunk
    tracer_adj, eta_adj = call(
        final_kernel,
        [(2,) + field, tile],
        "finish",
        None,
        [pltpu.VMEM((2,) + field, F32), pltpu.VMEM(tile, F32), pltpu.SemaphoreType.DMA((pieces + 1,))],
        out_spec=HBM,
    )(all_sums, basis, base, shares)
    return (tracer_adj, eta_adj)


def solution(mesh):
    return jax.shard_map(
        per_device,
        mesh=mesh,
        in_specs=(
            P(None, None, "gy", "gx"),
            P(None, "gy", "gx"),
            P(None, "gy", "gx"),
            P("gy", "gx"),
            P("gy", "gx"),
            P(None, None, "gy", "gx"),
            P("gy", "gx"),
        ),
        out_specs=(P(None, None, "gy", "gx"), P("gy", "gx")),
        check_vma=False,
    )
```

```python
import jax
import jax.numpy as jnp
from jax import lax
from jax.experimental import pallas as pl
from jax.experimental.pallas import tpu as pltpu
from jax.sharding import PartitionSpec as P

advect_rate = 0.25
mix_floor = 0.2
mix_boost = 2.0
mix_slope = 2.0
mix_rate = 1.0
surface_stiffness = 2.0
thermal_steric = 0.5
haline_steric = 0.5
sterics = (thermal_steric, -haline_steric)
spread = 4.0 * surface_stiffness
F32 = jnp.float32
VMEM = pl.BlockSpec(memory_space=pltpu.VMEM)
HBM = pl.BlockSpec(memory_space=pltpu.HBM)
vmem_grant = 8 << 20
chunk = 6
U_TILE, V_TILE, LAST_TILE = 2, 3, 4
surface_turn = 18


def lanes_of(shape):
    return lax.broadcasted_iota(jnp.int32, shape, 1)


def rows_of(shape):
    return lax.broadcasted_iota(jnp.int32, shape, 0)


def roll(cells, shift, axis):
    size = cells.shape[axis]
    shift = shift % size
    return cells if shift == 0 else pltpu.roll(cells, shift, axis)


def layer_rows(count, width):
    return rows_of((count, width)).astype(F32)


def pack_columns(
    mask_in, levels_in, eta_in, tracer_in, u_in, v_in, bar_in,
    out_ref, level_ref, eta_ref, tracer_ref, u_ref, v_ref, bar_ref,
    mask_ref, levels_ref, sems,
):
    pairs = (
        (tracer_in, tracer_ref), (u_in, u_ref), (v_in, v_ref), (bar_in, bar_ref),
        (mask_in, mask_ref), (levels_in, levels_ref), (eta_in, eta_ref),
    )
    copies = [pltpu.make_async_copy(source, target, sems.at[i]) for i, (source, target) in enumerate(pairs)]
    for copy in copies:
        copy.start()
    count, height, width = u_ref.shape
    lane = lanes_of((height, width))
    group = lane // 4
    middle = jnp.where((lane % 4 == 1) | (lane % 4 == 2), group, -1)
    beside = jnp.where((lane + 1) % 4 < 2, (lane + 1) // 4 - 1, -1)

    def gathered(field, place, turn, tile):
        for k in range(count):
            tile = jnp.where(place == k, roll(field[k], 4 * k + turn, 1), tile)
        return tile

    empty = jnp.zeros((height, width), F32)
    copies[0].wait()
    for f in range(2):
        out_ref[f] = gathered(tracer_ref.at[f], group, 2, empty)
    copies[1].wait()
    out_ref[U_TILE] = gathered(u_ref, group, 2, empty)
    copies[2].wait()
    v_tile = gathered(v_ref, middle, 2, empty)
    copies[3].wait()
    out_ref[V_TILE] = gathered(bar_ref.at[0], beside, 4, v_tile)
    last = gathered(bar_ref.at[1], middle, 2, empty)
    for copy in copies[4:]:
        copy.wait()
    level = (mask_ref[...] * levels_ref[...]).astype(F32)
    level_ref[...] = level
    depth = jnp.where(lane < width // 2, roll(level, 3, 1), roll(level, -3, 1))
    surface = roll(jnp.where((lane < 3) | (lane >= width - 3), eta_ref[...], depth), -surface_turn, 1)
    start = width - 6 - surface_turn
    out_ref[LAST_TILE] = jnp.where((lane >= start) & (lane < start + 12), surface, last)


class Sides:
    def __init__(self, first_ref, second_ref, level):
        self.refs = (first_ref, second_ref)
        self.level = level
        self.shape = level.shape
        lane = lanes_of(self.shape)
        self.lane = lane
        self.layer = (lane // 4).astype(F32)
        self.eastern = lane % 4 == 1
        east, west = (roll(tile, surface_turn, 1) for tile in self.pick(LAST_TILE))
        half = lane < self.shape[1] // 2
        self.eta = jnp.where(half, east, west)
        self.depth = jnp.where(half, roll(self.eta, -3, 1), roll(self.eta, 3, 1))

    def pick(self, tile):
        first, second = (ref[tile] for ref in self.refs)
        even = is_even("gx", self.shape)
        return jnp.where(even, first, second), jnp.where(even, second, first)

    def inner(self, tile):
        east, west = self.pick(tile)
        return jnp.where(self.eastern, roll(east, -1, 1), roll(west, 1, 1))

    def bars(self):
        east, west = self.pick(V_TILE)
        return [jnp.where(self.eastern, roll(east, -3, 1), roll(west, -1, 1)), self.inner(LAST_TILE)]

    def outer(self, tile):
        east, west = self.pick(tile)
        return jnp.where(self.eastern, roll(east, -2, 1), roll(west, 2, 1))

    def columns(self, cells, east, west):
        return jnp.where(self.eastern, cells[:, east : east + 1], cells[:, west : west + 1])

    def edge_flow(self, own_ref, u_inner):
        width = self.shape[1]
        own_depth = self.columns(self.level, width - 1, 0)
        beyond = self.columns(self.depth, 0, width - 1)
        flow = jnp.where(self.eastern, own_ref[U_TILE], u_inner)
        return jnp.where(self.layer < jnp.minimum(own_depth, beyond), flow, 0.0)


def pack_rows(level_ref, tracer_ref, u_ref, v_ref, bar_ref, c_out, n_out, u_out, b_out, v_out):
    count, height, width = u_ref.shape
    level = level_ref[...]
    layer = layer_rows(count, width)
    for side, (row, inside, face) in enumerate(((height - 1, height - 2, height - 2), (0, 1, 0))):
        depth = jnp.minimum(level[row : row + 1, :], level[inside : inside + 1, :])
        flow = jnp.where(layer < depth, 0.5 * v_ref[:, face, :], 0.0)
        u_out[side] = u_ref[:, row, :]
        for f in range(2):
            part = slice(f * count, (f + 1) * count)
            c = tracer_ref[f, :, row, :]
            c_out[side, part, :] = c
            n_out[side, part, :] = flow * (c + tracer_ref[f, :, inside, :])
            b_out[side, part, :] = bar_ref[f, :, row, :]
    v_out[...] = jnp.where(layer < level[height - 1 :, :], v_ref[:, height - 1, :], 0.0)


class Message:
    def __init__(self, count):
        self.tracers = [slice(f * count, (f + 1) * count) for f in range(2)]
        self.summed = [slice(f * count, (f + 1) * count) for f in range(2, 4)]
        self.bars = [slice(f * count, (f + 1) * count) for f in range(4, 6)]
        self.v = slice(6 * count, 7 * count)
        self.surface = [slice(7 * count + 8 * i, 7 * count + 8 * i + 8) for i in range(2)]
        self.corner = self.surface[1]
        self.rows = 7 * count + 16


def is_even(axis, shape):
    return jnp.full(shape, lax.rem(lax.axis_index(axis), 2), jnp.int32) == 0


def join_rows(
    level_ref, eta_ref, own_ref, first_ref, second_ref, c_ref, n_ref, u_ref, b_ref, v_ref,
    first_out, second_out,
):
    count, width = v_ref.shape
    level = level_ref[...]
    height = level.shape[0]
    plan = Message(count)
    sides = Sides(first_ref, second_ref, level)
    inner = [sides.inner(f) for f in range(2)]
    v_inner = sides.inner(V_TILE)
    flow = 0.5 * sides.edge_flow(own_ref, sides.inner(U_TILE))
    flux = [flow * (own_ref[f] + inner[f]) for f in range(2)]
    layer = layer_rows(count, width)
    lane = lanes_of((count, width))
    level_row = rows_of((count, width))
    row8 = rows_of((8, width))
    no_flow, pad = jnp.zeros((count, width), F32), jnp.zeros((8, width), F32)

    def put(part, north, south):
        even = is_even("gy", north.shape)
        first_out[part, :] = jnp.where(even, south, north)
        second_out[part, :] = jnp.where(even, north, south)

    def summed(side, f, row, sign):
        depth = level[row : row + 1, :]
        east_flow = jnp.where(layer < jnp.minimum(depth, roll(depth, -1, 1)), 0.5 * u_ref[side], 0.0)
        rate = jnp.where(layer < depth, advect_rate, 0.0)
        c = c_ref[side, plan.tracers[f], :]
        line = flux[f][row : row + 1, :]
        east_end, west_end = (
            jnp.sum(jnp.where(lane == 4 * level_row + m, line, 0.0), axis=1, keepdims=True) for m in (1, 2)
        )
        flux_e = jnp.where(lane == width - 1, east_end, east_flow * (c + roll(c, -1, 1)))
        flux_w = jnp.where(lane == 0, west_end, roll(flux_e, 1, 1))
        return c - rate * ((flux_e - flux_w) + sign * n_ref[side, plan.tracers[f], :])

    for f in range(2):
        part = plan.tracers[f]
        put(part, c_ref[0, part, :], c_ref[1, part, :])
        put(plan.summed[f], summed(0, f, height - 1, -1.0), summed(1, f, 0, 1.0))
        put(plan.bars[f], b_ref[0, part, :], b_ref[1, part, :])
    put(plan.v, v_ref[...], no_flow)
    def ends(eta, depth):
        north = jnp.where(row8 < 4, roll(depth[height - 8 :, :], 4, 0), eta[height - 8 :, :])
        return north, jnp.where(row8 < 4, eta[:8, :], roll(depth[:8, :], 4, 0))

    put(plan.surface[0], *ends(eta_ref[...], level))
    lines = [inner[0], inner[1], v_inner]
    north = south = pad
    for index, cells in enumerate(lines):
        north = jnp.where(row8 == index, cells[height - 1 :, :], north)
        south = jnp.where(row8 == index, cells[:1, :], south)
    start = width - 6 - surface_turn
    lane8 = lanes_of((8, width))
    beyond = (lane8 >= start) & (lane8 < start + 12)
    moved = [roll(cells, -surface_turn, 1) for cells in ends(sides.eta, sides.depth)]
    put(plan.corner, jnp.where(beyond, moved[0], north), jnp.where(beyond, moved[1], south))


def extended(own, side, north, south, turn):
    row8 = rows_of((8, own.shape[1]))
    parts = []
    for index, tile in enumerate((own, side)):
        up, down = (roll(roll(msg[index], index * surface_turn, 1), turn, 0) for msg in (north, south))
        parts.append(jnp.concatenate([tile, jnp.where(row8 < 4, up, down)], axis=0))
    return jnp.concatenate(parts, axis=1)


pairs = ((0, 0), (0, 1), (0, 2), (1, 1), (1, 2), (2, 2), (2, 3))
centers = ((0.0, 0.25), (1.0, 0.25), (2.0, -0.25))


def surface_kernel(
    level_ref, eta_ref, first_ref, second_ref, first_row, second_row,
    basis_out, level_out, sums_out, *, count,
):
    level = level_ref[...]
    height, width = level.shape
    sides = Sides(first_ref, second_ref, level)
    north, south = [], []
    for part in Message(count).surface:
        even = is_even("gy", (8, width))
        north.append(jnp.where(even, second_row[part, :], first_row[part, :]))
        south.append(jnp.where(even, first_row[part, :], second_row[part, :]))
    eta_ext = extended(eta_ref[...], sides.eta, north, south, 0)
    level_ext = extended(level, sides.depth, north, south, 4)
    level_out[...] = level_ext
    rate = surface_stiffness / (spread * count)
    east_weight, west_weight = (rate * jnp.minimum(level_ext, roll(level_ext, step, 1)) for step in (-1, 1))
    north_weight, south_weight = (rate * jnp.minimum(level_ext, roll(level_ext, step, 0)) for step in (-1, 1))

    def scaled(field):
        along_x = east_weight * (field - roll(field, -1, 1)) + west_weight * (field - roll(field, 1, 1))
        along_y = north_weight * (field - roll(field, -1, 0)) + south_weight * (field - roll(field, 1, 0))
        return along_x + along_y

    powers = [eta_ext]
    for _ in range(3):
        powers.append(scaled(powers[-1]))
    for index in range(3):
        basis_out[index] = powers[index]
    powers = [x[:height, :width] for x in powers]
    table = []
    row = rows_of((8, width))
    for center, tilt in centers:
        one, two, three = powers[1:]
        if center:
            moved = [x - center * y for x, y in zip(powers[1:], powers)]
            twice = [x - center * y for x, y in zip(moved[1:], moved)]
            one, two, three = moved[0], twice[0], twice[1] - center * twice[0]
        vectors = (powers[0], one, two - tilt * one, three - tilt * two)
        part = jnp.zeros((8, width), F32)
        for index, (i, j) in enumerate(pairs):
            part = jnp.where(row == index, jnp.sum(vectors[i] * vectors[j], axis=0, keepdims=True), part)
        table.append(part)
    table = jnp.concatenate(table, axis=0)
    totals = jnp.sum(table, axis=1, keepdims=True)
    place = lanes_of(table.shape) == rows_of(table.shape)
    line = jnp.sum(jnp.where(place, totals, 0.0), axis=0, keepdims=True)
    sums_out[...] = jnp.broadcast_to(line, sums_out.shape)


def galerkin(sums):
    lane = lanes_of(sums.shape)
    d00, d01, d02, d11, d12, d22, d2q = [roll(sums, -i, 1) for i in range(7)]
    mean, square = d01[:, :1], d00[:, :1]
    place = jnp.zeros(mean.shape, jnp.int32)
    center = jnp.full(sums.shape, centers[0][0], F32)
    tilt = jnp.full(sums.shape, centers[0][1], F32)
    for index in range(1, len(centers)):
        place = jnp.where(mean > 0.5 * (centers[index - 1][0] + centers[index][0]) * square, 8 * index, place)
        center = jnp.where(lane == 8 * index, centers[index][0], center)
        tilt = jnp.where(lane == 8 * index, centers[index][1], tilt)
    base = 1.0 + spread * center
    k00 = base * d00 + spread * d01
    k01 = base * d01 + spread * d11
    k02 = base * d02 + spread * d12
    k11 = base * d11 + spread * (tilt * d11 + d12)
    k12 = base * d12 + spread * (tilt * d12 + d22)
    k22 = base * d22 + spread * d2q
    i00 = 1.0 / k00
    s11 = k11 - k01 * k01 * i00
    s12 = k12 - k01 * k02 * i00
    s22 = k22 - k02 * k02 * i00
    g1 = spread * (d01 * d01 - d00 * d11) * i00
    g2 = spread * (d02 * d01 - d00 * d12) * i00
    second = s11 > 1e-7 * k11
    i11 = jnp.where(second, 1.0 / s11, 0.0)
    c12 = s12 * i11
    last = s22 - s12 * c12
    third = second & (last > 4e-7 * s22)
    y2 = jnp.where(third, (g2 - g1 * c12) / last, 0.0)
    y1 = (g1 - s12 * y2) * i11
    y0 = (d00 - k01 * y1 - k02 * y2) * i00
    inner = center + tilt
    results = (y0 - center * y1 + center * inner * y2, y1 - (center + inner) * y2, y2)
    return [jnp.sum(jnp.where(lane == place, y, 0.0), axis=1, keepdims=True) for y in results]


def column_kernel(
    tracer_ref, u_ref, v_ref, bar_ref,
    own_ref, first_ref, second_ref, c_rows, v_row, first_row, second_row, level_ref, basis_ref,
    base_out, share_out,
    side_ref, turn_ref, ratio_ref, slope_ref, value_ref, adjoint_ref,
):
    count, height, width = u_ref.shape
    level_ext = level_ref[...]
    level = level_ext[:height, :width]
    sides = Sides(first_ref, second_ref, level)
    lane, row = lanes_of((height, width)), rows_of((height, width))
    layer = layer_rows(count, width)
    last_row, last_lane = level_ext.shape[0] - 1, level_ext.shape[1] - 1
    plan = Message(count)

    def from_north(part):
        even = is_even("gy", (part.stop - part.start, width))
        return jnp.where(even, second_row[part, :], first_row[part, :])

    def from_south(part):
        even = is_even("gy", (part.stop - part.start, width))
        return jnp.where(even, first_row[part, :], second_row[part, :])


    inner = [sides.inner(f) for f in range(2)]
    u_inner, v_inner = sides.inner(U_TILE), sides.inner(V_TILE)
    edge_flow = sides.edge_flow(own_ref, u_inner)
    edge_flux = [0.5 * edge_flow * (own_ref[f] + inner[f]) for f in range(2)]
    depth_in = sides.columns(sides.depth, 0, width - 1)
    depth_out = sides.columns(sides.depth, 1, width - 2)
    far_flow = jnp.where(sides.eastern, u_inner, sides.outer(U_TILE))
    far_flow = jnp.where(sides.layer < jnp.minimum(depth_in, depth_out), far_flow, 0.0)
    corner_depth = [
        jnp.where(sides.eastern[:1], level_ext[r : r + 1, width : width + 1], level_ext[r : r + 1, last_lane:])
        for r in (height, last_row)
    ]
    corner_north, corner_south = from_north(plan.corner), from_south(plan.corner)
    depth_up = jnp.where(row == height - 1, corner_depth[0], roll(depth_in, -1, 0))
    up_flow = jnp.where(sides.layer < jnp.minimum(depth_in, depth_up), v_inner, 0.0)
    low_flow = jnp.where(
        sides.layer[:1] < jnp.minimum(depth_in[:1], corner_depth[1]), corner_south[2:3, :], 0.0
    )
    rate = jnp.where(sides.layer < depth_in, advect_rate, 0.0)
    outward = jnp.where(sides.eastern, 1.0, -1.0)
    beyond = []
    for f in range(2):
        c = inner[f]
        far_flux = 0.5 * far_flow * (c + sides.outer(f))
        c_up = jnp.where(row == height - 1, corner_north[f : f + 1, :], roll(c, -1, 0))
        flux_n = 0.5 * up_flow * (c + c_up)
        low_flux = 0.5 * low_flow * (corner_south[f : f + 1, :] + c[:1])
        flux_s = jnp.where(row == 0, low_flux, roll(flux_n, 1, 0))
        beyond.append(c - rate * (outward * (far_flux - edge_flux[f]) + (flux_n - flux_s)))
    beyond += sides.bars() + [depth_in]
    filler = jnp.zeros((width - height * len(beyond), width), F32)
    turned = jnp.transpose(jnp.concatenate(beyond + [filler], axis=0))

    south_flow = jnp.where(layer < level[:1, :], from_south(plan.v), 0.0)
    north_flow = jnp.where(layer < level_ext[height : height + 1, :width], v_row[...], 0.0)
    south_flux, north_flux = [], []
    side_ref[...] = jnp.zeros_like(side_ref)
    for f in range(2):
        part = plan.tracers[f]
        south_flux.append(0.5 * south_flow * (from_south(part) + c_rows[1, part, :]))
        north_flux.append(0.5 * north_flow * (c_rows[0, part, :] + from_north(part)))
        side_ref[f, pl.ds(4, count, stride=8), :] = from_south(plan.summed[f]) - advect_rate * south_flux[f]
        side_ref[f, pl.ds(5, count, stride=8), :] = from_north(plan.summed[f]) + advect_rate * north_flux[f]
        side_ref[2 + f, pl.ds(4, count, stride=8), :] = from_south(plan.bars[f])
        side_ref[2 + f, pl.ds(5, count, stride=8), :] = from_north(plan.bars[f])
    for f in range(4):
        turn_ref[f] = roll(turned, -height * f, 1)
        for m in (1, 2):
            side_ref[f, pl.ds(m, count, stride=8), :] = turn_ref[f, pl.ds(m, count, stride=4), :]
    row8 = rows_of((8, width))
    side_level = roll(turned[:8, :], -4 * height, 1)
    side_level = jnp.where((row8 == 1) | (row8 == 2), side_level, 0.0)
    side_level = jnp.where(row8 == 4, level_ext[last_row:, :width], side_level)
    side_level = jnp.where(row8 == 5, level_ext[height : height + 1, :width], side_level)
    level_all = jnp.concatenate([level, side_level], axis=0)

    east_depth = jnp.minimum(level_ext, roll(level_ext, -1, 1))[:height, :width]
    north_depth = jnp.minimum(level_ext, roll(level_ext, -1, 0))[:height, :width]

    def with_side(own, f, k):
        return jnp.concatenate([own, side_ref[f, 8 * k : 8 * k + 8, :]], axis=0)

    def advected(k):
        flow_e = jnp.where(east_depth > k, 0.5 * u_ref[k], 0.0)
        flow_n = jnp.where(north_depth > k, 0.5 * v_ref[k], 0.0)
        wet_rate = jnp.where(level > k, advect_rate, 0.0)
        result = []
        for f in range(2):
            c = tracer_ref[f, k]
            ends = roll(edge_flux[f], -(4 * k + 2), 1)
            flux_e = jnp.where(lane == width - 1, ends, flow_e * (c + roll(c, -1, 1)))
            flux_w = jnp.where(lane == 0, ends, roll(flux_e, 1, 1))
            flux_n = jnp.where(row == height - 1, north_flux[f][k : k + 1, :], flow_n * (c + roll(c, -1, 0)))
            flux_s = jnp.where(row == 0, south_flux[f][k : k + 1, :], roll(flux_n, 1, 0))
            result.append(with_side(c - wet_rate * ((flux_e - flux_w) + (flux_n - flux_s)), f, k))
        return result

    now = advected(0)
    kappa_up = ratio_up = values = None
    for k in range(count):
        diagonal = 1.0
        kappa = later = None
        if k < count - 1:
            later = advected(k + 1)
            step = (now[1] - now[0]) - (later[1] - later[0])
            gate = jax.nn.sigmoid(mix_slope * step)
            wet_below = level_all > k + 1
            kappa = jnp.where(wet_below, mix_floor + mix_boost * gate, 0.0)
            slope_ref[k] = jnp.where(wet_below, (mix_boost * mix_slope) * gate * (1.0 - gate), 0.0)
            diagonal = diagonal + mix_rate * kappa
        if k > 0:
            diagonal = diagonal + mix_rate * kappa_up * (1.0 - ratio_up)
        inverse = 1.0 / diagonal
        right = [now[0], now[1], with_side(bar_ref[0, k], 2, k), with_side(bar_ref[1, k], 3, k)]
        if k > 0:
            right = [cells + mix_rate * kappa_up * value for cells, value in zip(right, values)]
        values = [cells * inverse for cells in right]
        for f in range(4):
            value_ref[f, k] = values[f]
        if kappa is not None:
            ratio_up, kappa_up = mix_rate * kappa * inverse, kappa
            ratio_ref[k] = ratio_up
        now = later

    def emit(k, cells, change):
        for f, sign in ((0, -1.0), (1, 1.0)):
            full = cells[2 + f] + sign * change
            adjoint_ref[f, k] = full[:height, :]
            side_ref[f, 8 * k : 8 * k + 8, :] = full[height:, :]

    below = values
    pull_below = None
    for k in range(count - 2, -1, -1):
        here = [value_ref[f, k] + ratio_ref[k] * below[f] for f in range(4)]
        pull = (-mix_rate) * slope_ref[k] * (
            (here[2] - below[2]) * (here[0] - below[0]) + (here[3] - below[3]) * (here[1] - below[1])
        )
        emit(k + 1, below, -pull if pull_below is None else pull_below - pull)
        below, pull_below = here, pull
    emit(0, below, pull_below)

    for f in range(2):
        for m in (1, 2):
            turn_ref[f, pl.ds(m, count, stride=4), :] = side_ref[f, pl.ds(m, count, stride=8), :]
    wide = lanes_of((width, width)) < height
    back = jnp.transpose(jnp.where(wide, turn_ref[0], roll(turn_ref[1], height, 1)))
    ends_of = [back[f * height : (f + 1) * height, :] for f in range(2)]
    south_line = [side_ref[f, pl.ds(4, count, stride=8), :] for f in range(2)]
    north_line = [side_ref[f, pl.ds(5, count, stride=8), :] for f in range(2)]
    steps = []
    for b in range(3):
        field = basis_ref[b]
        east = (0.5 * advect_rate) * (field - roll(field, -1, 1))
        north = (0.5 * advect_rate) * (field - roll(field, -1, 0))
        around = (field, east, roll(east, 1, 1), north, roll(north, 1, 0))
        steps.append([cells[:height, :width] for cells in around])
    for k in range(count):
        flow_e = jnp.where(east_depth > k, u_ref[k], 0.0)
        flow_n = jnp.where(north_depth > k, v_ref[k], 0.0)
        ends_flow = roll(edge_flow, -(4 * k + 2), 1)
        low = south_flow[k : k + 1, :]
        flow_w = jnp.where(lane == 0, ends_flow, roll(flow_e, 1, 1))
        flow_s = jnp.where(row == 0, low, roll(flow_n, 1, 0))
        for b, (field, east, west, north, south) in enumerate(steps):
            part = (flow_e * east + flow_w * west) + (flow_n * north + flow_s * south)
            share_out[b, k] = jnp.where(level > k, field, 0.0) - part
        for f in range(2):
            y = adjoint_ref[f, k]
            ends = roll(ends_of[f], -(4 * k + 2), 1)
            y_east = jnp.where(lane == width - 1, ends, roll(y, -1, 1))
            y_north = jnp.where(row == height - 1, north_line[f][k : k + 1, :], roll(y, -1, 0))
            part_e = flow_e * (y - y_east)
            part_n = flow_n * (y - y_north)
            part_w = jnp.where(lane == 0, ends_flow * (ends - y), roll(part_e, 1, 1))
            part_s = jnp.where(row == 0, low * (south_line[f][k : k + 1, :] - y), roll(part_n, 1, 0))
            base_out[f, k] = y - (0.5 * advect_rate) * ((part_e + part_w) + (part_n + part_s))


def final_kernel(sums_ref, basis_ref, base_ref, share_ref, tracer_hbm, eta_hbm, tracer_out, eta_out, sems):
    _, count, height, width = base_ref.shape
    y0, y1, y2 = galerkin(jnp.sum(sums_ref[...], axis=0, keepdims=True))

    def combined(fields):
        return y0 * fields[0] + (y1 * fields[1] + y2 * fields[2])

    eta_out[...] = combined([basis_ref[b, :height, :width] for b in range(3)])
    copies = [pltpu.make_async_copy(eta_out, eta_hbm, sems.at[0])]
    copies[0].start()
    for k in range(count):
        share = combined([share_ref[b, k] for b in range(3)])
        for f in range(2):
            tracer_out[f, k] = base_ref[f, k] + sterics[f] * share
        if (k + 1) % chunk == 0 or k == count - 1:
            levels = pl.ds(k - k % chunk, k % chunk + 1)
            at = len(copies)
            copies.append(pltpu.make_async_copy(tracer_out.at[:, levels], tracer_hbm.at[:, levels], sems.at[at]))
            copies[-1].start()
    for copy in copies:
        copy.wait()


def call(kernel, outs, name, specs=None, scratch=(), cost=None, out_spec=VMEM):
    def run(*operands):
        return pl.pallas_call(
            kernel,
            out_shape=[jax.ShapeDtypeStruct(shape, F32) for shape in outs],
            in_specs=specs or [VMEM] * len(operands),
            out_specs=[out_spec] * len(outs),
            scratch_shapes=list(scratch),
            cost_estimate=cost,
            compiler_params=pltpu.CompilerParams(vmem_limit_bytes=vmem_grant),
            name=name,
        )(*operands)

    return run


def swap(cells, axis, first, wrap):
    count = lax.axis_size(axis)
    pairs = []
    for i in range(first, count, 2):
        if i + 1 < count or wrap:
            j = (i + 1) % count
            pairs += [(i, j), (j, i)]
    return lax.ppermute(cells, axis, pairs)


def per_device(tracers, uvel, vvel, sea_mask, levels, tracer_bar, eta_bar):
    _, count, height, width = tracers.shape
    devices = lax.axis_size("gx") * lax.axis_size("gy")
    tile = (height, width)
    rows = (2, 2 * count, width)
    field = (count,) + tile
    inputs = (sea_mask, levels, eta_bar, tracers, uvel, vvel, tracer_bar)
    own, level, eta, tracers, uvel, vvel, tracer_bar = call(
        pack_columns,
        [(LAST_TILE + 1,) + tile, tile, tile, (2,) + field, field, field, (2,) + field],
        "pack_columns",
        [HBM] * 7,
        [pltpu.VMEM(tile, jnp.int32), pltpu.VMEM(tile, jnp.int32), pltpu.SemaphoreType.DMA((7,))],
    )(*(pltpu.with_memory_space_constraint(x, pltpu.HBM) for x in inputs))
    first, second = swap(own, "gx", 0, True), swap(own, "gx", 1, True)
    c_rows, n_rows, u_rows, b_rows, v_row = call(
        pack_rows, [rows, rows, (2, count, width), rows, (count, width)], "pack_rows"
    )(level, tracers, uvel, vvel, tracer_bar)
    plan = Message(count)
    message = (plan.rows, width)
    first_msg, second_msg = call(join_rows, [message, message], "join_rows")(
        level, eta, own, first, second, c_rows, n_rows, u_rows, b_rows, v_row
    )
    first_row, second_row = swap(first_msg, "gy", 1, False), swap(second_msg, "gy", 0, False)
    ext = (height + 8, 2 * width)

    def surface(*refs):
        surface_kernel(*refs, count=count)

    basis, level_ext, sums = call(surface, [(3,) + ext, ext, (devices, width)], "surface")(
        level, eta, first, second, first_row, second_row
    )
    all_sums = lax.all_to_all(sums.reshape(devices, 1, width), ("gx", "gy"), 0, 0).reshape(devices, width)
    taller = (count, height + 8, width)
    base, shares = call(
        column_kernel,
        [(2,) + field, (3,) + field],
        "columns",
        None,
        [
            pltpu.VMEM((4, 8 * count, width), F32),
            pltpu.VMEM((4, width, width), F32),
            pltpu.VMEM(taller, F32),
            pltpu.VMEM(taller, F32),
            pltpu.VMEM((4,) + taller, F32),
            pltpu.VMEM((2,) + field, F32),
        ],
        pl.CostEstimate(flops=400 * count * height * width, transcendentals=count * height * width, bytes_accessed=1 << 22),
    )(tracers, uvel, vvel, tracer_bar, own, first, second, c_rows, v_row, first_row, second_row, level_ext, basis)
    pieces = (count + chunk - 1) // chunk
    tracer_adj, eta_adj = call(
        final_kernel,
        [(2,) + field, tile],
        "finish",
        None,
        [pltpu.VMEM((2,) + field, F32), pltpu.VMEM(tile, F32), pltpu.SemaphoreType.DMA((pieces + 1,))],
        out_spec=HBM,
    )(all_sums, basis, base, shares)
    return (tracer_adj, eta_adj)


def solution(mesh):
    return jax.shard_map(
        per_device,
        mesh=mesh,
        in_specs=(
            P(None, None, "gy", "gx"),
            P(None, "gy", "gx"),
            P(None, "gy", "gx"),
            P("gy", "gx"),
            P("gy", "gx"),
            P(None, None, "gy", "gx"),
            P("gy", "gx"),
        ),
        out_specs=(P(None, None, "gy", "gx"), P("gy", "gx")),
        check_vma=False,
    )
```

```python
import jax
import jax.numpy as jnp
from jax import lax
from jax.experimental import pallas as pl
from jax.experimental.pallas import tpu as pltpu
from jax.sharding import PartitionSpec as P

advect_rate = 0.25
mix_floor = 0.2
mix_boost = 2.0
mix_slope = 2.0
mix_rate = 1.0
surface_stiffness = 2.0
thermal_steric = 0.5
haline_steric = 0.5
sterics = (thermal_steric, -haline_steric)
spread = 4.0 * surface_stiffness
F32 = jnp.float32
VMEM = pl.BlockSpec(memory_space=pltpu.VMEM)
HBM = pl.BlockSpec(memory_space=pltpu.HBM)
vmem_grant = 8 << 20
chunk = 6
U_TILE, V_TILE, LAST_TILE = 2, 3, 4
surface_turn = 18


def lanes_of(shape):
    return lax.broadcasted_iota(jnp.int32, shape, 1)


def rows_of(shape):
    return lax.broadcasted_iota(jnp.int32, shape, 0)


def roll(cells, shift, axis):
    size = cells.shape[axis]
    shift = shift % size
    return cells if shift == 0 else pltpu.roll(cells, shift, axis)


def layer_rows(count, width):
    return rows_of((count, width)).astype(F32)


def pack_columns(
    mask_in, levels_in, eta_in, tracer_in, u_in, v_in, bar_in,
    out_ref, level_ref, eta_ref, tracer_ref, u_ref, v_ref, bar_ref,
    mask_ref, levels_ref, sems,
):
    pairs = (
        (tracer_in, tracer_ref), (u_in, u_ref), (v_in, v_ref), (bar_in, bar_ref),
        (mask_in, mask_ref), (levels_in, levels_ref), (eta_in, eta_ref),
    )
    copies = [pltpu.make_async_copy(source, target, sems.at[i]) for i, (source, target) in enumerate(pairs)]
    for copy in copies[4:] + copies[:4]:
        copy.start()
    count, height, width = u_ref.shape
    lane = lanes_of((height, width))
    group = lane // 4
    middle = jnp.where((lane % 4 == 1) | (lane % 4 == 2), group, -1)
    beside = jnp.where((lane + 1) % 4 < 2, (lane + 1) // 4 - 1, -1)

    def gathered(field, place, turn, tile):
        for k in range(count):
            tile = jnp.where(place == k, roll(field[k], 4 * k + turn, 1), tile)
        return tile

    empty = jnp.zeros((height, width), F32)
    copies[0].wait()
    for f in range(2):
        out_ref[f] = gathered(tracer_ref.at[f], group, 2, empty)
    copies[1].wait()
    out_ref[U_TILE] = gathered(u_ref, group, 2, empty)
    copies[2].wait()
    v_tile = gathered(v_ref, middle, 2, empty)
    copies[3].wait()
    out_ref[V_TILE] = gathered(bar_ref.at[0], beside, 4, v_tile)
    last = gathered(bar_ref.at[1], middle, 2, empty)
    for copy in copies[4:]:
        copy.wait()
    level = (mask_ref[...] * levels_ref[...]).astype(F32)
    level_ref[...] = level
    depth = jnp.where(lane < width // 2, roll(level, 3, 1), roll(level, -3, 1))
    surface = roll(jnp.where((lane < 3) | (lane >= width - 3), eta_ref[...], depth), -surface_turn, 1)
    start = width - 6 - surface_turn
    out_ref[LAST_TILE] = jnp.where((lane >= start) & (lane < start + 12), surface, last)


class Sides:
    def __init__(self, first_ref, second_ref, level):
        self.refs = (first_ref, second_ref)
        self.level = level
        self.shape = level.shape
        lane = lanes_of(self.shape)
        self.lane = lane
        self.layer = (lane // 4).astype(F32)
        self.eastern = lane % 4 == 1
        east, west = (roll(tile, surface_turn, 1) for tile in self.pick(LAST_TILE))
        half = lane < self.shape[1] // 2
        self.eta = jnp.where(half, east, west)
        self.depth = jnp.where(half, roll(self.eta, -3, 1), roll(self.eta, 3, 1))

    def pick(self, tile):
        first, second = (ref[tile] for ref in self.refs)
        even = is_even("gx", self.shape)
        return jnp.where(even, first, second), jnp.where(even, second, first)

    def inner(self, tile):
        east, west = self.pick(tile)
        return jnp.where(self.eastern, roll(east, -1, 1), roll(west, 1, 1))

    def bars(self):
        east, west = self.pick(V_TILE)
        return [jnp.where(self.eastern, roll(east, -3, 1), roll(west, -1, 1)), self.inner(LAST_TILE)]

    def outer(self, tile):
        east, west = self.pick(tile)
        return jnp.where(self.eastern, roll(east, -2, 1), roll(west, 2, 1))

    def columns(self, cells, east, west):
        return jnp.where(self.eastern, cells[:, east : east + 1], cells[:, west : west + 1])

    def edge_flow(self, own_ref, u_inner):
        width = self.shape[1]
        own_depth = self.columns(self.level, width - 1, 0)
        beyond = self.columns(self.depth, 0, width - 1)
        flow = jnp.where(self.eastern, own_ref[U_TILE], u_inner)
        return jnp.where(self.layer < jnp.minimum(own_depth, beyond), flow, 0.0)


def pack_rows(level_ref, tracer_ref, u_ref, v_ref, bar_ref, c_out, n_out, u_out, b_out, v_out):
    count, height, width = u_ref.shape
    level = level_ref[...]
    layer = layer_rows(count, width)
    for side, (row, inside, face) in enumerate(((height - 1, height - 2, height - 2), (0, 1, 0))):
        depth = jnp.minimum(level[row : row + 1, :], level[inside : inside + 1, :])
        flow = jnp.where(layer < depth, 0.5 * v_ref[:, face, :], 0.0)
        u_out[side] = u_ref[:, row, :]
        for f in range(2):
            part = slice(f * count, (f + 1) * count)
            c = tracer_ref[f, :, row, :]
            c_out[side, part, :] = c
            n_out[side, part, :] = flow * (c + tracer_ref[f, :, inside, :])
            b_out[side, part, :] = bar_ref[f, :, row, :]
    v_out[...] = jnp.where(layer < level[height - 1 :, :], v_ref[:, height - 1, :], 0.0)


class Message:
    def __init__(self, count):
        self.tracers = [slice(f * count, (f + 1) * count) for f in range(2)]
        self.summed = [slice(f * count, (f + 1) * count) for f in range(2, 4)]
        self.bars = [slice(f * count, (f + 1) * count) for f in range(4, 6)]
        self.v = slice(6 * count, 7 * count)
        self.surface = [slice(7 * count + 8 * i, 7 * count + 8 * i + 8) for i in range(2)]
        self.corner = self.surface[1]
        self.rows = 7 * count + 16


def is_even(axis, shape):
    return jnp.full(shape, lax.rem(lax.axis_index(axis), 2), jnp.int32) == 0


def join_rows(
    level_ref, eta_ref, own_ref, first_ref, second_ref, c_ref, n_ref, u_ref, b_ref, v_ref,
    first_out, second_out,
):
    count, width = v_ref.shape
    level = level_ref[...]
    height = level.shape[0]
    plan = Message(count)
    sides = Sides(first_ref, second_ref, level)
    inner = [sides.inner(f) for f in range(2)]
    v_inner = sides.inner(V_TILE)
    flow = 0.5 * sides.edge_flow(own_ref, sides.inner(U_TILE))
    flux = [flow * (own_ref[f] + inner[f]) for f in range(2)]
    layer = layer_rows(count, width)
    lane = lanes_of((count, width))
    level_row = rows_of((count, width))
    row8 = rows_of((8, width))
    no_flow, pad = jnp.zeros((count, width), F32), jnp.zeros((8, width), F32)

    def put(part, north, south):
        even = is_even("gy", north.shape)
        first_out[part, :] = jnp.where(even, south, north)
        second_out[part, :] = jnp.where(even, north, south)

    def summed(side, f, row, sign):
        depth = level[row : row + 1, :]
        east_flow = jnp.where(layer < jnp.minimum(depth, roll(depth, -1, 1)), 0.5 * u_ref[side], 0.0)
        rate = jnp.where(layer < depth, advect_rate, 0.0)
        c = c_ref[side, plan.tracers[f], :]
        line = flux[f][row : row + 1, :]
        east_end, west_end = (
            jnp.sum(jnp.where(lane == 4 * level_row + m, line, 0.0), axis=1, keepdims=True) for m in (1, 2)
        )
        flux_e = jnp.where(lane == width - 1, east_end, east_flow * (c + roll(c, -1, 1)))
        flux_w = jnp.where(lane == 0, west_end, roll(flux_e, 1, 1))
        return c - rate * ((flux_e - flux_w) + sign * n_ref[side, plan.tracers[f], :])

    for f in range(2):
        part = plan.tracers[f]
        put(part, c_ref[0, part, :], c_ref[1, part, :])
        put(plan.summed[f], summed(0, f, height - 1, -1.0), summed(1, f, 0, 1.0))
        put(plan.bars[f], b_ref[0, part, :], b_ref[1, part, :])
    put(plan.v, v_ref[...], no_flow)
    def ends(eta, depth):
        north = jnp.where(row8 < 4, roll(depth[height - 8 :, :], 4, 0), eta[height - 8 :, :])
        return north, jnp.where(row8 < 4, eta[:8, :], roll(depth[:8, :], 4, 0))

    put(plan.surface[0], *ends(eta_ref[...], level))
    lines = [inner[0], inner[1], v_inner]
    north = south = pad
    for index, cells in enumerate(lines):
        north = jnp.where(row8 == index, cells[height - 1 :, :], north)
        south = jnp.where(row8 == index, cells[:1, :], south)
    start = width - 6 - surface_turn
    lane8 = lanes_of((8, width))
    beyond = (lane8 >= start) & (lane8 < start + 12)
    moved = [roll(cells, -surface_turn, 1) for cells in ends(sides.eta, sides.depth)]
    put(plan.corner, jnp.where(beyond, moved[0], north), jnp.where(beyond, moved[1], south))


def extended(own, side, north, south, turn):
    row8 = rows_of((8, own.shape[1]))
    parts = []
    for index, tile in enumerate((own, side)):
        up, down = (roll(roll(msg[index], index * surface_turn, 1), turn, 0) for msg in (north, south))
        parts.append(jnp.concatenate([tile, jnp.where(row8 < 4, up, down)], axis=0))
    return jnp.concatenate(parts, axis=1)


pairs = ((0, 0), (0, 1), (0, 2), (1, 1), (1, 2), (2, 2), (2, 3))
centers = ((0.0, 0.25), (1.0, 0.25), (2.0, -0.25))


def surface_kernel(
    level_ref, eta_ref, first_ref, second_ref, first_row, second_row,
    basis_out, level_out, sums_out, *, count,
):
    level = level_ref[...]
    height, width = level.shape
    sides = Sides(first_ref, second_ref, level)
    north, south = [], []
    for part in Message(count).surface:
        even = is_even("gy", (8, width))
        north.append(jnp.where(even, second_row[part, :], first_row[part, :]))
        south.append(jnp.where(even, first_row[part, :], second_row[part, :]))
    eta_ext = extended(eta_ref[...], sides.eta, north, south, 0)
    level_ext = extended(level, sides.depth, north, south, 4)
    level_out[...] = level_ext
    rate = surface_stiffness / (spread * count)
    east_weight, west_weight = (rate * jnp.minimum(level_ext, roll(level_ext, step, 1)) for step in (-1, 1))
    north_weight, south_weight = (rate * jnp.minimum(level_ext, roll(level_ext, step, 0)) for step in (-1, 1))

    def scaled(field):
        along_x = east_weight * (field - roll(field, -1, 1)) + west_weight * (field - roll(field, 1, 1))
        along_y = north_weight * (field - roll(field, -1, 0)) + south_weight * (field - roll(field, 1, 0))
        return along_x + along_y

    powers = [eta_ext]
    for _ in range(3):
        powers.append(scaled(powers[-1]))
    for index in range(3):
        basis_out[index] = powers[index]
    powers = [x[:height, :width] for x in powers]
    table = []
    row = rows_of((8, width))
    for center, tilt in centers:
        one, two, three = powers[1:]
        if center:
            moved = [x - center * y for x, y in zip(powers[1:], powers)]
            twice = [x - center * y for x, y in zip(moved[1:], moved)]
            one, two, three = moved[0], twice[0], twice[1] - center * twice[0]
        vectors = (powers[0], one, two - tilt * one, three - tilt * two)
        part = jnp.zeros((8, width), F32)
        for index, (i, j) in enumerate(pairs):
            part = jnp.where(row == index, jnp.sum(vectors[i] * vectors[j], axis=0, keepdims=True), part)
        table.append(part)
    table = jnp.concatenate(table, axis=0)
    totals = jnp.sum(table, axis=1, keepdims=True)
    place = lanes_of(table.shape) == rows_of(table.shape)
    line = jnp.sum(jnp.where(place, totals, 0.0), axis=0, keepdims=True)
    sums_out[...] = jnp.broadcast_to(line, sums_out.shape)


def galerkin(sums):
    lane = lanes_of(sums.shape)
    d00, d01, d02, d11, d12, d22, d2q = [roll(sums, -i, 1) for i in range(7)]
    mean, square = d01[:, :1], d00[:, :1]
    place = jnp.zeros(mean.shape, jnp.int32)
    center = jnp.full(sums.shape, centers[0][0], F32)
    tilt = jnp.full(sums.shape, centers[0][1], F32)
    for index in range(1, len(centers)):
        place = jnp.where(mean > 0.5 * (centers[index - 1][0] + centers[index][0]) * square, 8 * index, place)
        center = jnp.where(lane == 8 * index, centers[index][0], center)
        tilt = jnp.where(lane == 8 * index, centers[index][1], tilt)
    base = 1.0 + spread * center
    k00 = base * d00 + spread * d01
    k01 = base * d01 + spread * d11
    k02 = base * d02 + spread * d12
    k11 = base * d11 + spread * (tilt * d11 + d12)
    k12 = base * d12 + spread * (tilt * d12 + d22)
    k22 = base * d22 + spread * d2q
    i00 = 1.0 / k00
    s11 = k11 - k01 * k01 * i00
    s12 = k12 - k01 * k02 * i00
    s22 = k22 - k02 * k02 * i00
    g1 = spread * (d01 * d01 - d00 * d11) * i00
    g2 = spread * (d02 * d01 - d00 * d12) * i00
    second = s11 > 1e-7 * k11
    i11 = jnp.where(second, 1.0 / s11, 0.0)
    c12 = s12 * i11
    last = s22 - s12 * c12
    third = second & (last > 4e-7 * s22)
    y2 = jnp.where(third, (g2 - g1 * c12) / last, 0.0)
    y1 = (g1 - s12 * y2) * i11
    y0 = (d00 - k01 * y1 - k02 * y2) * i00
    inner = center + tilt
    results = (y0 - center * y1 + center * inner * y2, y1 - (center + inner) * y2, y2)
    return [jnp.sum(jnp.where(lane == place, y, 0.0), axis=1, keepdims=True) for y in results]


def column_kernel(
    tracer_ref, u_ref, v_ref, bar_ref,
    own_ref, first_ref, second_ref, c_rows, v_row, first_row, second_row, level_ref, basis_ref,
    base_out, share_out,
    side_ref, turn_ref, ratio_ref, slope_ref, value_ref, adjoint_ref,
):
    count, height, width = u_ref.shape
    level_ext = level_ref[...]
    level = level_ext[:height, :width]
    sides = Sides(first_ref, second_ref, level)
    lane, row = lanes_of((height, width)), rows_of((height, width))
    layer = layer_rows(count, width)
    last_row, last_lane = level_ext.shape[0] - 1, level_ext.shape[1] - 1
    plan = Message(count)

    def from_north(part):
        even = is_even("gy", (part.stop - part.start, width))
        return jnp.where(even, second_row[part, :], first_row[part, :])

    def from_south(part):
        even = is_even("gy", (part.stop - part.start, width))
        return jnp.where(even, first_row[part, :], second_row[part, :])


    inner = [sides.inner(f) for f in range(2)]
    u_inner, v_inner = sides.inner(U_TILE), sides.inner(V_TILE)
    edge_flow = sides.edge_flow(own_ref, u_inner)
    edge_flux = [0.5 * edge_flow * (own_ref[f] + inner[f]) for f in range(2)]
    depth_in = sides.columns(sides.depth, 0, width - 1)
    depth_out = sides.columns(sides.depth, 1, width - 2)
    far_flow = jnp.where(sides.eastern, u_inner, sides.outer(U_TILE))
    far_flow = jnp.where(sides.layer < jnp.minimum(depth_in, depth_out), far_flow, 0.0)
    corner_depth = [
        jnp.where(sides.eastern[:1], level_ext[r : r + 1, width : width + 1], level_ext[r : r + 1, last_lane:])
        for r in (height, last_row)
    ]
    corner_north, corner_south = from_north(plan.corner), from_south(plan.corner)
    depth_up = jnp.where(row == height - 1, corner_depth[0], roll(depth_in, -1, 0))
    up_flow = jnp.where(sides.layer < jnp.minimum(depth_in, depth_up), v_inner, 0.0)
    low_flow = jnp.where(
        sides.layer[:1] < jnp.minimum(depth_in[:1], corner_depth[1]), corner_south[2:3, :], 0.0
    )
    rate = jnp.where(sides.layer < depth_in, advect_rate, 0.0)
    outward = jnp.where(sides.eastern, 1.0, -1.0)
    beyond = []
    for f in range(2):
        c = inner[f]
        far_flux = 0.5 * far_flow * (c + sides.outer(f))
        c_up = jnp.where(row == height - 1, corner_north[f : f + 1, :], roll(c, -1, 0))
        flux_n = 0.5 * up_flow * (c + c_up)
        low_flux = 0.5 * low_flow * (corner_south[f : f + 1, :] + c[:1])
        flux_s = jnp.where(row == 0, low_flux, roll(flux_n, 1, 0))
        beyond.append(c - rate * (outward * (far_flux - edge_flux[f]) + (flux_n - flux_s)))
    beyond += sides.bars() + [depth_in]
    filler = jnp.zeros((width - height * len(beyond), width), F32)
    turned = jnp.transpose(jnp.concatenate(beyond + [filler], axis=0))

    south_flow = jnp.where(layer < level[:1, :], from_south(plan.v), 0.0)
    north_flow = jnp.where(layer < level_ext[height : height + 1, :width], v_row[...], 0.0)
    south_flux, north_flux = [], []
    side_ref[...] = jnp.zeros_like(side_ref)
    for f in range(2):
        part = plan.tracers[f]
        south_flux.append(0.5 * south_flow * (from_south(part) + c_rows[1, part, :]))
        north_flux.append(0.5 * north_flow * (c_rows[0, part, :] + from_north(part)))
        side_ref[f, pl.ds(4, count, stride=8), :] = from_south(plan.summed[f]) - advect_rate * south_flux[f]
        side_ref[f, pl.ds(5, count, stride=8), :] = from_north(plan.summed[f]) + advect_rate * north_flux[f]
        side_ref[2 + f, pl.ds(4, count, stride=8), :] = from_south(plan.bars[f])
        side_ref[2 + f, pl.ds(5, count, stride=8), :] = from_north(plan.bars[f])
    for f in range(4):
        turn_ref[f] = roll(turned, -height * f, 1)
        for m in (1, 2):
            side_ref[f, pl.ds(m, count, stride=8), :] = turn_ref[f, pl.ds(m, count, stride=4), :]
    row8 = rows_of((8, width))
    side_level = roll(turned[:8, :], -4 * height, 1)
    side_level = jnp.where((row8 == 1) | (row8 == 2), side_level, 0.0)
    side_level = jnp.where(row8 == 4, level_ext[last_row:, :width], side_level)
    side_level = jnp.where(row8 == 5, level_ext[height : height + 1, :width], side_level)
    level_all = jnp.concatenate([level, side_level], axis=0)

    east_depth = jnp.minimum(level_ext, roll(level_ext, -1, 1))[:height, :width]
    north_depth = jnp.minimum(level_ext, roll(level_ext, -1, 0))[:height, :width]

    def with_side(own, f, k):
        return jnp.concatenate([own, side_ref[f, 8 * k : 8 * k + 8, :]], axis=0)

    def advected(k):
        flow_e = jnp.where(east_depth > k, 0.5 * u_ref[k], 0.0)
        flow_n = jnp.where(north_depth > k, 0.5 * v_ref[k], 0.0)
        wet_rate = jnp.where(level > k, advect_rate, 0.0)
        result = []
        for f in range(2):
            c = tracer_ref[f, k]
            ends = roll(edge_flux[f], -(4 * k + 2), 1)
            flux_e = jnp.where(lane == width - 1, ends, flow_e * (c + roll(c, -1, 1)))
            flux_w = jnp.where(lane == 0, ends, roll(flux_e, 1, 1))
            flux_n = jnp.where(row == height - 1, north_flux[f][k : k + 1, :], flow_n * (c + roll(c, -1, 0)))
            flux_s = jnp.where(row == 0, south_flux[f][k : k + 1, :], roll(flux_n, 1, 0))
            result.append(with_side(c - wet_rate * ((flux_e - flux_w) + (flux_n - flux_s)), f, k))
        return result

    now = advected(0)
    kappa_up = ratio_up = values = None
    for k in range(count):
        diagonal = 1.0
        kappa = later = None
        if k < count - 1:
            later = advected(k + 1)
            step = (now[1] - now[0]) - (later[1] - later[0])
            gate = jax.nn.sigmoid(mix_slope * step)
            wet_below = level_all > k + 1
            kappa = jnp.where(wet_below, mix_floor + mix_boost * gate, 0.0)
            slope_ref[k] = jnp.where(wet_below, (mix_boost * mix_slope) * gate * (1.0 - gate), 0.0)
            diagonal = diagonal + mix_rate * kappa
        if k > 0:
            diagonal = diagonal + mix_rate * kappa_up * (1.0 - ratio_up)
        inverse = 1.0 / diagonal
        right = [now[0], now[1], with_side(bar_ref[0, k], 2, k), with_side(bar_ref[1, k], 3, k)]
        if k > 0:
            right = [cells + mix_rate * kappa_up * value for cells, value in zip(right, values)]
        values = [cells * inverse for cells in right]
        for f in range(4):
            value_ref[f, k] = values[f]
        if kappa is not None:
            ratio_up, kappa_up = mix_rate * kappa * inverse, kappa
            ratio_ref[k] = ratio_up
        now = later

    def emit(k, cells, change):
        for f, sign in ((0, -1.0), (1, 1.0)):
            full = cells[2 + f] + sign * change
            adjoint_ref[f, k] = full[:height, :]
            side_ref[f, 8 * k : 8 * k + 8, :] = full[height:, :]

    below = values
    pull_below = None
    for k in range(count - 2, -1, -1):
        here = [value_ref[f, k] + ratio_ref[k] * below[f] for f in range(4)]
        pull = (-mix_rate) * slope_ref[k] * (
            (here[2] - below[2]) * (here[0] - below[0]) + (here[3] - below[3]) * (here[1] - below[1])
        )
        emit(k + 1, below, -pull if pull_below is None else pull_below - pull)
        below, pull_below = here, pull
    emit(0, below, pull_below)

    for f in range(2):
        for m in (1, 2):
            turn_ref[f, pl.ds(m, count, stride=4), :] = side_ref[f, pl.ds(m, count, stride=8), :]
    wide = lanes_of((width, width)) < height
    back = jnp.transpose(jnp.where(wide, turn_ref[0], roll(turn_ref[1], height, 1)))
    ends_of = [back[f * height : (f + 1) * height, :] for f in range(2)]
    south_line = [side_ref[f, pl.ds(4, count, stride=8), :] for f in range(2)]
    north_line = [side_ref[f, pl.ds(5, count, stride=8), :] for f in range(2)]
    steps = []
    for b in range(3):
        field = basis_ref[b]
        east = (0.5 * advect_rate) * (field - roll(field, -1, 1))
        north = (0.5 * advect_rate) * (field - roll(field, -1, 0))
        around = (field, east, roll(east, 1, 1), north, roll(north, 1, 0))
        steps.append([cells[:height, :width] for cells in around])
    for k in range(count):
        flow_e = jnp.where(east_depth > k, u_ref[k], 0.0)
        flow_n = jnp.where(north_depth > k, v_ref[k], 0.0)
        ends_flow = roll(edge_flow, -(4 * k + 2), 1)
        low = south_flow[k : k + 1, :]
        flow_w = jnp.where(lane == 0, ends_flow, roll(flow_e, 1, 1))
        flow_s = jnp.where(row == 0, low, roll(flow_n, 1, 0))
        for b, (field, east, west, north, south) in enumerate(steps):
            part = (flow_e * east + flow_w * west) + (flow_n * north + flow_s * south)
            share_out[b, k] = jnp.where(level > k, field, 0.0) - part
        for f in range(2):
            y = adjoint_ref[f, k]
            ends = roll(ends_of[f], -(4 * k + 2), 1)
            y_east = jnp.where(lane == width - 1, ends, roll(y, -1, 1))
            y_north = jnp.where(row == height - 1, north_line[f][k : k + 1, :], roll(y, -1, 0))
            part_e = flow_e * (y - y_east)
            part_n = flow_n * (y - y_north)
            part_w = jnp.where(lane == 0, ends_flow * (ends - y), roll(part_e, 1, 1))
            part_s = jnp.where(row == 0, low * (south_line[f][k : k + 1, :] - y), roll(part_n, 1, 0))
            base_out[f, k] = y - (0.5 * advect_rate) * ((part_e + part_w) + (part_n + part_s))


def final_kernel(sums_ref, basis_ref, base_ref, share_ref, tracer_hbm, eta_hbm, tracer_out, eta_out, sems):
    _, count, height, width = base_ref.shape
    y0, y1, y2 = galerkin(jnp.sum(sums_ref[...], axis=0, keepdims=True))

    def combined(fields):
        return y0 * fields[0] + (y1 * fields[1] + y2 * fields[2])

    eta_out[...] = combined([basis_ref[b, :height, :width] for b in range(3)])
    copies = [pltpu.make_async_copy(eta_out, eta_hbm, sems.at[0])]
    copies[0].start()
    for k in range(count):
        share = combined([share_ref[b, k] for b in range(3)])
        for f in range(2):
            tracer_out[f, k] = base_ref[f, k] + sterics[f] * share
        if (k + 1) % chunk == 0 or k == count - 1:
            levels = pl.ds(k - k % chunk, k % chunk + 1)
            at = len(copies)
            copies.append(pltpu.make_async_copy(tracer_out.at[:, levels], tracer_hbm.at[:, levels], sems.at[at]))
            copies[-1].start()
    for copy in copies:
        copy.wait()


def call(kernel, outs, name, specs=None, scratch=(), cost=None, out_spec=VMEM):
    def run(*operands):
        return pl.pallas_call(
            kernel,
            out_shape=[jax.ShapeDtypeStruct(shape, F32) for shape in outs],
            in_specs=specs or [VMEM] * len(operands),
            out_specs=[out_spec] * len(outs),
            scratch_shapes=list(scratch),
            cost_estimate=cost,
            compiler_params=pltpu.CompilerParams(vmem_limit_bytes=vmem_grant),
            name=name,
        )(*operands)

    return run


def swap(cells, axis, first, wrap):
    count = lax.axis_size(axis)
    pairs = []
    for i in range(first, count, 2):
        if i + 1 < count or wrap:
            j = (i + 1) % count
            pairs += [(i, j), (j, i)]
    return lax.ppermute(cells, axis, pairs)


def per_device(tracers, uvel, vvel, sea_mask, levels, tracer_bar, eta_bar):
    _, count, height, width = tracers.shape
    devices = lax.axis_size("gx") * lax.axis_size("gy")
    tile = (height, width)
    rows = (2, 2 * count, width)
    field = (count,) + tile
    inputs = (sea_mask, levels, eta_bar, tracers, uvel, vvel, tracer_bar)
    own, level, eta, tracers, uvel, vvel, tracer_bar = call(
        pack_columns,
        [(LAST_TILE + 1,) + tile, tile, tile, (2,) + field, field, field, (2,) + field],
        "pack_columns",
        [HBM] * 7,
        [pltpu.VMEM(tile, jnp.int32), pltpu.VMEM(tile, jnp.int32), pltpu.SemaphoreType.DMA((7,))],
    )(*(pltpu.with_memory_space_constraint(x, pltpu.HBM) for x in inputs))
    first, second = swap(own, "gx", 0, True), swap(own, "gx", 1, True)
    c_rows, n_rows, u_rows, b_rows, v_row = call(
        pack_rows, [rows, rows, (2, count, width), rows, (count, width)], "pack_rows"
    )(level, tracers, uvel, vvel, tracer_bar)
    plan = Message(count)
    message = (plan.rows, width)
    first_msg, second_msg = call(join_rows, [message, message], "join_rows")(
        level, eta, own, first, second, c_rows, n_rows, u_rows, b_rows, v_row
    )
    first_row, second_row = swap(first_msg, "gy", 1, False), swap(second_msg, "gy", 0, False)
    ext = (height + 8, 2 * width)

    def surface(*refs):
        surface_kernel(*refs, count=count)

    basis, level_ext, sums = call(surface, [(3,) + ext, ext, (devices, width)], "surface")(
        level, eta, first, second, first_row, second_row
    )
    all_sums = lax.all_to_all(sums.reshape(devices, 1, width), ("gx", "gy"), 0, 0).reshape(devices, width)
    taller = (count, height + 8, width)
    base, shares = call(
        column_kernel,
        [(2,) + field, (3,) + field],
        "columns",
        None,
        [
            pltpu.VMEM((4, 8 * count, width), F32),
            pltpu.VMEM((4, width, width), F32),
            pltpu.VMEM(taller, F32),
            pltpu.VMEM(taller, F32),
            pltpu.VMEM((4,) + taller, F32),
            pltpu.VMEM((2,) + field, F32),
        ],
        pl.CostEstimate(flops=400 * count * height * width, transcendentals=count * height * width, bytes_accessed=1 << 22),
    )(tracers, uvel, vvel, tracer_bar, own, first, second, c_rows, v_row, first_row, second_row, level_ext, basis)
    pieces = (count + chunk - 1) // chunk
    tracer_adj, eta_adj = call(
        final_kernel,
        [(2,) + field, tile],
        "finish",
        None,
        [pltpu.VMEM((2,) + field, F32), pltpu.VMEM(tile, F32), pltpu.SemaphoreType.DMA((pieces + 1,))],
        out_spec=HBM,
    )(all_sums, basis, base, shares)
    return (tracer_adj, eta_adj)


def solution(mesh):
    return jax.shard_map(
        per_device,
        mesh=mesh,
        in_specs=(
            P(None, None, "gy", "gx"),
            P(None, "gy", "gx"),
            P(None, "gy", "gx"),
            P("gy", "gx"),
            P("gy", "gx"),
            P(None, None, "gy", "gx"),
            P("gy", "gx"),
        ),
        out_specs=(P(None, None, "gy", "gx"), P("gy", "gx")),
        check_vma=False,
    )
```
